32 devices in a mesh: ctx: 16 (over z, x, core), fsdp: 2 (over y).
Axes of the slice: x: 2, y: 2, z: 4, core: 2. Of those that a mesh axis runs over, the one named last changes fastest.
Arguments:
- tokens: bfloat16 [2, 2048, 2048], P('fsdp', 'ctx'), may hold values from -6 to 6
- doc_lengths: int32 [2, 8], P('fsdp'), may hold values from 1 to 1024, 2048 in all within a row
- ln1_gain: bfloat16 [2048], P(('ctx', 'fsdp')), may hold values from 0.099609375 to 1.8984375
- ln1_bias: bfloat16 [2048], P(('ctx', 'fsdp')), may hold values from -1.75 to 1.75
- w_qkv: bfloat16 [2048, 6144], P(('ctx', 'fsdp')), may hold values from -0.125 to 0.125
- bias_q: bfloat16 [2048], P(('ctx', 'fsdp')), may hold values from -3 to 3
- bias_v: bfloat16 [2048], P(('ctx', 'fsdp')), may hold values from -3 to 3
- w_out: bfloat16 [2048, 2048], P(('ctx', 'fsdp')), may hold values from -0.25 to 0.25
- b_out: bfloat16 [2048], P(('ctx', 'fsdp')), may hold values from -1.75 to 1.75
- ln2_gain: bfloat16 [2048], P(('ctx', 'fsdp')), may hold values from 0.099609375 to 1.8984375
- ln2_bias: bfloat16 [2048], P(('ctx', 'fsdp')), may hold values from -1.75 to 1.75
- w_up: bfloat16 [2048, 8192], P(('ctx', 'fsdp')), may hold values from -0.125 to 0.125
- b_up: bfloat16 [8192], P(('ctx', 'fsdp')), may hold values from -3 to 3
- w_down: bfloat16 [8192, 2048], P(('ctx', 'fsdp')), may hold values from -0.0625 to 0.0625
- b_down: bfloat16 [2048], P(('ctx', 'fsdp')), may hold values from -1.75 to 1.75
- cotangent: bfloat16 [2, 2048, 2048], P('fsdp', 'ctx'), may hold values from -6 to 6
Outputs:
- outputs: bfloat16 [2, 2048, 2048], P('fsdp', 'ctx')
- grad_tokens: float32 [2, 2048, 2048], P('fsdp', 'ctx')
- grad_ln1_gain: float32 [2048], P(('ctx', 'fsdp'))
- grad_ln1_bias: float32 [2048], P(('ctx', 'fsdp'))
- grad_w_qkv: float32 [2048, 6144], P(('ctx', 'fsdp'))
- grad_bias_q: float32 [2048], P(('ctx', 'fsdp'))
- grad_bias_v: float32 [2048], P(('ctx', 'fsdp'))
- grad_w_out: float32 [2048, 2048], P(('ctx', 'fsdp'))
- grad_b_out: float32 [2048], P(('ctx', 'fsdp'))
- grad_ln2_gain: float32 [2048], P(('ctx', 'fsdp'))
- grad_ln2_bias: float32 [2048], P(('ctx', 'fsdp'))
- grad_w_up: float32 [2048, 8192], P(('ctx', 'fsdp'))
- grad_b_up: float32 [8192], P(('ctx', 'fsdp'))
- grad_w_down: float32 [8192, 2048], P(('ctx', 'fsdp'))
- grad_b_down: float32 [2048], P(('ctx', 'fsdp'))
The draws below stay inside these ranges and needn't reach their ends.
Inputs may be any that keep to these rules, and one draw needn't show every extreme that they name: `doc_lengths`: each row lists the lengths of 8 documents that together fill one sequence of 2048 positions in order; in every row the longest is exactly 1024.
All inputs are finite; a program needn't handle non-finite values.
Results may differ from the reference program's by a relative error of at most 0.015.
Values may be sent and summed in bfloat16 or wider, within the bound.
A program may use at most 576 MiB of HBM per device.

```python
import math
import jax
import jax.numpy as jnp
import numpy as np
from jax import lax

D = 2048
HEAD_DIM = 64
FF = 8192
TOK_DEV = 128
NDOCS = 8
SEQ_LEN = 2048
SEQS = 2
DOC_MOST = 1024
N_CTX = 16


def spiked(values, own_key, source, target, blocks, factor):
    owner, partner = [(jnp.arange(values.shape[axis_at]) // (values.shape[axis_at] // blocks)).reshape([-1 if axis == axis_at else 1 for axis in range(values.ndim)]) for axis_at in (source, target)]
    chosen = jax.random.permutation(own_key, blocks)[partner]
    strong = (owner == chosen) | (owner == (partner + blocks // 2) % blocks)
    return jnp.where(strong, factor * values, values)


def block_levels(key, shape, shards, low, largest):
    def one(axis_at, blocks):
        heights = jax.random.uniform(jax.random.fold_in(jax.random.fold_in(key, 6), axis_at), (blocks,), jnp.float32, low / len(shards), largest / len(shards))
        return jnp.repeat(jnp.exp(heights), shape[axis_at] // blocks).reshape((-1,) + (1,) * (len(shape) - axis_at - 1))

    level = one(*shards[0])
    for cut in shards[1:]:
        level = level * one(*cut)
    return level


def profile(count, total, most, slope):
    weights = [(1 << 20) // math.isqrt(rank ** slope) + 1 for rank in range(2, count + 1)]
    rest, counts = total - most - (count - 1), [1] * (count - 1)
    while rest > 0:
        movable = [i for i in range(count - 1) if counts[i] < most]
        pool, left = sum([weights[i] for i in movable]), rest
        for i in movable:
            addition = min(most - counts[i], max(1, left * weights[i] // pool), rest)
            counts[i] = counts[i] + addition
            rest = rest - addition
    return np.array([most] + counts)


def uneven_parts(key, number_of, total, bound, skew):
    if number_of == 2:
        one = jax.random.randint(key, (), max(1, total - bound), min(bound, total - 1) + 1)
        return jnp.stack([one, total - one])
    sizes = jnp.asarray(profile(number_of, total, bound, skew), jnp.int32)
    pairs = (number_of - 1) // 2
    giver, sink = sizes[1:1 + 2 * pairs:2], sizes[2:2 + 2 * pairs:2]
    margin = jnp.minimum(giver - 1, bound - sink)
    moved = jax.random.randint(jax.random.fold_in(key, 1), (pairs,), 0, 1 << 20) % (margin + 1)
    sizes = sizes.at[1:1 + 2 * pairs:2].set(giver - moved).at[2:2 + 2 * pairs:2].set(sink + moved)
    return sizes[jax.random.permutation(jax.random.fold_in(key, 2), number_of)]


def bell_draw(stream_key, extent, width, bound, cuts=(), kind=jnp.bfloat16):
    values = width * jax.random.normal(stream_key, extent, jnp.float32)
    if cuts:
        values = values * block_levels(stream_key, extent, cuts, -0.22, 0.18)
    return jnp.clip(values, -bound, bound).astype(kind)


def bell_draw_with(rng, extent, deviation, reach, cuts, heavy, kind=jnp.bfloat16):
    values = deviation * jax.random.normal(rng, extent, jnp.float32)
    if cuts:
        values = values * block_levels(rng, extent, cuts, -0.22, 0.18)
    return jnp.clip(spiked(values, jax.random.fold_in(rng, 3), *heavy), -reach, reach).astype(kind)


def setup_inputs(seed: int = 0) -> dict:
    key_list = jax.random.split(jax.random.key(seed), 17)
    tokens = bell_draw(key_list[0], (SEQS, SEQ_LEN, D), 1.0, 6.0, ((0, 2), (1, 16)))
    doc_lengths = jax.vmap(lambda own: uneven_parts(own, NDOCS, SEQ_LEN, DOC_MOST, 2))(jax.random.split(key_list[1], SEQS)).reshape((SEQS, NDOCS)).astype(jnp.int32)
    ln1_gain = jnp.clip(1.0 + 0.18 * jax.random.normal(key_list[2], (D,), jnp.float32), 0.099609375, 1.8984375).astype(jnp.bfloat16)
    ln1_bias = bell_draw(key_list[3], (D,), 0.3, 1.75, ((0, 32),))
    w_qkv = bell_draw(key_list[4], (D, 3 * D), D ** -0.5, 0.125, ((0, 32),))
    bias_q = bell_draw(key_list[5], (D,), 0.5, 3.0, ((0, 32),))
    bias_v = bell_draw(key_list[6], (D,), 0.5, 3.0, ((0, 32),))
    w_out = bell_draw(key_list[7], (D, D), (D // 4) ** -0.5, 0.25, ((0, 32),))
    b_out = bell_draw(key_list[8], (D,), 0.3, 1.75, ((0, 32),))
    ln2_gain = jnp.clip(1.0 + 0.18 * jax.random.normal(key_list[9], (D,), jnp.float32), 0.099609375, 1.8984375).astype(jnp.bfloat16)
    ln2_bias = bell_draw(key_list[10], (D,), 0.3, 1.75, ((0, 32),))
    w_up = bell_draw(key_list[11], (D, FF), D ** -0.5, 0.125, ((0, 32),))
    b_up = bell_draw(key_list[12], (FF,), 0.5, 3.0, ((0, 32),))
    w_down = bell_draw(key_list[13], (FF, D), FF ** -0.5, 0.0625, ((0, 32),))
    b_down = bell_draw(key_list[14], (D,), 0.3, 1.75, ((0, 32),))
    cotangent = bell_draw_with(key_list[15], (SEQS, SEQ_LEN, D), 1.0, 6.0, ((0, 2), (1, 16)), (1, 2, 16, 2.0))
    return {"tokens": tokens, "doc_lengths": doc_lengths, "ln1_gain": ln1_gain, "ln1_bias": ln1_bias, "w_qkv": w_qkv, "bias_q": bias_q, "bias_v": bias_v, "w_out": w_out, "b_out": b_out, "ln2_gain": ln2_gain, "ln2_bias": ln2_bias, "w_up": w_up, "b_up": b_up, "w_down": w_down, "b_down": b_down, "cotangent": cotangent}


@jax.custom_vjp
def low(v):
    return lax.optimization_barrier(v.astype(jnp.bfloat16)).astype(jnp.float32)

@jax.custom_vjp
def low_back(v):
    return v

def low_keep(v):
    return (low(v), None)

def low_pass(kept, grad):
    return (grad,)

def back_keep(v):
    return (v, None)

def back_low(kept, grad):
    return (low(grad),)
low.defvjp(low_keep, low_pass)
low_back.defvjp(back_keep, back_low)
epsilon = 1e-05
highest = lax.Precision.HIGHEST

def layer_norm(values, gain, shift):
    mean_value = lax.optimization_barrier(jnp.mean(values, axis=-1, keepdims=True))
    centred = values - mean_value
    variance = lax.optimization_barrier(jnp.mean(centred * centred, axis=-1, keepdims=True))
    return centred * lax.rsqrt(variance + epsilon) * gain + shift

def head_slopes(head_count):
    return 2.0 ** (-8.0 * (jnp.arange(head_count, dtype=jnp.float32) + 1.0) / head_count)

def sequence_rows(seq_len):
    half_rows = TOK_DEV // 2
    positions = jnp.arange(seq_len, dtype=jnp.int32)
    block_index = positions // half_rows
    early = block_index < N_CTX
    device_index = jnp.where(early, block_index, 2 * N_CTX - 1 - block_index)
    within = jnp.where(early, positions % half_rows, half_rows + positions % half_rows)
    return (device_index * TOK_DEV + within).astype(jnp.int32)

def layout_positions(seq_len):
    half_rows = TOK_DEV // 2
    row_index = jnp.arange(seq_len, dtype=jnp.int32)
    device_index = row_index // TOK_DEV
    within = row_index % TOK_DEV
    block_index = jnp.where(within < half_rows, device_index, 2 * N_CTX - 1 - device_index)
    return (block_index * half_rows + within % half_rows).astype(jnp.int32)

def attention(queries, key_rows, value_rows, segment_ids):
    seq_len = queries.shape[0]
    block_rows = math.gcd(512, seq_len)
    block_count = seq_len // block_rows
    head_count = queries.shape[1] // HEAD_DIM
    slopes = head_slopes(head_count)
    positions = jnp.arange(seq_len, dtype=jnp.int32)
    key_heads = key_rows.reshape(seq_len, head_count, HEAD_DIM)
    value_heads = value_rows.reshape(seq_len, head_count, HEAD_DIM)

    def one_block(pieces):
        query_block, query_pos, query_seg = pieces
        query_heads = query_block.reshape(block_rows, head_count, HEAD_DIM)
        raw = jnp.einsum('qhd,khd->hqk', query_heads, key_heads, precision=highest) * HEAD_DIM ** (-0.5)
        distance = (query_pos[:, None] - positions[None, :]).astype(jnp.float32)
        scores = low_back(raw - slopes[:, None, None] * distance[None])
        allowed = (query_seg[:, None] == segment_ids[None, :]) & (distance >= 0)
        scores = jnp.where(allowed[None], scores, -1e+30)
        row_top = lax.optimization_barrier(jnp.max(scores, axis=-1, keepdims=True))
        weights = jnp.exp(scores - row_top)
        weights = weights / lax.optimization_barrier(jnp.sum(weights, axis=-1, keepdims=True))
        attended = jnp.einsum('hqk,khd->qhd', low(weights), value_heads, precision=highest)
        return attended.reshape(block_rows, head_count * HEAD_DIM)
    blocks = lax.map(jax.checkpoint(one_block), (queries.reshape(block_count, block_rows, -1), positions.reshape(block_count, block_rows), segment_ids.reshape(block_count, block_rows)))
    return blocks.reshape(seq_len, -1)

def forward(inputs, weights, segment_ids):
    ln1_gain, ln1_bias, w_qkv, bias_q, bias_v, w_out, b_out, ln2_gain, ln2_bias, w_up, b_up, w_down, b_down = weights
    model_width = inputs.shape[1]
    normed = low(layer_norm(inputs, ln1_gain, ln1_bias))
    projected = jnp.dot(normed, w_qkv, precision=highest, preferred_element_type=jnp.float32)
    queries = low(low_back(projected[:, :model_width] + bias_q))
    key_rows = low(low_back(projected[:, model_width:2 * model_width]))
    value_rows = low(low_back(projected[:, 2 * model_width:] + bias_v))
    attended = low(low_back(attention(queries, key_rows, value_rows, segment_ids)))
    branch = low_back(jnp.dot(attended, w_out, precision=highest, preferred_element_type=jnp.float32) + b_out)
    middle = inputs + branch
    normed_two = low(layer_norm(middle, ln2_gain, ln2_bias))
    hidden = low_back(jnp.dot(normed_two, w_up, precision=highest, preferred_element_type=jnp.float32) + b_up)
    activated = low(jax.nn.gelu(hidden, approximate=False))
    out_branch = low_back(jnp.dot(activated, w_down, precision=highest, preferred_element_type=jnp.float32) + b_down)
    return middle + out_branch

def reference(tokens, doc_lengths, ln1_gain, ln1_bias, w_qkv, bias_q, bias_v, w_out, b_out, ln2_gain, ln2_bias, w_up, b_up, w_down, b_down, cotangent):
    params = tuple((weight.astype(jnp.float32) for weight in (ln1_gain, ln1_bias, w_qkv, bias_q, bias_v, w_out, b_out, ln2_gain, ln2_bias, w_up, b_up, w_down, b_down)))
    seq_len = tokens.shape[1]
    to_sequence = sequence_rows(seq_len)
    to_layout = layout_positions(seq_len)
    totals = [jnp.zeros(weight.shape, jnp.float32) for weight in params]
    out_rows = []
    grad_rows = []
    for sequence in range(tokens.shape[0]):
        lengths = doc_lengths[sequence]
        doc_starts = jnp.cumsum(lengths) - lengths
        positions = jnp.arange(seq_len, dtype=jnp.int32)
        segment_ids = (lax.optimization_barrier(jnp.sum((doc_starts[None, :] <= positions[:, None]).astype(jnp.int32), axis=1)) - 1).astype(jnp.int32)
        inputs = tokens[sequence][to_sequence].astype(jnp.float32)
        tangent = cotangent[sequence][to_sequence].astype(jnp.float32)

        def run_layer(layer_in, *weights):
            return forward(layer_in, weights, segment_ids)
        result, pullback = jax.vjp(run_layer, inputs, *params)
        gradients = pullback(tangent)
        out_rows.append(result[to_layout].astype(jnp.bfloat16))
        grad_rows.append(gradients[0][to_layout].astype(jnp.float32))
        totals = [total_grad + piece for total_grad, piece in zip(totals, gradients[1:])]
    return (jnp.stack(out_rows), jnp.stack(grad_rows), totals[0], totals[1], totals[2], totals[3], totals[4], totals[5], totals[6], totals[7], totals[8], totals[9], totals[10], totals[11], totals[12])
```

```python
import functools

import jax
import jax.numpy as jnp
from jax import lax
from jax.experimental import pallas as pl
from jax.experimental.pallas import tpu as pltpu
from jax.sharding import PartitionSpec as P

HEAD_DIM = 64
EPSILON = 1e-05
MASKED = -1e30
BOTH = ("ctx", "fsdp")
NT = (((1,), (1,)), ((), ()))
TN = (((0,), (0,)), ((), ()))
F32 = jnp.float32
BF16 = jnp.bfloat16


def gelu_exact(pre_activation):
    return jax.nn.gelu(pre_activation, approximate=False)


def norm_parts(values):
    centred = values - jnp.mean(values, axis=-1, keepdims=True)
    rate = lax.rsqrt(jnp.mean(centred * centred, axis=-1, keepdims=True) + EPSILON)
    return centred * rate, rate


def norm_back(unit, rate, gain, grad):
    scaled = grad * gain
    return rate * (
        scaled
        - jnp.mean(scaled, axis=-1, keepdims=True)
        - unit * jnp.mean(scaled * unit, axis=-1, keepdims=True)
    )


def block_parts(key_block, query_block, rows):
    key_at = key_block * rows + lax.broadcasted_iota(jnp.int32, (rows, rows), 0)
    query_at = query_block * rows + lax.broadcasted_iota(jnp.int32, (rows, rows), 1)
    return key_at, query_at


def head_mask(values, head):
    lanes = lax.broadcasted_iota(jnp.int32, values.shape, 1)
    return jnp.where(lanes // HEAD_DIM == head, values, jnp.zeros_like(values))


def scores_block(keys, query_head, slope, distance, allowed):
    raw = lax.dot_general(keys, query_head, NT, preferred_element_type=F32)
    return jnp.where(allowed, raw * HEAD_DIM ** (-0.5) - slope * distance, MASKED)


def attend_kernel(rows, heads, low_ref, slope_ref, start_ref, q_ref, k_ref, v_ref, out_ref, total_ref):
    block = pl.program_id(0)
    low = low_ref[block]
    starts = start_ref[...]
    queries = q_ref[...]
    query_heads = [head_mask(queries, head) for head in range(heads)]

    def parts(key_block):
        key_at, query_at = block_parts(key_block, block, rows)
        allowed = (key_at <= query_at) & (key_at >= starts)
        at = pl.ds(pl.multiple_of(key_block * rows, rows), rows)
        return (query_at - key_at).astype(F32), allowed, at

    def total_step(key_block, carried):
        distance, allowed, at = parts(key_block)
        keys = k_ref[at, :]
        following = []
        for head in range(heads):
            top, total = carried[head]
            scores = scores_block(keys, query_heads[head], slope_ref[head], distance, allowed)
            new_top = jnp.maximum(top, jnp.max(scores, axis=0, keepdims=True))
            total = total * jnp.exp(top - new_top) + jnp.sum(
                jnp.exp(scores - new_top), axis=0, keepdims=True
            )
            following.append((new_top, total))
        return following

    begin = [(jnp.full((1, rows), MASKED, F32), jnp.zeros((1, rows), F32))] * heads
    totals = lax.fori_loop(low, block + 1, total_step, begin)
    log_totals = [top + jnp.log(total) for top, total in totals]
    for head in range(heads):
        total_ref[head : head + 1, :] = log_totals[head]

    def output_step(key_block, accum):
        distance, allowed, at = parts(key_block)
        keys = k_ref[at, :]
        values = v_ref[at, :]
        for head in range(heads):
            scores = scores_block(keys, query_heads[head], slope_ref[head], distance, allowed)
            probs = jnp.exp(scores - log_totals[head]).astype(BF16)
            accum = accum + lax.dot_general(
                probs, head_mask(values, head), TN, preferred_element_type=F32
            )
        return accum

    out_ref[...] = lax.fori_loop(low, block + 1, output_step, jnp.zeros(out_ref.shape, F32))


def attend_back_kernel(
    rows, heads, low_ref, slope_ref, start_ref, total_ref, delta_ref, q_ref, g_ref, k_ref, v_ref,
    dq_ref, dk_ref, dv_ref, dk_sum, dv_sum,
):
    block = pl.program_id(0)
    low = low_ref[block]
    starts = start_ref[...]
    query_heads = [head_mask(q_ref[...], head) for head in range(heads)]
    grad_heads = [head_mask(g_ref[...], head) for head in range(heads)]
    log_totals = [total_ref[head : head + 1, :] for head in range(heads)]
    deltas = [delta_ref[head : head + 1, :] for head in range(heads)]

    @pl.when(block == 0)
    def clear():
        dk_sum[...] = jnp.zeros_like(dk_sum)
        dv_sum[...] = jnp.zeros_like(dv_sum)

    def step(key_block, accum):
        key_at, query_at = block_parts(key_block, block, rows)
        allowed = (key_at <= query_at) & (key_at >= starts)
        distance = (query_at - key_at).astype(F32)
        at = pl.ds(pl.multiple_of(key_block * rows, rows), rows)
        keys = k_ref[at, :]
        values = v_ref[at, :]
        dk_part = jnp.zeros(keys.shape, F32)
        dv_part = jnp.zeros(keys.shape, F32)
        for head in range(heads):
            scores = scores_block(keys, query_heads[head], slope_ref[head], distance, allowed)
            probs = jnp.exp(scores - log_totals[head])
            grad_probs = lax.dot_general(values, grad_heads[head], NT, preferred_element_type=F32)
            grad_scores = (probs * (grad_probs - deltas[head])).astype(BF16)
            dv_part = dv_part + jnp.dot(
                probs.astype(BF16), grad_heads[head], preferred_element_type=F32
            )
            dk_part = dk_part + jnp.dot(grad_scores, query_heads[head], preferred_element_type=F32)
            accum = accum + lax.dot_general(
                grad_scores, head_mask(keys, head), TN, preferred_element_type=F32
            )
        dk_sum[at, :] += dk_part
        dv_sum[at, :] += dv_part
        return accum

    grad = lax.fori_loop(low, block + 1, step, jnp.zeros(dq_ref.shape, F32))
    dq_ref[...] = (grad * HEAD_DIM ** (-0.5)).astype(BF16)

    @pl.when(block == pl.num_programs(0) - 1)
    def store():
        dk_ref[...] = (dk_sum[...] * HEAD_DIM ** (-0.5)).astype(BF16)
        dv_ref[...] = dv_sum[...].astype(BF16)


def attend(queries, keys, values, starts, low, slopes, rows):
    seq_len, width = queries.shape
    heads = width // HEAD_DIM
    whole = pl.BlockSpec((seq_len, width), lambda i: (0, 0))
    block = pl.BlockSpec((rows, width), lambda i: (i, 0))
    row = pl.BlockSpec((1, rows), lambda i: (0, i))
    stat = pl.BlockSpec((heads, rows), lambda i: (0, i))
    scalar = pl.BlockSpec(memory_space=pltpu.SMEM)
    return pl.pallas_call(
        functools.partial(attend_kernel, rows, heads),
        grid=(seq_len // rows,),
        in_specs=[scalar, scalar, row, block, whole, whole],
        out_specs=[block, stat],
        out_shape=[
            jax.ShapeDtypeStruct((seq_len, width), F32),
            jax.ShapeDtypeStruct((heads, seq_len), F32),
        ],
        name="attend",
    )(low, slopes, starts, queries, keys, values)


def attend_back(queries, keys, values, grads, starts, low, slopes, log_total, delta, rows):
    seq_len, width = queries.shape
    heads = width // HEAD_DIM
    whole = pl.BlockSpec((seq_len, width), lambda i: (0, 0))
    block = pl.BlockSpec((rows, width), lambda i: (i, 0))
    row = pl.BlockSpec((1, rows), lambda i: (0, i))
    stat = pl.BlockSpec((heads, rows), lambda i: (0, i))
    scalar = pl.BlockSpec(memory_space=pltpu.SMEM)
    return pl.pallas_call(
        functools.partial(attend_back_kernel, rows, heads),
        grid=(seq_len // rows,),
        in_specs=[scalar, scalar, row, stat, stat, block, block, whole, whole],
        out_specs=[block, whole, whole],
        out_shape=[jax.ShapeDtypeStruct((seq_len, width), BF16)] * 3,
        scratch_shapes=[pltpu.VMEM((seq_len, width), F32)] * 2,
        name="attend_back",
    )(low, slopes, starts, log_total, delta, queries, grads, keys, values)


def to_sequence(rows_in, count):
    halves = rows_in.reshape(count, 2, rows_in.shape[0] // (2 * count), -1)
    return jnp.concatenate([halves[:, 0], halves[::-1, 1]], axis=0).reshape(rows_in.shape)


def to_layout(rows_in, count):
    blocks = rows_in.reshape(2, count, rows_in.shape[0] // (2 * count), -1)
    return jnp.stack([blocks[0], blocks[1, ::-1]], axis=1).reshape(rows_in.shape)


def gather_rows(rows_in):
    return lax.all_gather(rows_in, "ctx", axis=0, tiled=True)


def sum_rows(partial):
    return lax.psum_scatter(partial.astype(BF16), "ctx", scatter_dimension=0, tiled=True).astype(F32)


def columns_of_rows(weight, parts):
    count = lax.axis_size("ctx")
    rows = weight.shape[0]
    split = weight.reshape(rows, parts, count, -1).transpose(2, 0, 1, 3)
    mine = lax.all_to_all(split, "ctx", split_axis=0, concat_axis=0)
    both = lax.all_gather(mine, "fsdp", axis=1)
    return both.reshape(count * both.shape[1] * rows, parts, -1)


def rows_of_columns(grad):
    count = lax.axis_size("ctx")
    pair = lax.axis_size("fsdp")
    rows = grad.shape[0] // (count * pair)
    pieces = grad.astype(BF16).reshape(count, pair, rows, *grad.shape[1:])
    summed = lax.psum_scatter(pieces, "fsdp", scatter_dimension=1, tiled=False)
    mine = lax.all_to_all(summed, "ctx", split_axis=0, concat_axis=0)
    return mine.transpose(1, 2, 0, 3).reshape(rows, -1).astype(F32)


def pair_sum(grad):
    return lax.psum_scatter(grad, "fsdp", scatter_dimension=0, tiled=True)


def rows_to_columns(local):
    count = lax.axis_size("ctx")
    rows = local.shape[0]
    split = local.reshape(rows, count, -1).transpose(1, 0, 2)
    mine = lax.all_to_all(split, "ctx", split_axis=0, concat_axis=0)
    return mine.reshape(count * rows, -1)


def columns_to_rows(slice_in):
    count = lax.axis_size("ctx")
    rows = slice_in.shape[0] // count
    mine = lax.all_to_all(slice_in.reshape(count, rows, -1), "ctx", split_axis=0, concat_axis=0)
    return mine.transpose(1, 0, 2).reshape(rows, -1)


def widen(columns, share):
    if share == 1:
        return columns
    count = lax.axis_size("ctx")
    groups = [list(range(first, first + share)) for first in range(0, count, share)]
    return lax.all_gather(
        columns, "ctx", axis=columns.ndim - 1, tiled=True, axis_index_groups=groups
    )


def narrow(columns, share):
    if share == 1:
        return columns
    width = columns.shape[-1] // share
    place = lax.rem(lax.axis_index("ctx"), share)
    return lax.dynamic_slice_in_dim(columns, place * width, width, columns.ndim - 1)


def on_device(
    tokens, doc_lengths, ln1_gain, ln1_bias, w_qkv, bias_q, bias_v, w_out, b_out,
    ln2_gain, ln2_bias, w_up, b_up, w_down, b_down, cotangent,
):
    count = lax.axis_size("ctx")
    rank = lax.axis_index("ctx")
    pair_rank = lax.axis_index("fsdp")
    tok_rows, width = tokens.shape[1:]
    seq_len = tok_rows * count
    own_cols = width // count
    share = max(1, HEAD_DIM // own_cols)
    head_count = width // HEAD_DIM
    heads = own_cols * share // HEAD_DIM
    rows = min(256, seq_len)

    lengths = doc_lengths[0]
    doc_starts = jnp.cumsum(lengths) - lengths
    positions = jnp.arange(seq_len, dtype=jnp.int32)
    starts = jnp.max(
        jnp.where(doc_starts[None, :] <= positions[:, None], doc_starts[None, :], 0), axis=1
    ).astype(jnp.int32)
    low = starts[::rows] // rows
    starts = starts[None, :]
    first_head = (rank // share) * heads
    head_ids = (first_head + jnp.arange(heads)).astype(F32)
    slopes = 2.0 ** (-8.0 * (head_ids + 1.0) / head_count)

    vectors = jnp.stack([ln1_gain, ln1_bias, b_out, ln2_gain, ln2_bias, b_down])
    vectors = lax.all_gather(vectors, BOTH, axis=1, tiled=True).astype(F32)
    gain_one, shift_one, b_out_all, gain_two, shift_two, b_down_all = vectors
    pair_vectors = lax.all_gather(jnp.stack([bias_q, bias_v]), "fsdp", axis=1, tiled=True)
    pair_vectors = widen(pair_vectors.astype(F32), share)
    b_up_own = lax.all_gather(b_up, "fsdp", axis=0, tiled=True).astype(F32)

    w_qkv_own = columns_of_rows(w_qkv, 3)
    w_qkv_head = widen(w_qkv_own, share).reshape(width, -1)
    w_qkv_own = w_qkv_own.reshape(width, -1)
    w_up_own = columns_of_rows(w_up, 1).reshape(width, -1)
    w_down_own = lax.all_gather(w_down, "fsdp", axis=0, tiled=True)
    w_out_all = lax.all_gather(w_out, BOTH, axis=0, tiled=True)

    inputs = tokens[0].astype(F32)
    unit_one, rate_one = norm_parts(inputs)
    normed = (unit_one * gain_one + shift_one).astype(BF16)
    normed_all = gather_rows(normed)
    grad_out = cotangent[0]
    grad_out_all = gather_rows(grad_out)

    projected = jnp.dot(normed_all, w_qkv_head, preferred_element_type=F32)
    head_width = heads * HEAD_DIM
    shift = jnp.concatenate([pair_vectors[0], jnp.zeros(head_width, F32), pair_vectors[1]])
    projected = to_sequence((projected + shift).astype(BF16), count)
    queries, keys, values = (
        projected[:, part * head_width : (part + 1) * head_width] for part in range(3)
    )
    attended_full, log_total = attend(queries, keys, values, starts, low, slopes, rows)
    attended_own = narrow(to_layout(attended_full.astype(BF16), count), share)
    attended = columns_to_rows(attended_own)
    middle = inputs + jnp.dot(attended, w_out_all, preferred_element_type=F32) + b_out_all

    unit_two, rate_two = norm_parts(middle)
    normed_two = (unit_two * gain_two + shift_two).astype(BF16)
    normed_two_all = gather_rows(normed_two)
    hidden = jnp.dot(normed_two_all, w_up_own, preferred_element_type=F32) + b_up_own
    activated, gelu_pull = jax.vjp(gelu_exact, hidden)
    activated = activated.astype(BF16)

    grad_activated = lax.dot_general(grad_out_all, w_down_own, NT, preferred_element_type=F32)
    grad_hidden = gelu_pull(grad_activated)[0].astype(BF16)
    grad_normed_two = sum_rows(
        lax.dot_general(grad_hidden, w_up_own, NT, preferred_element_type=F32)
    )
    branch = sum_rows(jnp.dot(activated, w_down_own, preferred_element_type=F32))
    outputs = (middle + branch + b_down_all).astype(BF16)

    grad_w_down = pair_sum(
        lax.dot_general(activated, grad_out_all, TN, preferred_element_type=F32).astype(BF16)
    ).astype(F32)
    grad_w_up = rows_of_columns(
        lax.dot_general(normed_two_all, grad_hidden, TN, preferred_element_type=F32)[:, None]
    )
    grad_b_up = pair_sum(jnp.sum(grad_hidden.astype(F32), axis=0))
    own = rank * own_cols
    grad_b_down = pair_sum(
        jnp.sum(lax.dynamic_slice_in_dim(grad_out_all, own, own_cols, 1).astype(F32), axis=0)
    )

    grad_middle = grad_out.astype(F32) + norm_back(unit_two, rate_two, gain_two, grad_normed_two)
    grad_branch = grad_middle.astype(BF16)
    grad_attended = lax.dot_general(
        grad_branch, w_out_all, NT, preferred_element_type=F32
    ).astype(BF16)
    grad_heads = to_sequence(widen(rows_to_columns(grad_attended), share), count)
    grad_branch_all = gather_rows(grad_branch)
    grad_w_out = pair_sum(
        lax.dot_general(attended_own, grad_branch_all, TN, preferred_element_type=F32).astype(BF16)
    ).astype(F32)
    grad_b_out = pair_sum(
        jnp.sum(lax.dynamic_slice_in_dim(grad_branch_all, own, own_cols, 1).astype(F32), axis=0)
    )

    delta = (grad_heads.astype(F32) * attended_full).reshape(seq_len, heads, HEAD_DIM)
    delta = jnp.sum(delta, axis=-1).T
    grad_parts = attend_back(
        queries, keys, values, grad_heads, starts, low, slopes, log_total, delta, rows
    )
    grad_qkv = jnp.concatenate(
        [narrow(to_layout(part, count), share) for part in grad_parts], axis=1
    )
    column_sums = jnp.sum(grad_qkv.astype(F32), axis=0)
    grad_bias_q = pair_sum(column_sums[:own_cols])
    grad_bias_v = pair_sum(column_sums[2 * own_cols :])
    grad_normed = sum_rows(lax.dot_general(grad_qkv, w_qkv_own, NT, preferred_element_type=F32))
    grad_w_qkv = rows_of_columns(
        lax.dot_general(normed_all, grad_qkv, TN, preferred_element_type=F32).reshape(
            width, 3, own_cols
        )
    )
    grad_inputs = grad_middle + norm_back(unit_one, rate_one, gain_one, grad_normed)

    norm_sums = jnp.stack(
        [
            jnp.sum(grad_normed * unit_one, axis=0),
            jnp.sum(grad_normed, axis=0),
            jnp.sum(grad_normed_two * unit_two, axis=0),
            jnp.sum(grad_normed_two, axis=0),
        ]
    )
    norm_sums = lax.psum_scatter(norm_sums, BOTH, scatter_dimension=1, tiled=True)
    return (
        outputs[None],
        grad_inputs[None],
        norm_sums[0],
        norm_sums[1],
        grad_w_qkv,
        grad_bias_q,
        grad_bias_v,
        grad_w_out,
        grad_b_out,
        norm_sums[2],
        norm_sums[3],
        grad_w_up,
        grad_b_up,
        grad_w_down,
        grad_b_down,
    )


def solution(mesh):
    spread = P(BOTH)
    matrix = P(BOTH, None)
    rows = P("fsdp", "ctx", None)
    placed = (
        rows, P("fsdp", None), spread, spread, matrix, spread, spread, matrix, spread,
        spread, spread, matrix, spread, matrix, spread, rows,
    )
    results = (
        rows, rows, spread, spread, matrix, spread, spread, matrix, spread,
        spread, spread, matrix, spread, matrix, spread,
    )
    return jax.shard_map(
        on_device, mesh=mesh, in_specs=placed, out_specs=results, check_vma=False
    )
```

```python
import functools

import jax
import jax.numpy as jnp
from jax import lax
from jax.experimental import pallas as pl
from jax.experimental.pallas import tpu as pltpu
from jax.sharding import PartitionSpec as P

HEAD_DIM = 64
EPSILON = 1e-05
MASKED = -1e30
BOTH = ("ctx", "fsdp")
NT = (((1,), (1,)), ((), ()))
TN = (((0,), (0,)), ((), ()))
F32 = jnp.float32
BF16 = jnp.bfloat16


def gelu_exact(pre_activation):
    return jax.nn.gelu(pre_activation, approximate=False)


def norm_parts(values):
    centred = values - jnp.mean(values, axis=-1, keepdims=True)
    rate = lax.rsqrt(jnp.mean(centred * centred, axis=-1, keepdims=True) + EPSILON)
    return centred * rate, rate


def norm_back(unit, rate, gain, grad):
    scaled = grad * gain
    return rate * (
        scaled
        - jnp.mean(scaled, axis=-1, keepdims=True)
        - unit * jnp.mean(scaled * unit, axis=-1, keepdims=True)
    )


def block_parts(key_block, query_block, rows):
    key_at = key_block * rows + lax.broadcasted_iota(jnp.int32, (rows, rows), 0)
    query_at = query_block * rows + lax.broadcasted_iota(jnp.int32, (rows, rows), 1)
    return key_at, query_at


def head_mask(values, head):
    lanes = lax.broadcasted_iota(jnp.int32, values.shape, 1)
    return jnp.where(lanes // HEAD_DIM == head, values, jnp.zeros_like(values))


def scores_block(keys, query_head, slope, distance, allowed):
    raw = lax.dot_general(keys, query_head, NT, preferred_element_type=F32)
    return jnp.where(allowed, raw * HEAD_DIM ** (-0.5) - slope * distance, MASKED)


def attend_kernel(rows, heads, low_ref, slope_ref, start_ref, q_ref, k_ref, v_ref, out_ref, total_ref):
    block = pl.program_id(0)
    low = low_ref[block]
    starts = start_ref[...]
    queries = q_ref[...]
    query_heads = [head_mask(queries, head) for head in range(heads)]

    def parts(key_block):
        key_at, query_at = block_parts(key_block, block, rows)
        allowed = (key_at <= query_at) & (key_at >= starts)
        at = pl.ds(pl.multiple_of(key_block * rows, rows), rows)
        return (query_at - key_at).astype(F32), allowed, at

    def total_step(key_block, carried):
        distance, allowed, at = parts(key_block)
        keys = k_ref[at, :]
        following = []
        for head in range(heads):
            top, total = carried[head]
            scores = scores_block(keys, query_heads[head], slope_ref[head], distance, allowed)
            new_top = jnp.maximum(top, jnp.max(scores, axis=0, keepdims=True))
            total = total * jnp.exp(top - new_top) + jnp.sum(
                jnp.exp(scores - new_top), axis=0, keepdims=True
            )
            following.append((new_top, total))
        return following

    begin = [(jnp.full((1, rows), MASKED, F32), jnp.zeros((1, rows), F32))] * heads
    totals = lax.fori_loop(low, block + 1, total_step, begin)
    log_totals = [top + jnp.log(total) for top, total in totals]
    for head in range(heads):
        total_ref[head : head + 1, :] = log_totals[head]

    def output_step(key_block, accum):
        distance, allowed, at = parts(key_block)
        keys = k_ref[at, :]
        values = v_ref[at, :]
        for head in range(heads):
            scores = scores_block(keys, query_heads[head], slope_ref[head], distance, allowed)
            probs = jnp.exp(scores - log_totals[head]).astype(BF16)
            accum = accum + lax.dot_general(
                probs, head_mask(values, head), TN, preferred_element_type=F32
            )
        return accum

    out_ref[...] = lax.fori_loop(low, block + 1, output_step, jnp.zeros(out_ref.shape, F32))


def attend_back_kernel(
    rows, heads, low_ref, slope_ref, start_ref, total_ref, delta_ref, q_ref, g_ref, k_ref, v_ref,
    dq_ref, dk_ref, dv_ref, dk_sum, dv_sum,
):
    block = pl.program_id(0)
    low = low_ref[block]
    starts = start_ref[...]
    query_heads = [head_mask(q_ref[...], head) for head in range(heads)]
    grad_heads = [head_mask(g_ref[...], head) for head in range(heads)]
    log_totals = [total_ref[head : head + 1, :] for head in range(heads)]
    deltas = [delta_ref[head : head + 1, :] for head in range(heads)]

    @pl.when(block == 0)
    def clear():
        dk_sum[...] = jnp.zeros_like(dk_sum)
        dv_sum[...] = jnp.zeros_like(dv_sum)

    def step(key_block, accum):
        key_at, query_at = block_parts(key_block, block, rows)
        allowed = (key_at <= query_at) & (key_at >= starts)
        distance = (query_at - key_at).astype(F32)
        at = pl.ds(pl.multiple_of(key_block * rows, rows), rows)
        keys = k_ref[at, :]
        values = v_ref[at, :]
        dk_part = jnp.zeros(keys.shape, F32)
        dv_part = jnp.zeros(keys.shape, F32)
        for head in range(heads):
            scores = scores_block(keys, query_heads[head], slope_ref[head], distance, allowed)
            probs = jnp.exp(scores - log_totals[head])
            grad_probs = lax.dot_general(values, grad_heads[head], NT, preferred_element_type=F32)
            grad_scores = (probs * (grad_probs - deltas[head])).astype(BF16)
            dv_part = dv_part + jnp.dot(
                probs.astype(BF16), grad_heads[head], preferred_element_type=F32
            )
            dk_part = dk_part + jnp.dot(grad_scores, query_heads[head], preferred_element_type=F32)
            accum = accum + lax.dot_general(
                grad_scores, head_mask(keys, head), TN, preferred_element_type=F32
            )
        dk_sum[at, :] += dk_part
        dv_sum[at, :] += dv_part
        return accum

    grad = lax.fori_loop(low, block + 1, step, jnp.zeros(dq_ref.shape, F32))
    dq_ref[...] = (grad * HEAD_DIM ** (-0.5)).astype(BF16)

    @pl.when(block == pl.num_programs(0) - 1)
    def store():
        dk_ref[...] = (dk_sum[...] * HEAD_DIM ** (-0.5)).astype(BF16)
        dv_ref[...] = dv_sum[...].astype(BF16)


def attend(queries, keys, values, starts, low, slopes, rows):
    seq_len, width = queries.shape
    heads = width // HEAD_DIM
    whole = pl.BlockSpec((seq_len, width), lambda i: (0, 0))
    block = pl.BlockSpec((rows, width), lambda i: (i, 0))
    row = pl.BlockSpec((1, rows), lambda i: (0, i))
    stat = pl.BlockSpec((heads, rows), lambda i: (0, i))
    scalar = pl.BlockSpec(memory_space=pltpu.SMEM)
    return pl.pallas_call(
        functools.partial(attend_kernel, rows, heads),
        grid=(seq_len // rows,),
        in_specs=[scalar, scalar, row, block, whole, whole],
        out_specs=[block, stat],
        out_shape=[
            jax.ShapeDtypeStruct((seq_len, width), F32),
            jax.ShapeDtypeStruct((heads, seq_len), F32),
        ],
        name="attend",
    )(low, slopes, starts, queries, keys, values)


def attend_back(queries, keys, values, grads, starts, low, slopes, log_total, delta, rows):
    seq_len, width = queries.shape
    heads = width // HEAD_DIM
    whole = pl.BlockSpec((seq_len, width), lambda i: (0, 0))
    block = pl.BlockSpec((rows, width), lambda i: (i, 0))
    row = pl.BlockSpec((1, rows), lambda i: (0, i))
    stat = pl.BlockSpec((heads, rows), lambda i: (0, i))
    scalar = pl.BlockSpec(memory_space=pltpu.SMEM)
    return pl.pallas_call(
        functools.partial(attend_back_kernel, rows, heads),
        grid=(seq_len // rows,),
        in_specs=[scalar, scalar, row, stat, stat, block, block, whole, whole],
        out_specs=[block, whole, whole],
        out_shape=[jax.ShapeDtypeStruct((seq_len, width), BF16)] * 3,
        scratch_shapes=[pltpu.VMEM((seq_len, width), F32)] * 2,
        name="attend_back",
    )(low, slopes, starts, log_total, delta, queries, grads, keys, values)


def to_sequence(rows_in, count):
    halves = rows_in.reshape(count, 2, rows_in.shape[0] // (2 * count), -1)
    return jnp.concatenate([halves[:, 0], halves[::-1, 1]], axis=0).reshape(rows_in.shape)


def to_layout(rows_in, count):
    blocks = rows_in.reshape(2, count, rows_in.shape[0] // (2 * count), -1)
    return jnp.stack([blocks[0], blocks[1, ::-1]], axis=1).reshape(rows_in.shape)


def gather_beside(rows_in):
    return lax.all_gather(rows_in, "ctx", axis=0, tiled=True)


def sum_beside(partial):
    return lax.psum_scatter(partial.astype(BF16), "ctx", scatter_dimension=0, tiled=True).astype(F32)


def from_pair(mine):
    return lax.ppermute(mine, "fsdp", [(0, 1), (1, 0)])


def pair_gather(mine, axis):
    other = from_pair(mine)
    first = lax.axis_index("fsdp") == 0
    return jnp.where(
        first, jnp.stack([mine, other], axis=axis), jnp.stack([other, mine], axis=axis)
    )


def pair_reduce(grad, axis):
    here = lax.axis_index("fsdp")
    given = lax.dynamic_index_in_dim(grad, 1 - here, axis, keepdims=False).astype(BF16)
    kept = lax.dynamic_index_in_dim(grad, here, axis, keepdims=False)
    return kept.astype(F32) + from_pair(given).astype(F32)


def exchange(blocks):
    total, width = blocks.shape
    tiles = -(-width // 1024) * 8
    padded = jnp.pad(blocks, ((0, 0), (0, tiles * 128 - width))).reshape(total, tiles, 128)
    got = lax.all_to_all(padded, BOTH, split_axis=0, concat_axis=0)
    return got.reshape(total, tiles * 128)[:, :width]


MESH_ID = pl.DeviceIdType.MESH

def remote(source, target, send_sem, recv_sem, device):
    return pltpu.make_async_remote_copy(
        src_ref=source, dst_ref=target, send_sem=send_sem, recv_sem=recv_sem,
        device_id=device, device_id_type=MESH_ID,
    )


def place_of(line, side, core):
    return (line * 2 + side) * 2 + core


def own_place():
    me = lax.axis_index("ctx")
    return me, me // 4, (me // 2) % 2, me % 2


def greet(lines):
    me, line, side, core = own_place()
    barrier = pltpu.get_barrier_semaphore()

    def signal(target):
        pl.semaphore_signal(barrier, inc=1, device_id={"ctx": target}, device_id_type=MESH_ID)

    signal(place_of(line, side, 1 - core))
    signal(place_of(line, 1 - side, core))

    @pl.when(line > 0)
    def below():
        signal(me - 4)

    @pl.when(line < lines - 1)
    def above():
        signal(me + 4)

    pl.semaphore_wait(
        barrier, 2 + jnp.where(line > 0, 1, 0) + jnp.where(line < lines - 1, 1, 0)
    )


def gather_kernel(
    count, pieces, own_ref, out_ref, keep_sem, up_sem, down_sem, across_sem, chip_sem, recv_sem
):
    lines = count // 4
    me, line, side, core = own_place()
    partner = place_of(line, side, 1 - core)
    across = place_of(line, 1 - side, core)
    rows = own_ref.shape[0] // pieces

    def part(block, k):
        return out_ref.at[block, pl.ds(pl.multiple_of(k * rows, rows), rows), :]

    def mine(k):
        return own_ref.at[pl.ds(pl.multiple_of(k * rows, rows), rows), :]

    def to_up(source, block, slot, k):
        return remote(source, part(block, k), up_sem.at[slot, k], recv_sem.at[block, k], {"ctx": me + 4})

    def to_down(source, block, slot, k):
        return remote(source, part(block, k), down_sem.at[slot, k], recv_sem.at[block, k], {"ctx": me - 4})

    def to_across(source, block, k):
        return remote(
            source, part(block, k), across_sem.at[block // 4, k], recv_sem.at[block, k], {"ctx": across}
        )

    def to_partner(source, block, k):
        return remote(
            source, part(block, k), chip_sem.at[block // 2, k], recv_sem.at[block, k], {"ctx": partner}
        )

    def arrived(block, k):
        to_partner(part(block, k), block, k).wait_recv()

    def each_piece(body):
        def step(k, carried):
            body(k)
            return carried

        lax.fori_loop(0, pieces, step, 0)

    greet(lines)
    keep = pltpu.make_async_copy(own_ref, out_ref.at[me], keep_sem)
    keep.start()

    def first(k):
        @pl.when(line < lines - 1)
        def up():
            to_up(mine(k), me, 0, k).start()

        @pl.when(line > 0)
        def down():
            to_down(mine(k), me, 0, k).start()

        to_across(mine(k), me, k).start()
        to_partner(mine(k), me, k).start()

    each_piece(first)
    for hops in range(1, lines):
        def relay(k, hops=hops):
            @pl.when(line >= hops)
            def from_below():
                block = me - 4 * hops
                arrived(block, k)
                if hops < lines - 1:
                    @pl.when(line < lines - 1)
                    def up():
                        to_up(part(block, k), block, hops, k).start()

                to_across(part(block, k), block, k).start()
                to_partner(part(block, k), block, k).start()

            @pl.when(line < lines - hops)
            def from_above():
                block = me + 4 * hops
                arrived(block, k)
                if hops < lines - 1:
                    @pl.when(line > 0)
                    def down():
                        to_down(part(block, k), block, hops, k).start()

                to_across(part(block, k), block, k).start()
                to_partner(part(block, k), block, k).start()

        each_piece(relay)

    def hand_over(block):
        def one(k):
            arrived(block, k)
            to_partner(part(block, k), block, k).start()

        each_piece(one)

    hand_over(across)
    for hops in range(1, lines):
        @pl.when(line >= hops)
        def from_below(hops=hops):
            hand_over(across - 4 * hops)

        @pl.when(line < lines - hops)
        def from_above(hops=hops):
            hand_over(across + 4 * hops)

    def settle(index, carried):
        def one(k):
            arrived(index * 2 + 1 - core, k)
            to_partner(part(me, k), index * 2 + core, k).wait_send()

        each_piece(one)
        return carried

    lax.fori_loop(0, count // 2, settle, 0)

    def settle_across(index, carried):
        each_piece(lambda k: to_across(part(me, k), index * 4, k).wait_send())
        return carried

    lax.fori_loop(0, lines, settle_across, 0)
    for hops in range(lines - 1):
        @pl.when((line >= hops) & (line < lines - 1))
        def up(hops=hops):
            each_piece(lambda k: to_up(part(me, k), me, hops, k).wait_send())

        @pl.when((line < lines - hops) & (line > 0))
        def down(hops=hops):
            each_piece(lambda k: to_down(part(me, k), me, hops, k).wait_send())

    keep.wait()


def gather_rows(own, pieces=2):
    count = lax.axis_size("ctx")
    lines = count // 4
    rows, width = own.shape
    gathered = pl.pallas_call(
        functools.partial(gather_kernel, count, pieces),
        out_shape=jax.ShapeDtypeStruct((count, rows, width), own.dtype),
        in_specs=[pl.BlockSpec(memory_space=pltpu.VMEM)],
        out_specs=pl.BlockSpec(memory_space=pl.ANY),
        scratch_shapes=[
            pltpu.SemaphoreType.DMA,
            pltpu.SemaphoreType.DMA((lines, pieces)),
            pltpu.SemaphoreType.DMA((lines, pieces)),
            pltpu.SemaphoreType.DMA((lines, pieces)),
            pltpu.SemaphoreType.DMA((count // 2, pieces)),
            pltpu.SemaphoreType.DMA((count, pieces)),
        ],
        compiler_params=pltpu.CompilerParams(collective_id=0, has_side_effects=True),
        cost_estimate=pl.CostEstimate(flops=0, bytes_accessed=count * rows * width * 16, transcendentals=0),
        name="gather_rows",
    )(own)
    return gathered.reshape(count * rows, width)


def sum_kernel(
    count, pieces, part_ref, out_ref, held, chip_in, across_in, line_in, load_sem,
    chip_send, chip_recv, across_send, across_recv, line_send, line_recv,
):
    lines = count // 4
    me, line, side, core = own_place()
    partner = place_of(line, side, 1 - core)
    across = place_of(line, 1 - side, core)
    rows = out_ref.shape[0] // pieces

    def at(ref, block, k):
        return ref.at[block, pl.ds(pl.multiple_of(k * rows, rows), rows), :]

    def to_partner(pair, k):
        return remote(
            at(part_ref, pair * 2 + 1 - core, k), at(chip_in, pair, k),
            chip_send.at[pair, k], chip_recv.at[pair, k], {"ctx": partner},
        )

    def to_across(goal, k):
        return remote(
            at(held, goal * 2 + 1 - side, k), at(across_in, goal, k),
            across_send.at[goal, k], across_recv.at[goal, k], {"ctx": across},
        )

    def to_next(goal, target, slot, k):
        return remote(
            at(held, goal * 2 + side, k), at(line_in, slot, k),
            line_send.at[goal, k], line_recv.at[slot, k], {"ctx": target},
        )

    def each_piece(body):
        def step(k, carried):
            body(k)
            return carried

        lax.fori_loop(0, pieces, step, 0)

    def far_first(visit):
        for hops in range(lines - 1, 0, -1):
            @pl.when(line + hops < lines)
            def ahead(hops=hops):
                visit(line + hops, 1)

            @pl.when(line >= hops)
            def behind(hops=hops):
                visit(line - hops, -1)

    loads = [
        pltpu.make_async_copy(part_ref.at[pair * 2 + core], held.at[pair], load_sem.at[pair])
        for pair in range(count // 2)
    ]
    for load in loads:
        load.start()
    greet(lines)

    def give(goal, way):
        each_piece(lambda k: to_partner(goal * 2 + 1 - side, k).start())

    def give_same(goal, way):
        each_piece(lambda k: to_partner(goal * 2 + side, k).start())

    far_first(give)
    give(line, 0)
    far_first(give_same)
    give_same(line, 0)
    for load in loads:
        load.wait()

    def read(ref, block, k):
        return ref[block, pl.ds(pl.multiple_of(k * rows, rows), rows), :].astype(F32)

    def write(block, k, value):
        held[block, pl.ds(pl.multiple_of(k * rows, rows), rows), :] = value.astype(held.dtype)

    def cross(goal, way):
        pair = goal * 2 + 1 - side

        def one(k):
            to_partner(pair, k).wait_recv()
            write(pair, k, read(held, pair, k) + read(chip_in, pair, k))
            to_across(goal, k).start()

        each_piece(one)

    far_first(cross)
    cross(line, 0)

    def two_sums(goal, k):
        pair = goal * 2 + side
        to_partner(pair, k).wait_recv()
        to_across(goal, k).wait_recv()
        return read(held, pair, k) + read(chip_in, pair, k) + read(across_in, goal, k)

    def along(goal, way):
        pair = goal * 2 + side
        target = me + 4 * way
        arriving = goal
        if way == 1:
            slot = goal
            fed = line > 0
        else:
            fed = line < lines - 1
            slot = jnp.where(goal == line - 1, lines, goal)

        def one(k):
            total = two_sums(goal, k)
            write(pair, k, total)

            @pl.when(fed)
            def add():
                to_next(goal, target, arriving, k).wait_recv()
                write(pair, k, total + read(line_in, arriving, k))

            to_next(goal, target, slot, k).start()

        each_piece(one)

    far_first(along)

    def last(k):
        span = pl.ds(pl.multiple_of(k * rows, rows), rows)
        out_ref[span, :] = two_sums(line, k)

        @pl.when(line > 0)
        def from_below():
            to_next(line, me, line, k).wait_recv()
            out_ref[span, :] += read(line_in, line, k)

        @pl.when(line < lines - 1)
        def from_above():
            to_next(line, me, lines, k).wait_recv()
            out_ref[span, :] += read(line_in, lines, k)

    each_piece(last)

    def settle(index, carried):
        each_piece(lambda k: to_partner(index, k).wait_send())
        return carried

    lax.fori_loop(0, count // 2, settle, 0)

    def settle_line(goal, carried):
        each_piece(lambda k: to_across(goal, k).wait_send())

        @pl.when(goal != line)
        def sent():
            each_piece(lambda k: to_next(goal, me, goal, k).wait_send())

        return carried

    lax.fori_loop(0, lines, settle_line, 0)


def sum_rows(partial, pieces=2):
    count = lax.axis_size("ctx")
    lines = count // 4
    width = partial.shape[1]
    rows = partial.shape[0] // count
    return pl.pallas_call(
        functools.partial(sum_kernel, count, pieces),
        out_shape=jax.ShapeDtypeStruct((rows, width), F32),
        in_specs=[pl.BlockSpec(memory_space=pl.ANY)],
        out_specs=pl.BlockSpec(memory_space=pltpu.VMEM),
        scratch_shapes=[
            pltpu.VMEM((count // 2, rows, width), BF16),
            pltpu.VMEM((count // 2, rows, width), BF16),
            pltpu.VMEM((lines, rows, width), BF16),
            pltpu.VMEM((lines + 1, rows, width), BF16),
            pltpu.SemaphoreType.DMA((count // 2,)),
            pltpu.SemaphoreType.DMA((count // 2, pieces)),
            pltpu.SemaphoreType.DMA((count // 2, pieces)),
            pltpu.SemaphoreType.DMA((lines, pieces)),
            pltpu.SemaphoreType.DMA((lines, pieces)),
            pltpu.SemaphoreType.DMA((lines, pieces)),
            pltpu.SemaphoreType.DMA((lines + 1, pieces)),
        ],
        compiler_params=pltpu.CompilerParams(
            collective_id=1, has_side_effects=True, vmem_limit_bytes=63 * 2**20
        ),
        cost_estimate=pl.CostEstimate(flops=0, bytes_accessed=count * rows * width * 16, transcendentals=0),
        name="sum_rows",
    )(partial.astype(BF16).reshape(count, rows, width))


def columns_of_rows(weight, parts):
    count = lax.axis_size("ctx")
    rows = weight.shape[0]
    split = weight.reshape(rows, parts, count, -1).transpose(2, 0, 1, 3)
    mine = lax.all_to_all(split, "ctx", split_axis=0, concat_axis=0)
    both = pair_gather(mine, 1)
    return both.reshape(count * both.shape[1] * rows, parts, -1)


def rows_of_columns(grad):
    count = lax.axis_size("ctx")
    pair = lax.axis_size("fsdp")
    rows = grad.shape[0] // (count * pair)
    pieces = grad.reshape(count, pair, rows, *grad.shape[1:])
    summed = pair_reduce(pieces, 1).astype(BF16)
    mine = lax.all_to_all(summed, "ctx", split_axis=0, concat_axis=0)
    return mine.transpose(1, 2, 0, 3).reshape(rows, -1).astype(F32)


def pair_sum(grad):
    return pair_reduce(grad.reshape(2, grad.shape[0] // 2, *grad.shape[1:]), 0)


def rows_to_columns(local):
    count = lax.axis_size("ctx")
    rows = local.shape[0]
    split = local.reshape(rows, count, -1).transpose(1, 0, 2)
    mine = lax.all_to_all(split, "ctx", split_axis=0, concat_axis=0)
    return mine.reshape(count * rows, -1)


def columns_to_rows(slice_in):
    count = lax.axis_size("ctx")
    rows = slice_in.shape[0] // count
    mine = lax.all_to_all(slice_in.reshape(count, rows, -1), "ctx", split_axis=0, concat_axis=0)
    return mine.transpose(1, 0, 2).reshape(rows, -1)


def widen(columns, share):
    if share == 1:
        return columns
    count = lax.axis_size("ctx")
    groups = [list(range(first, first + share)) for first in range(0, count, share)]
    return lax.all_gather(
        columns, "ctx", axis=columns.ndim - 1, tiled=True, axis_index_groups=groups
    )


def narrow(columns, share):
    if share == 1:
        return columns
    width = columns.shape[-1] // share
    place = lax.rem(lax.axis_index("ctx"), share)
    return lax.dynamic_slice_in_dim(columns, place * width, width, columns.ndim - 1)


def on_device(
    tokens, doc_lengths, ln1_gain, ln1_bias, w_qkv, bias_q, bias_v, w_out, b_out,
    ln2_gain, ln2_bias, w_up, b_up, w_down, b_down, cotangent,
):
    count = lax.axis_size("ctx")
    rank = lax.axis_index("ctx")
    pair_rank = lax.axis_index("fsdp")
    tok_rows, width = tokens.shape[1:]
    seq_len = tok_rows * count
    own_cols = width // count
    share = max(1, HEAD_DIM // own_cols)
    head_count = width // HEAD_DIM
    heads = own_cols * share // HEAD_DIM
    rows = min(256, seq_len)

    lengths = doc_lengths[0]
    doc_starts = jnp.cumsum(lengths) - lengths
    positions = jnp.arange(seq_len, dtype=jnp.int32)
    starts = jnp.max(
        jnp.where(doc_starts[None, :] <= positions[:, None], doc_starts[None, :], 0), axis=1
    ).astype(jnp.int32)
    low = starts[::rows] // rows
    starts = starts[None, :]
    first_head = (rank // share) * heads
    head_ids = (first_head + jnp.arange(heads)).astype(F32)
    slopes = 2.0 ** (-8.0 * (head_ids + 1.0) / head_count)

    vectors = [ln1_gain, ln1_bias, b_out, ln2_gain, ln2_bias, b_down, bias_q, bias_v, b_up]
    devices = count * lax.axis_size("fsdp")
    own_vectors = jnp.concatenate([vector.astype(F32) for vector in vectors])
    everywhere = exchange(jnp.broadcast_to(own_vectors, (devices, own_vectors.shape[0])))
    at = 0
    whole_vectors = []
    for vector in vectors:
        whole_vectors.append(everywhere[:, at : at + vector.shape[0]].reshape(-1))
        at += vector.shape[0]
    gain_one, shift_one, b_out_all, gain_two, shift_two, b_down_all = whole_vectors[:6]
    head_at = first_head * HEAD_DIM
    bias_q_own, bias_v_own = (
        lax.dynamic_slice_in_dim(vector, head_at, heads * HEAD_DIM) for vector in whole_vectors[6:8]
    )
    ff_cols = whole_vectors[8].shape[0] // count
    b_up_own = lax.dynamic_slice_in_dim(whole_vectors[8], rank * ff_cols, ff_cols)

    w_qkv_own = columns_of_rows(w_qkv, 3)
    w_qkv_head = widen(w_qkv_own, share).reshape(width, -1)
    w_qkv_own = w_qkv_own.reshape(width, -1)
    w_up_own = columns_of_rows(w_up, 1).reshape(width, -1)
    w_down_own = pair_gather(w_down, 0).reshape(-1, width)
    w_out_all = lax.all_gather(w_out, BOTH, axis=0, tiled=True)

    inputs = tokens[0].astype(F32)
    unit_one, rate_one = norm_parts(inputs)
    normed = (unit_one * gain_one + shift_one).astype(BF16)
    normed_all = gather_rows(normed)
    grad_out = cotangent[0]
    grad_out_all = gather_beside(grad_out)

    projected = jnp.dot(normed_all, w_qkv_head, preferred_element_type=F32)
    head_width = heads * HEAD_DIM
    shift = jnp.concatenate([bias_q_own, jnp.zeros(head_width, F32), bias_v_own])
    projected = to_sequence((projected + shift).astype(BF16), count)
    queries, keys, values = (
        projected[:, part * head_width : (part + 1) * head_width] for part in range(3)
    )
    attended_full, log_total = attend(queries, keys, values, starts, low, slopes, rows)
    attended_own = narrow(to_layout(attended_full.astype(BF16), count), share)
    attended = columns_to_rows(attended_own)
    middle = inputs + jnp.dot(attended, w_out_all, preferred_element_type=F32) + b_out_all

    unit_two, rate_two = norm_parts(middle)
    normed_two = (unit_two * gain_two + shift_two).astype(BF16)
    normed_two_all = gather_rows(normed_two)
    hidden = jnp.dot(normed_two_all, w_up_own, preferred_element_type=F32) + b_up_own
    activated, gelu_pull = jax.vjp(gelu_exact, hidden)
    activated = activated.astype(BF16)

    grad_activated = lax.dot_general(grad_out_all, w_down_own, NT, preferred_element_type=F32)
    grad_hidden = gelu_pull(grad_activated)[0].astype(BF16)
    grad_normed_two = sum_rows(
        lax.dot_general(grad_hidden, w_up_own, NT, preferred_element_type=F32)
    )
    branch = sum_beside(jnp.dot(activated, w_down_own, preferred_element_type=F32))
    outputs = (middle + branch + b_down_all).astype(BF16)

    grad_w_down = pair_sum(
        lax.dot_general(activated, grad_out_all, TN, preferred_element_type=F32)
    )
    grad_w_up = rows_of_columns(
        lax.dot_general(normed_two_all, grad_hidden, TN, preferred_element_type=F32)[:, None]
    )

    grad_middle = grad_out.astype(F32) + norm_back(unit_two, rate_two, gain_two, grad_normed_two)
    grad_branch = grad_middle.astype(BF16)
    grad_attended = lax.dot_general(
        grad_branch, w_out_all, NT, preferred_element_type=F32
    ).astype(BF16)
    grad_heads = to_sequence(widen(rows_to_columns(grad_attended), share), count)
    grad_branch_all = gather_beside(grad_branch)
    grad_w_out = pair_sum(
        lax.dot_general(attended_own, grad_branch_all, TN, preferred_element_type=F32)
    )

    delta = (grad_heads.astype(F32) * attended_full).reshape(seq_len, heads, HEAD_DIM)
    delta = jnp.sum(delta, axis=-1).T
    grad_parts = attend_back(
        queries, keys, values, grad_heads, starts, low, slopes, log_total, delta, rows
    )
    grad_qkv = jnp.concatenate(
        [narrow(to_layout(part, count), share) for part in grad_parts], axis=1
    )
    column_sums = jnp.sum(grad_qkv.astype(F32), axis=0)
    grad_normed = sum_rows(lax.dot_general(grad_qkv, w_qkv_own, NT, preferred_element_type=F32))
    grad_w_qkv = rows_of_columns(
        lax.dot_general(normed_all, grad_qkv, TN, preferred_element_type=F32).reshape(
            width, 3, own_cols
        )
    )
    grad_inputs = grad_middle + norm_back(unit_one, rate_one, gain_one, grad_normed)

    pair = devices // count
    full_sums = jnp.stack(
        [
            jnp.sum(grad_normed * unit_one, axis=0),
            jnp.sum(grad_normed, axis=0),
            jnp.sum(grad_normed_two * unit_two, axis=0),
            jnp.sum(grad_normed_two, axis=0),
            jnp.sum(grad_branch.astype(F32), axis=0),
            jnp.sum(grad_out.astype(F32), axis=0),
        ]
    )
    full_sums = full_sums.reshape(6, devices, -1).transpose(1, 0, 2).reshape(devices, -1)
    own_sums = jnp.concatenate(
        [
            column_sums[:own_cols].reshape(pair, -1),
            column_sums[2 * own_cols :].reshape(pair, -1),
            jnp.sum(grad_hidden.astype(F32), axis=0).reshape(pair, -1),
        ],
        axis=1,
    )
    here = (jnp.arange(count) == rank)[:, None, None]
    own_sums = jnp.where(here, own_sums[None], 0.0).reshape(devices, -1)
    sums = jnp.sum(exchange(jnp.concatenate([full_sums, own_sums], axis=1)), axis=0)
    share_of = width // devices
    (
        grad_ln1_gain, grad_ln1_bias, grad_ln2_gain, grad_ln2_bias, grad_b_out, grad_b_down,
        grad_bias_q, grad_bias_v,
    ) = sums[: 8 * share_of].reshape(8, share_of)
    grad_b_up = sums[8 * share_of :]
    return (
        outputs[None],
        grad_inputs[None],
        grad_ln1_gain,
        grad_ln1_bias,
        grad_w_qkv,
        grad_bias_q,
        grad_bias_v,
        grad_w_out,
        grad_b_out,
        grad_ln2_gain,
        grad_ln2_bias,
        grad_w_up,
        grad_b_up,
        grad_w_down,
        grad_b_down,
    )


def solution(mesh):
    spread = P(BOTH)
    matrix = P(BOTH, None)
    rows = P("fsdp", "ctx", None)
    placed = (
        rows, P("fsdp", None), spread, spread, matrix, spread, spread, matrix, spread,
        spread, spread, matrix, spread, matrix, spread, rows,
    )
    results = (
        rows, rows, spread, spread, matrix, spread, spread, matrix, spread,
        spread, spread, matrix, spread, matrix, spread,
    )
    return jax.shard_map(
        on_device, mesh=mesh, in_specs=placed, out_specs=results, check_vma=False
    )
```

```python
import functools

import jax
import jax.numpy as jnp
from jax import lax
from jax.experimental import pallas as pl
from jax.experimental.pallas import tpu as pltpu
from jax.sharding import PartitionSpec as P

HEAD_DIM = 64
EPSILON = 1e-05
MASKED = -1e30
BOTH = ("ctx", "fsdp")
NT = (((1,), (1,)), ((), ()))
TN = (((0,), (0,)), ((), ()))
F32 = jnp.float32
BF16 = jnp.bfloat16
BUSY = 160 * 2**20


def gelu_exact(pre_activation):
    return jax.nn.gelu(pre_activation, approximate=False)


def norm_parts(values):
    centred = values - jnp.mean(values, axis=-1, keepdims=True)
    rate = lax.rsqrt(jnp.mean(centred * centred, axis=-1, keepdims=True) + EPSILON)
    return centred * rate, rate


def norm_back(unit, rate, gain, grad):
    scaled = grad * gain
    return rate * (
        scaled
        - jnp.mean(scaled, axis=-1, keepdims=True)
        - unit * jnp.mean(scaled * unit, axis=-1, keepdims=True)
    )


def block_parts(key_block, query_block, rows):
    key_at = key_block * rows + lax.broadcasted_iota(jnp.int32, (rows, rows), 0)
    query_at = query_block * rows + lax.broadcasted_iota(jnp.int32, (rows, rows), 1)
    return key_at, query_at


def head_mask(values, head):
    lanes = lax.broadcasted_iota(jnp.int32, values.shape, 1)
    return jnp.where(lanes // HEAD_DIM == head, values, jnp.zeros_like(values))


def scores_block(keys, query_head, slope, distance, allowed):
    raw = lax.dot_general(keys, query_head, NT, preferred_element_type=F32)
    return jnp.where(allowed, raw * HEAD_DIM ** (-0.5) - slope * distance, MASKED)


def attend_kernel(rows, heads, low_ref, slope_ref, start_ref, q_ref, k_ref, v_ref, out_ref, total_ref):
    block = pl.program_id(0)
    low = low_ref[block]
    starts = start_ref[...]
    queries = q_ref[...]
    query_heads = [head_mask(queries, head) for head in range(heads)]

    def parts(key_block):
        key_at, query_at = block_parts(key_block, block, rows)
        allowed = (key_at <= query_at) & (key_at >= starts)
        at = pl.ds(pl.multiple_of(key_block * rows, rows), rows)
        return (query_at - key_at).astype(F32), allowed, at

    def step(key_block, carried):
        distance, allowed, at = parts(key_block)
        keys = k_ref[at, :]
        values = v_ref[at, :]
        following = []
        for head in range(heads):
            top, total, accum = carried[head]
            scores = scores_block(keys, query_heads[head], slope_ref[head], distance, allowed)
            new_top = jnp.maximum(top, jnp.max(scores, axis=0, keepdims=True))
            shrink = jnp.exp(top - new_top)
            weights = jnp.exp(scores - new_top)
            total = total * shrink + jnp.sum(weights, axis=0, keepdims=True)
            accum = accum * shrink + lax.dot_general(
                values, weights.astype(BF16), TN, preferred_element_type=F32
            )
            following.append((new_top, total, accum))
        return following

    width = out_ref.shape[1]
    begin = (jnp.full((1, rows), MASKED, F32), jnp.zeros((1, rows), F32), jnp.zeros((width, rows), F32))
    done = lax.fori_loop(low, block + 1, step, [begin] * heads)
    for head in range(heads):
        top, total, accum = done[head]
        total_ref[head : head + 1, :] = top + jnp.log(total)
        span = slice(head * HEAD_DIM, (head + 1) * HEAD_DIM)
        out_ref[:, span] = jnp.transpose(accum[span, :] / total)


def attend_back_kernel(
    rows, heads, low_ref, slope_ref, start_ref, total_ref, delta_ref, q_ref, g_ref, k_ref, v_ref,
    dq_ref, dk_ref, dv_ref, dk_sum, dv_sum,
):
    block = pl.program_id(0)
    low = low_ref[block]
    starts = start_ref[...]
    query_heads = [head_mask(q_ref[...], head) for head in range(heads)]
    grad_heads = [head_mask(g_ref[...], head) for head in range(heads)]
    log_totals = [total_ref[head : head + 1, :] for head in range(heads)]
    deltas = [delta_ref[head : head + 1, :] for head in range(heads)]

    @pl.when(block == 0)
    def clear():
        dk_sum[...] = jnp.zeros_like(dk_sum)
        dv_sum[...] = jnp.zeros_like(dv_sum)

    def step(key_block, accum):
        key_at, query_at = block_parts(key_block, block, rows)
        allowed = (key_at <= query_at) & (key_at >= starts)
        distance = (query_at - key_at).astype(F32)
        at = pl.ds(pl.multiple_of(key_block * rows, rows), rows)
        keys = k_ref[at, :]
        values = v_ref[at, :]
        dk_part = jnp.zeros(keys.shape, F32)
        dv_part = jnp.zeros(keys.shape, F32)
        for head in range(heads):
            scores = scores_block(keys, query_heads[head], slope_ref[head], distance, allowed)
            probs = jnp.exp(scores - log_totals[head])
            grad_probs = lax.dot_general(values, grad_heads[head], NT, preferred_element_type=F32)
            grad_scores = (probs * (grad_probs - deltas[head])).astype(BF16)
            dv_part = dv_part + jnp.dot(
                probs.astype(BF16), grad_heads[head], preferred_element_type=F32
            )
            dk_part = dk_part + jnp.dot(grad_scores, query_heads[head], preferred_element_type=F32)
            accum = accum + lax.dot_general(
                grad_scores, head_mask(keys, head), TN, preferred_element_type=F32
            )
        dk_sum[at, :] += dk_part
        dv_sum[at, :] += dv_part
        return accum

    grad = lax.fori_loop(low, block + 1, step, jnp.zeros(dq_ref.shape, F32))
    dq_ref[...] = (grad * HEAD_DIM ** (-0.5)).astype(BF16)

    @pl.when(block == pl.num_programs(0) - 1)
    def store():
        dk_ref[...] = (dk_sum[...] * HEAD_DIM ** (-0.5)).astype(BF16)
        dv_ref[...] = dv_sum[...].astype(BF16)


def attend(queries, keys, values, starts, low, slopes, rows):
    seq_len, width = queries.shape
    heads = width // HEAD_DIM
    whole = pl.BlockSpec((seq_len, width), lambda i: (0, 0))
    block = pl.BlockSpec((rows, width), lambda i: (i, 0))
    row = pl.BlockSpec((1, rows), lambda i: (0, i))
    stat = pl.BlockSpec((heads, rows), lambda i: (0, i))
    scalar = pl.BlockSpec(memory_space=pltpu.SMEM)
    return pl.pallas_call(
        functools.partial(attend_kernel, rows, heads),
        grid=(seq_len // rows,),
        in_specs=[scalar, scalar, row, block, whole, whole],
        out_specs=[block, stat],
        out_shape=[
            jax.ShapeDtypeStruct((seq_len, width), F32),
            jax.ShapeDtypeStruct((heads, seq_len), F32),
        ],
        cost_estimate=pl.CostEstimate(flops=0, bytes_accessed=BUSY // 3, transcendentals=0),
        name="attend",
    )(low, slopes, starts, queries, keys, values)


def attend_back(queries, keys, values, grads, starts, low, slopes, log_total, delta, rows):
    seq_len, width = queries.shape
    heads = width // HEAD_DIM
    whole = pl.BlockSpec((seq_len, width), lambda i: (0, 0))
    block = pl.BlockSpec((rows, width), lambda i: (i, 0))
    row = pl.BlockSpec((1, rows), lambda i: (0, i))
    stat = pl.BlockSpec((heads, rows), lambda i: (0, i))
    scalar = pl.BlockSpec(memory_space=pltpu.SMEM)
    return pl.pallas_call(
        functools.partial(attend_back_kernel, rows, heads),
        grid=(seq_len // rows,),
        in_specs=[scalar, scalar, row, stat, stat, block, block, whole, whole],
        out_specs=[block, whole, whole],
        out_shape=[jax.ShapeDtypeStruct((seq_len, width), BF16)] * 3,
        scratch_shapes=[pltpu.VMEM((seq_len, width), F32)] * 2,
        cost_estimate=pl.CostEstimate(flops=0, bytes_accessed=BUSY // 3, transcendentals=0),
        name="attend_back",
    )(low, slopes, starts, log_total, delta, queries, grads, keys, values)


def to_sequence(rows_in, count):
    halves = rows_in.reshape(count, 2, rows_in.shape[0] // (2 * count), -1)
    return jnp.concatenate([halves[:, 0], halves[::-1, 1]], axis=0).reshape(rows_in.shape)


def to_layout(rows_in, count):
    blocks = rows_in.reshape(2, count, rows_in.shape[0] // (2 * count), -1)
    return jnp.stack([blocks[0], blocks[1, ::-1]], axis=1).reshape(rows_in.shape)


def gather_beside(rows_in):
    return lax.all_gather(rows_in, "ctx", axis=0, tiled=True)


def sum_beside(partial):
    return lax.psum_scatter(partial.astype(BF16), "ctx", scatter_dimension=0, tiled=True).astype(F32)


def from_pair(mine):
    return lax.ppermute(mine, "fsdp", [(0, 1), (1, 0)])


def pair_reduce(grad, axis):
    here = lax.axis_index("fsdp")
    grad = grad.astype(BF16)
    given = lax.dynamic_index_in_dim(grad, 1 - here, axis, keepdims=False)
    kept = lax.dynamic_index_in_dim(grad, here, axis, keepdims=False)
    return kept.astype(F32) + from_pair(given).astype(F32)


def exchange(blocks):
    total, width = blocks.shape
    tiles = -(-width // 1024) * 8
    padded = jnp.pad(blocks, ((0, 0), (0, tiles * 128 - width))).reshape(total, tiles, 128)
    got = lax.all_to_all(padded, BOTH, split_axis=0, concat_axis=0)
    return got.reshape(total, tiles * 128)[:, :width]


MESH_ID = pl.DeviceIdType.MESH

def remote(source, target, send_sem, recv_sem, device):
    return pltpu.make_async_remote_copy(
        src_ref=source, dst_ref=target, send_sem=send_sem, recv_sem=recv_sem,
        device_id=device, device_id_type=MESH_ID,
    )


def place_of(line, side, core):
    return (line * 2 + side) * 2 + core


def own_place():
    me = lax.axis_index("ctx")
    return me, me // 4, (me // 2) % 2, me % 2


def greet(lines):
    me, line, side, core = own_place()
    barrier = pltpu.get_barrier_semaphore()

    def signal(target):
        pl.semaphore_signal(barrier, inc=1, device_id={"ctx": target}, device_id_type=MESH_ID)

    signal(place_of(line, side, 1 - core))
    signal(place_of(line, 1 - side, core))

    @pl.when(line > 0)
    def below():
        signal(me - 4)

    @pl.when(line < lines - 1)
    def above():
        signal(me + 4)

    pl.semaphore_wait(
        barrier, 2 + jnp.where(line > 0, 1, 0) + jnp.where(line < lines - 1, 1, 0)
    )


def gather_kernel(
    count, pieces, own_ref, out_ref, keep_sem, up_sem, down_sem, across_sem, chip_sem, recv_sem
):
    lines = count // 4
    me, line, side, core = own_place()
    partner = place_of(line, side, 1 - core)
    across = place_of(line, 1 - side, core)
    rows = own_ref.shape[0] // pieces

    def part(block, k):
        return out_ref.at[block, pl.ds(pl.multiple_of(k * rows, rows), rows), :]

    def mine(k):
        return own_ref.at[pl.ds(pl.multiple_of(k * rows, rows), rows), :]

    def to_up(source, block, slot, k):
        return remote(source, part(block, k), up_sem.at[slot, k], recv_sem.at[block, k], {"ctx": me + 4})

    def to_down(source, block, slot, k):
        return remote(source, part(block, k), down_sem.at[slot, k], recv_sem.at[block, k], {"ctx": me - 4})

    def to_across(source, block, k):
        return remote(
            source, part(block, k), across_sem.at[block // 4, k], recv_sem.at[block, k], {"ctx": across}
        )

    def to_partner(source, block, k):
        return remote(
            source, part(block, k), chip_sem.at[block // 2, k], recv_sem.at[block, k], {"ctx": partner}
        )

    def arrived(block, k):
        to_partner(part(block, k), block, k).wait_recv()

    def each_piece(body):
        def step(k, carried):
            body(k)
            return carried

        lax.fori_loop(0, pieces, step, 0)

    greet(lines)
    keep = pltpu.make_async_copy(own_ref, out_ref.at[me], keep_sem)
    keep.start()

    def first(k):
        @pl.when(line < lines - 1)
        def up():
            to_up(mine(k), me, 0, k).start()

        @pl.when(line > 0)
        def down():
            to_down(mine(k), me, 0, k).start()

        to_across(mine(k), me, k).start()
        to_partner(mine(k), me, k).start()

    each_piece(first)
    for hops in range(1, lines):
        def relay(k, hops=hops):
            @pl.when(line >= hops)
            def from_below():
                block = me - 4 * hops
                arrived(block, k)
                if hops < lines - 1:
                    @pl.when(line < lines - 1)
                    def up():
                        to_up(part(block, k), block, hops, k).start()

                to_across(part(block, k), block, k).start()
                to_partner(part(block, k), block, k).start()

            @pl.when(line < lines - hops)
            def from_above():
                block = me + 4 * hops
                arrived(block, k)
                if hops < lines - 1:
                    @pl.when(line > 0)
                    def down():
                        to_down(part(block, k), block, hops, k).start()

                to_across(part(block, k), block, k).start()
                to_partner(part(block, k), block, k).start()

        each_piece(relay)

    def hand_over(block):
        def one(k):
            arrived(block, k)
            to_partner(part(block, k), block, k).start()

        each_piece(one)

    hand_over(across)
    for hops in range(1, lines):
        @pl.when(line >= hops)
        def from_below(hops=hops):
            hand_over(across - 4 * hops)

        @pl.when(line < lines - hops)
        def from_above(hops=hops):
            hand_over(across + 4 * hops)

    def settle(index, carried):
        def one(k):
            arrived(index * 2 + 1 - core, k)
            to_partner(part(me, k), index * 2 + core, k).wait_send()

        each_piece(one)
        return carried

    lax.fori_loop(0, count // 2, settle, 0)

    def settle_across(index, carried):
        each_piece(lambda k: to_across(part(me, k), index * 4, k).wait_send())
        return carried

    lax.fori_loop(0, lines, settle_across, 0)
    for hops in range(lines - 1):
        @pl.when((line >= hops) & (line < lines - 1))
        def up(hops=hops):
            each_piece(lambda k: to_up(part(me, k), me, hops, k).wait_send())

        @pl.when((line < lines - hops) & (line > 0))
        def down(hops=hops):
            each_piece(lambda k: to_down(part(me, k), me, hops, k).wait_send())

    keep.wait()


def gather_rows(own, pieces=2):
    count = lax.axis_size("ctx")
    lines = count // 4
    rows, width = own.shape
    gathered = pl.pallas_call(
        functools.partial(gather_kernel, count, pieces),
        out_shape=jax.ShapeDtypeStruct((count, rows, width), own.dtype),
        in_specs=[pl.BlockSpec(memory_space=pltpu.VMEM)],
        out_specs=pl.BlockSpec(memory_space=pl.ANY),
        scratch_shapes=[
            pltpu.SemaphoreType.DMA,
            pltpu.SemaphoreType.DMA((lines, pieces)),
            pltpu.SemaphoreType.DMA((lines, pieces)),
            pltpu.SemaphoreType.DMA((lines, pieces)),
            pltpu.SemaphoreType.DMA((count // 2, pieces)),
            pltpu.SemaphoreType.DMA((count, pieces)),
        ],
        compiler_params=pltpu.CompilerParams(collective_id=0, has_side_effects=True),
        cost_estimate=pl.CostEstimate(flops=0, bytes_accessed=BUSY, transcendentals=0),
        name="gather_rows",
    )(own)
    return gathered.reshape(count * rows, width)


def begin_kernel(count, pieces, shared, *refs):
    inputs = len(shared) + 2
    own_ref, sources, down_ref = refs[0], refs[1 : inputs - 1], refs[inputs - 1]
    out_ref, targets, down_out = refs[inputs], refs[inputs + 1 : 2 * inputs - 1], refs[2 * inputs - 1]
    (
        keep_sem, up_sem, down_sem, across_sem, chip_sem, recv_sem,
        give_sem, take_sem, pass_sem, passed_sem, stay_sem, pair_sem,
    ) = refs[2 * inputs :]
    lines = count // 4
    me, line, side, core = own_place()
    half = lax.axis_index("fsdp")
    partner = place_of(line, side, 1 - core)
    across = place_of(line, 1 - side, core)
    rows = own_ref.shape[0] // pieces

    barrier = pltpu.get_barrier_semaphore()

    def enter(step, carried):
        pl.semaphore_signal(
            barrier, inc=1, device_id={"ctx": lax.rem(me + step, count)}, device_id_type=MESH_ID
        )
        return carried

    lax.fori_loop(1, count, enter, 0)
    pl.semaphore_signal(barrier, inc=1, device_id={"fsdp": 1 - half}, device_id_type=MESH_ID)
    pl.semaphore_wait(barrier, count)

    moves = []
    for source, target, (parts, kind) in zip(sources, targets, shared):
        wide = target.shape[2] // parts
        for part in range(parts):
            def block(goal, source=source, part=part, kind=kind, wide=wide, parts=parts):
                if kind == "same":
                    return source
                if kind == "blocks":
                    return source.at[goal]
                first = part * (source.shape[1] // parts) + goal * wide
                return source.at[:, pl.ds(pl.multiple_of(first, 128), wide)]

            def place(sender, side_of, target=target, part=part, wide=wide, parts=parts):
                at = target.at[sender * 2 + side_of]
                return at if parts == 1 else at.at[:, pl.ds(part * wide, wide)]

            moves.append((block, place))

    def origin(step):
        return lax.rem(me + count - step, count)

    def give(step, m):
        goal = lax.rem(me + step, count)
        block, place = moves[m]
        return remote(block(goal), place(me, half), give_sem.at[step, m], take_sem.at[step, m], {"ctx": goal})

    def taken(step, m):
        at = moves[m][1](origin(step), half)
        return remote(at, at, give_sem.at[step, m], take_sem.at[step, m], {"ctx": origin(step)})

    def hand(step, m, side_of):
        at = moves[m][1](origin(step), side_of)
        return remote(at, at, pass_sem.at[step, m], passed_sem.at[step, m], {"fsdp": 1 - half})

    def hand_own(m):
        block, place = moves[m]
        return remote(block(me), place(me, half), pass_sem.at[0, m], passed_sem.at[0, m], {"fsdp": 1 - half})

    def stay(m):
        block, place = moves[m]
        return pltpu.make_async_copy(block(me), place(me, half), stay_sem.at[m])

    def each_step(first, last, body):
        def step_body(step, carried):
            for m in range(len(moves)):
                body(step, m)
            return carried

        lax.fori_loop(first, last, step_body, 0)

    down_stay = pltpu.make_async_copy(down_ref, down_out.at[half], stay_sem.at[len(moves)])

    def down_pair(side_of):
        return remote(down_ref, down_out.at[side_of], pair_sem.at[0], pair_sem.at[1], {"fsdp": 1 - half})

    def part(block, k):
        return out_ref.at[block, pl.ds(pl.multiple_of(k * rows, rows), rows), :]

    def mine(k):
        return own_ref.at[pl.ds(pl.multiple_of(k * rows, rows), rows), :]

    def to_up(source, block, slot, k):
        return remote(source, part(block, k), up_sem.at[slot, k], recv_sem.at[block, k], {"ctx": me + 4})

    def to_down(source, block, slot, k):
        return remote(source, part(block, k), down_sem.at[slot, k], recv_sem.at[block, k], {"ctx": me - 4})

    def to_across(source, block, k):
        return remote(
            source, part(block, k), across_sem.at[block // 4, k], recv_sem.at[block, k], {"ctx": across}
        )

    def to_partner(source, block, k):
        return remote(
            source, part(block, k), chip_sem.at[block // 2, k], recv_sem.at[block, k], {"ctx": partner}
        )

    def arrived(block, k):
        to_partner(part(block, k), block, k).wait_recv()

    def each_piece(body):
        def step(k, carried):
            body(k)
            return carried

        lax.fori_loop(0, pieces, step, 0)

    keep = pltpu.make_async_copy(own_ref, out_ref.at[me], keep_sem)

    def first(k):
        @pl.when(line < lines - 1)
        def up():
            to_up(mine(k), me, 0, k).start()

        @pl.when(line > 0)
        def down():
            to_down(mine(k), me, 0, k).start()

        to_across(mine(k), me, k).start()
        to_partner(mine(k), me, k).start()

    each_piece(first)
    each_step(1, count, lambda step, m: give(step, m).start())
    down_pair(half).start()
    for m in range(len(moves)):
        hand_own(m).start()
    keep.start()
    down_stay.start()
    for m in range(len(moves)):
        stay(m).start()

    def pass_on(step, m):
        taken(step, m).wait_recv()
        hand(step, m, half).start()

    for hops in range(1, lines):
        def relay(k, hops=hops):
            @pl.when(line >= hops)
            def from_below():
                block = me - 4 * hops
                arrived(block, k)
                if hops < lines - 1:
                    @pl.when(line < lines - 1)
                    def up():
                        to_up(part(block, k), block, hops, k).start()

                to_across(part(block, k), block, k).start()
                to_partner(part(block, k), block, k).start()

            @pl.when(line < lines - hops)
            def from_above():
                block = me + 4 * hops
                arrived(block, k)
                if hops < lines - 1:
                    @pl.when(line > 0)
                    def down():
                        to_down(part(block, k), block, hops, k).start()

                to_across(part(block, k), block, k).start()
                to_partner(part(block, k), block, k).start()

        each_piece(relay)
        each_step(
            1 + (hops - 1) * (count - 1) // (lines - 1), 1 + hops * (count - 1) // (lines - 1), pass_on
        )

    def hand_over(block):
        def one(k):
            arrived(block, k)
            to_partner(part(block, k), block, k).start()

        each_piece(one)

    hand_over(across)
    for hops in range(1, lines):
        @pl.when(line >= hops)
        def from_below(hops=hops):
            hand_over(across - 4 * hops)

        @pl.when(line < lines - hops)
        def from_above(hops=hops):
            hand_over(across + 4 * hops)

    def settle(index, carried):
        def one(k):
            arrived(index * 2 + 1 - core, k)
            to_partner(part(me, k), index * 2 + core, k).wait_send()

        each_piece(one)
        return carried

    lax.fori_loop(0, count // 2, settle, 0)

    def settle_across(index, carried):
        each_piece(lambda k: to_across(part(me, k), index * 4, k).wait_send())
        return carried

    lax.fori_loop(0, lines, settle_across, 0)
    for hops in range(lines - 1):
        @pl.when((line >= hops) & (line < lines - 1))
        def up(hops=hops):
            each_piece(lambda k: to_up(part(me, k), me, hops, k).wait_send())

        @pl.when((line < lines - hops) & (line > 0))
        def down(hops=hops):
            each_piece(lambda k: to_down(part(me, k), me, hops, k).wait_send())

    each_step(0, count, lambda step, m: hand(step, m, 1 - half).wait_recv())
    each_step(1, count, lambda step, m: hand(step, m, half).wait_send())
    each_step(1, count, lambda step, m: give(step, m).wait_send())
    for m in range(len(moves)):
        hand_own(m).wait_send()
        stay(m).wait()
    down_pair(1 - half).wait_recv()
    down_pair(half).wait_send()
    down_stay.wait()
    keep.wait()


def begin(own, w_qkv, w_up, w_down, vectors, pieces=2):
    count = lax.axis_size("ctx")
    lines = count // 4
    rows, width = own.shape
    owned = w_qkv.shape[0]
    qkv_cols = w_qkv.shape[1] // count
    up_cols = w_up.shape[1] // count
    if qkv_cols % 384 == 0:
        shared = [(3, "columns")]
    else:
        w_qkv = w_qkv.reshape(owned, 3, count, -1).transpose(2, 0, 1, 3).reshape(count, owned, qkv_cols)
        shared = [(1, "blocks")]
    shared += [(1, "columns"), (1, "same")]
    moves = sum(parts for parts, _ in shared)
    in_vmem = pl.BlockSpec(memory_space=pltpu.VMEM)
    anywhere = pl.BlockSpec(memory_space=pl.ANY)
    rows_all, qkv, up, vectors_all, down = pl.pallas_call(
        functools.partial(begin_kernel, count, pieces, tuple(shared)),
        out_shape=[
            jax.ShapeDtypeStruct((count, rows, width), own.dtype),
            jax.ShapeDtypeStruct((count * 2, owned, qkv_cols), BF16),
            jax.ShapeDtypeStruct((count * 2, owned, up_cols), BF16),
            jax.ShapeDtypeStruct((count * 2, *vectors.shape), F32),
            jax.ShapeDtypeStruct((2, *w_down.shape), BF16),
        ],
        in_specs=[in_vmem] * 5,
        out_specs=[anywhere] * 5,
        scratch_shapes=[
            pltpu.SemaphoreType.DMA,
            pltpu.SemaphoreType.DMA((lines, pieces)),
            pltpu.SemaphoreType.DMA((lines, pieces)),
            pltpu.SemaphoreType.DMA((lines, pieces)),
            pltpu.SemaphoreType.DMA((count // 2, pieces)),
            pltpu.SemaphoreType.DMA((count, pieces)),
            pltpu.SemaphoreType.DMA((count, moves)),
            pltpu.SemaphoreType.DMA((count, moves)),
            pltpu.SemaphoreType.DMA((count, moves)),
            pltpu.SemaphoreType.DMA((count, moves)),
            pltpu.SemaphoreType.DMA((moves + 1,)),
            pltpu.SemaphoreType.DMA((2,)),
        ],
        compiler_params=pltpu.CompilerParams(collective_id=3, has_side_effects=True),
        cost_estimate=pl.CostEstimate(flops=0, bytes_accessed=BUSY, transcendentals=0),
        name="begin",
    )(own, w_qkv, w_up, vectors, w_down)
    return (
        rows_all.reshape(count * rows, width),
        qkv.reshape(-1, qkv_cols),
        up.reshape(-1, up_cols),
        down.reshape(-1, width),
        vectors_all.reshape(count * 2, -1),
    )


def project_kernel(rows_ref, gain_ref, shift_ref, weight_ref, bias_ref, normed_ref, out_ref):
    unit, _ = norm_parts(rows_ref[...].astype(F32))
    normed = (unit * gain_ref[...] + shift_ref[...]).astype(BF16)
    normed_ref[...] = normed
    projected = jnp.dot(normed, weight_ref[...], preferred_element_type=F32)
    out_ref[...] = (projected + bias_ref[...]).astype(BF16)


def project(rows_in, gain, shift, weight, bias, block=256):
    total, width = rows_in.shape
    columns = weight.shape[1]
    row = pl.BlockSpec((1, width), lambda i: (0, 0))
    return pl.pallas_call(
        project_kernel,
        grid=(total // block,),
        in_specs=[
            pl.BlockSpec((block, width), lambda i: (i, 0)),
            row,
            row,
            pl.BlockSpec((width, columns), lambda i: (0, 0)),
            pl.BlockSpec((1, columns), lambda i: (0, 0)),
        ],
        out_specs=[
            pl.BlockSpec((block, width), lambda i: (i, 0)),
            pl.BlockSpec((block, columns), lambda i: (i, 0)),
        ],
        out_shape=[
            jax.ShapeDtypeStruct((total, width), BF16),
            jax.ShapeDtypeStruct((total, columns), BF16),
        ],
        cost_estimate=pl.CostEstimate(
            flops=2 * total * width * columns, bytes_accessed=6 * total * width, transcendentals=0
        ),
        name="project",
    )(rows_in, gain[None], shift[None], weight, bias[None])


def sum_kernel(
    count, pieces, part_ref, out_ref, held, chip_in, across_in, line_in, load_sem,
    chip_send, chip_recv, across_send, across_recv, line_send, line_recv,
):
    lines = count // 4
    me, line, side, core = own_place()
    partner = place_of(line, side, 1 - core)
    across = place_of(line, 1 - side, core)
    rows = out_ref.shape[0] // pieces

    def at(ref, block, k):
        return ref.at[block, pl.ds(pl.multiple_of(k * rows, rows), rows), :]

    def to_partner(pair, k):
        return remote(
            at(part_ref, pair * 2 + 1 - core, k), at(chip_in, pair, k),
            chip_send.at[pair, k], chip_recv.at[pair, k], {"ctx": partner},
        )

    def to_across(goal, k):
        return remote(
            at(held, goal * 2 + 1 - side, k), at(across_in, goal, k),
            across_send.at[goal, k], across_recv.at[goal, k], {"ctx": across},
        )

    def to_next(goal, target, slot, k):
        return remote(
            at(held, goal * 2 + side, k), at(line_in, slot, k),
            line_send.at[goal, k], line_recv.at[slot, k], {"ctx": target},
        )

    def each_piece(body):
        def step(k, carried):
            body(k)
            return carried

        lax.fori_loop(0, pieces, step, 0)

    def far_first(visit):
        for hops in range(lines - 1, 0, -1):
            @pl.when(line + hops < lines)
            def ahead(hops=hops):
                visit(line + hops, 1)

            @pl.when(line >= hops)
            def behind(hops=hops):
                visit(line - hops, -1)

    loads = [
        pltpu.make_async_copy(part_ref.at[pair * 2 + core], held.at[pair], load_sem.at[pair])
        for pair in range(count // 2)
    ]
    for load in loads:
        load.start()
    greet(lines)

    def give(goal, way):
        each_piece(lambda k: to_partner(goal * 2 + 1 - side, k).start())

    def give_same(goal, way):
        each_piece(lambda k: to_partner(goal * 2 + side, k).start())

    far_first(give)
    give(line, 0)
    far_first(give_same)
    give_same(line, 0)
    for load in loads:
        load.wait()

    def read(ref, block, k):
        return ref[block, pl.ds(pl.multiple_of(k * rows, rows), rows), :].astype(F32)

    def write(block, k, value):
        held[block, pl.ds(pl.multiple_of(k * rows, rows), rows), :] = value.astype(held.dtype)

    def cross(goal, way):
        pair = goal * 2 + 1 - side

        def one(k):
            to_partner(pair, k).wait_recv()
            write(pair, k, read(held, pair, k) + read(chip_in, pair, k))
            to_across(goal, k).start()

        each_piece(one)

    far_first(cross)
    cross(line, 0)

    def two_sums(goal, k):
        pair = goal * 2 + side
        to_partner(pair, k).wait_recv()
        to_across(goal, k).wait_recv()
        return read(held, pair, k) + read(chip_in, pair, k) + read(across_in, goal, k)

    def along(goal, way):
        pair = goal * 2 + side
        target = me + 4 * way
        arriving = goal
        if way == 1:
            slot = goal
            fed = line > 0
        else:
            fed = line < lines - 1
            slot = jnp.where(goal == line - 1, lines, goal)

        def one(k):
            total = two_sums(goal, k)
            write(pair, k, total)

            @pl.when(fed)
            def add():
                to_next(goal, target, arriving, k).wait_recv()
                write(pair, k, total + read(line_in, arriving, k))

            to_next(goal, target, slot, k).start()

        each_piece(one)

    far_first(along)

    def last(k):
        span = pl.ds(pl.multiple_of(k * rows, rows), rows)
        out_ref[span, :] = two_sums(line, k)

        @pl.when(line > 0)
        def from_below():
            to_next(line, me, line, k).wait_recv()
            out_ref[span, :] += read(line_in, line, k)

        @pl.when(line < lines - 1)
        def from_above():
            to_next(line, me, lines, k).wait_recv()
            out_ref[span, :] += read(line_in, lines, k)

    each_piece(last)

    def settle(index, carried):
        each_piece(lambda k: to_partner(index, k).wait_send())
        return carried

    lax.fori_loop(0, count // 2, settle, 0)

    def settle_line(goal, carried):
        each_piece(lambda k: to_across(goal, k).wait_send())

        @pl.when(goal != line)
        def sent():
            each_piece(lambda k: to_next(goal, me, goal, k).wait_send())

        return carried

    lax.fori_loop(0, lines, settle_line, 0)


def sum_rows(partial, pieces=2):
    count = lax.axis_size("ctx")
    lines = count // 4
    width = partial.shape[1]
    rows = partial.shape[0] // count
    return pl.pallas_call(
        functools.partial(sum_kernel, count, pieces),
        out_shape=jax.ShapeDtypeStruct((rows, width), F32),
        in_specs=[pl.BlockSpec(memory_space=pl.ANY)],
        out_specs=pl.BlockSpec(memory_space=pltpu.VMEM),
        scratch_shapes=[
            pltpu.VMEM((count // 2, rows, width), BF16),
            pltpu.VMEM((count // 2, rows, width), BF16),
            pltpu.VMEM((lines, rows, width), BF16),
            pltpu.VMEM((lines + 1, rows, width), BF16),
            pltpu.SemaphoreType.DMA((count // 2,)),
            pltpu.SemaphoreType.DMA((count // 2, pieces)),
            pltpu.SemaphoreType.DMA((count // 2, pieces)),
            pltpu.SemaphoreType.DMA((lines, pieces)),
            pltpu.SemaphoreType.DMA((lines, pieces)),
            pltpu.SemaphoreType.DMA((lines, pieces)),
            pltpu.SemaphoreType.DMA((lines + 1, pieces)),
        ],
        compiler_params=pltpu.CompilerParams(
            collective_id=1, has_side_effects=True, vmem_limit_bytes=63 * 2**20
        ),
        cost_estimate=pl.CostEstimate(flops=0, bytes_accessed=BUSY, transcendentals=0),
        name="sum_rows",
    )(partial.astype(BF16).reshape(count, rows, width))


def weight_grad(rows_in, grads):
    terms = lax.dot_general(rows_in, grads, TN, preferred_element_type=F32).astype(BF16)
    return lax.optimization_barrier(terms)


def rows_of_columns(grad):
    count = lax.axis_size("ctx")
    pair = lax.axis_size("fsdp")
    rows = grad.shape[0] // (count * pair)
    pieces = grad.reshape(count, pair, rows, *grad.shape[1:])
    summed = pair_reduce(pieces, 1).astype(BF16)
    mine = lax.all_to_all(summed, "ctx", split_axis=0, concat_axis=0)
    return mine.transpose(1, 2, 0, 3).reshape(rows, -1).astype(F32)


def pair_sum(grad):
    return pair_reduce(grad.reshape(2, grad.shape[0] // 2, *grad.shape[1:]), 0)


def rows_to_columns(local):
    count = lax.axis_size("ctx")
    rows = local.shape[0]
    split = local.reshape(rows, count, -1).transpose(1, 0, 2)
    mine = lax.all_to_all(split, "ctx", split_axis=0, concat_axis=0)
    return mine.reshape(count * rows, -1)


def columns_to_rows(slice_in):
    count = lax.axis_size("ctx")
    rows = slice_in.shape[0] // count
    mine = lax.all_to_all(slice_in.reshape(count, rows, -1), "ctx", split_axis=0, concat_axis=0)
    return mine.transpose(1, 0, 2).reshape(rows, -1)


def widen(columns, share):
    if share == 1:
        return columns
    count = lax.axis_size("ctx")
    groups = [list(range(first, first + share)) for first in range(0, count, share)]
    return lax.all_gather(
        columns, "ctx", axis=columns.ndim - 1, tiled=True, axis_index_groups=groups
    )


def narrow(columns, share):
    if share == 1:
        return columns
    width = columns.shape[-1] // share
    place = lax.rem(lax.axis_index("ctx"), share)
    return lax.dynamic_slice_in_dim(columns, place * width, width, columns.ndim - 1)


def on_device(
    tokens, doc_lengths, ln1_gain, ln1_bias, w_qkv, bias_q, bias_v, w_out, b_out,
    ln2_gain, ln2_bias, w_up, b_up, w_down, b_down, cotangent,
):
    count = lax.axis_size("ctx")
    rank = lax.axis_index("ctx")
    pair_rank = lax.axis_index("fsdp")
    tok_rows, width = tokens.shape[1:]
    seq_len = tok_rows * count
    own_cols = width // count
    share = max(1, HEAD_DIM // own_cols)
    head_count = width // HEAD_DIM
    heads = own_cols * share // HEAD_DIM
    rows = min(256, seq_len)

    lengths = doc_lengths[0]
    doc_starts = jnp.cumsum(lengths) - lengths
    positions = jnp.arange(seq_len, dtype=jnp.int32)
    starts = jnp.max(
        jnp.where(doc_starts[None, :] <= positions[:, None], doc_starts[None, :], 0), axis=1
    ).astype(jnp.int32)
    low = starts[::rows] // rows
    starts = starts[None, :]
    first_head = (rank // share) * heads
    head_ids = (first_head + jnp.arange(heads)).astype(F32)
    slopes = 2.0 ** (-8.0 * (head_ids + 1.0) / head_count)

    vectors = [ln1_gain, ln1_bias, b_out, ln2_gain, ln2_bias, b_down, bias_q, bias_v, b_up]
    devices = count * lax.axis_size("fsdp")
    own_vectors = jnp.concatenate([vector.astype(F32) for vector in vectors])
    tiles = -(-own_vectors.shape[0] // 1024) * 8
    own_vectors = jnp.pad(own_vectors, (0, tiles * 128 - own_vectors.shape[0])).reshape(tiles, 128)
    tokens_all, w_qkv_own, w_up_own, w_down_own, everywhere = begin(
        tokens[0], w_qkv, w_up, w_down, own_vectors
    )
    at = 0
    whole_vectors = []
    for vector in vectors:
        whole_vectors.append(everywhere[:, at : at + vector.shape[0]].reshape(-1))
        at += vector.shape[0]
    gain_one, shift_one, b_out_all, gain_two, shift_two, b_down_all = whole_vectors[:6]
    head_at = first_head * HEAD_DIM
    bias_q_own, bias_v_own = (
        lax.dynamic_slice_in_dim(vector, head_at, heads * HEAD_DIM) for vector in whole_vectors[6:8]
    )
    ff_cols = whole_vectors[8].shape[0] // count
    b_up_own = lax.dynamic_slice_in_dim(whole_vectors[8], rank * ff_cols, ff_cols)

    w_qkv_head = widen(w_qkv_own.reshape(width, 3, -1), share).reshape(width, -1)
    w_out_all = lax.all_gather(w_out, BOTH, axis=0, tiled=True)

    inputs = tokens[0].astype(F32)
    unit_one, rate_one = norm_parts(inputs)
    grad_out = cotangent[0]
    tokens_all, cotangent_rows = lax.optimization_barrier((tokens_all, grad_out))
    grad_out_all = gather_beside(cotangent_rows)

    head_width = heads * HEAD_DIM
    shift = jnp.concatenate([bias_q_own, jnp.zeros(head_width, F32), bias_v_own])
    normed_all, projected = project(tokens_all, gain_one, shift_one, w_qkv_head, shift)
    projected = to_sequence(projected, count)
    queries, keys, values = (
        projected[:, part * head_width : (part + 1) * head_width] for part in range(3)
    )
    attended_full, log_total = attend(queries, keys, values, starts, low, slopes, rows)
    attended_own = narrow(to_layout(attended_full.astype(BF16), count), share)
    attended = columns_to_rows(attended_own)
    middle = inputs + jnp.dot(attended, w_out_all, preferred_element_type=F32) + b_out_all

    unit_two, rate_two = norm_parts(middle)
    normed_two = (unit_two * gain_two + shift_two).astype(BF16)
    normed_two_all = gather_rows(normed_two)
    hidden = jnp.dot(normed_two_all, w_up_own, preferred_element_type=F32) + b_up_own
    activated, gelu_pull = jax.vjp(gelu_exact, hidden)
    activated = activated.astype(BF16)

    grad_activated = lax.dot_general(grad_out_all, w_down_own, NT, preferred_element_type=F32)
    grad_hidden = gelu_pull(grad_activated)[0].astype(BF16)
    grad_normed_two = sum_rows(
        lax.dot_general(grad_hidden, w_up_own, NT, preferred_element_type=F32)
    )
    grad_w_down = pair_sum(weight_grad(activated, grad_out_all))
    grad_w_up = weight_grad(normed_two_all, grad_hidden)
    grad_w_up = rows_of_columns(grad_w_up[:, None])

    grad_middle = grad_out.astype(F32) + norm_back(unit_two, rate_two, gain_two, grad_normed_two)
    grad_branch = grad_middle.astype(BF16)
    grad_attended = lax.dot_general(
        grad_branch, w_out_all, NT, preferred_element_type=F32
    ).astype(BF16)
    grad_attended, late = lax.optimization_barrier((grad_attended, activated))
    grad_heads = to_sequence(widen(rows_to_columns(grad_attended), share), count)
    grad_branch_all = gather_beside(grad_branch)
    branch = sum_beside(jnp.dot(late, w_down_own, preferred_element_type=F32))
    grad_w_out = pair_sum(weight_grad(attended_own, grad_branch_all))

    delta = (grad_heads.astype(F32) * attended_full).reshape(seq_len, heads, HEAD_DIM)
    delta = jnp.sum(delta, axis=-1).T
    grad_parts = attend_back(
        queries, keys, values, grad_heads, starts, low, slopes, log_total, delta, rows
    )
    grad_qkv = jnp.concatenate(
        [narrow(to_layout(part, count), share) for part in grad_parts], axis=1
    )
    column_sums = jnp.sum(grad_qkv.astype(F32), axis=0)
    grad_normed = sum_rows(lax.dot_general(grad_qkv, w_qkv_own, NT, preferred_element_type=F32))
    grad_w_qkv = weight_grad(normed_all, grad_qkv)
    grad_w_qkv = rows_of_columns(grad_w_qkv.reshape(width, 3, own_cols))
    branch, middle, grad_normed = lax.optimization_barrier((branch, middle, grad_normed))
    outputs = (middle + branch + b_down_all).astype(BF16)
    grad_inputs = grad_middle + norm_back(unit_one, rate_one, gain_one, grad_normed)

    pair = devices // count
    full_sums = jnp.stack(
        [
            jnp.sum(grad_normed * unit_one, axis=0),
            jnp.sum(grad_normed, axis=0),
            jnp.sum(grad_normed_two * unit_two, axis=0),
            jnp.sum(grad_normed_two, axis=0),
            jnp.sum(grad_branch.astype(F32), axis=0),
            jnp.sum(grad_out.astype(F32), axis=0),
        ]
    )
    full_sums = full_sums.reshape(6, devices, -1).transpose(1, 0, 2).reshape(devices, -1)
    own_sums = jnp.concatenate(
        [
            column_sums[:own_cols].reshape(pair, -1),
            column_sums[2 * own_cols :].reshape(pair, -1),
            jnp.sum(grad_hidden.astype(F32), axis=0).reshape(pair, -1),
        ],
        axis=1,
    )
    here = (jnp.arange(count) == rank)[:, None, None]
    own_sums = jnp.where(here, own_sums[None], 0.0).reshape(devices, -1)
    sums = jnp.sum(exchange(jnp.concatenate([full_sums, own_sums], axis=1)), axis=0)
    share_of = width // devices
    (
        grad_ln1_gain, grad_ln1_bias, grad_ln2_gain, grad_ln2_bias, grad_b_out, grad_b_down,
        grad_bias_q, grad_bias_v,
    ) = sums[: 8 * share_of].reshape(8, share_of)
    grad_b_up = sums[8 * share_of :]
    return (
        outputs[None],
        grad_inputs[None],
        grad_ln1_gain,
        grad_ln1_bias,
        grad_w_qkv,
        grad_bias_q,
        grad_bias_v,
        grad_w_out,
        grad_b_out,
        grad_ln2_gain,
        grad_ln2_bias,
        grad_w_up,
        grad_b_up,
        grad_w_down,
        grad_b_down,
    )


def solution(mesh):
    spread = P(BOTH)
    matrix = P(BOTH, None)
    rows = P("fsdp", "ctx", None)
    placed = (
        rows, P("fsdp", None), spread, spread, matrix, spread, spread, matrix, spread,
        spread, spread, matrix, spread, matrix, spread, rows,
    )
    results = (
        rows, rows, spread, spread, matrix, spread, spread, matrix, spread,
        spread, spread, matrix, spread, matrix, spread,
    )
    return jax.shard_map(
        on_device, mesh=mesh, in_specs=placed, out_specs=results, check_vma=False
    )
```

```python
import functools
import math

import jax
import jax.numpy as jnp
from jax import lax
from jax.experimental import pallas as pl
from jax.experimental.pallas import tpu as pltpu
from jax.sharding import PartitionSpec as P

HEAD_DIM = 64
EPSILON = 1e-05
MASKED = -1e30
BOTH = ("ctx", "fsdp")
NT = (((1,), (1,)), ((), ()))
TN = (((0,), (0,)), ((), ()))
F32 = jnp.float32
BF16 = jnp.bfloat16
BUSY = 160 * 2**20


def norm_parts(values):
    centred = values - jnp.mean(values, axis=-1, keepdims=True)
    rate = lax.rsqrt(jnp.mean(centred * centred, axis=-1, keepdims=True) + EPSILON)
    return centred * rate, rate


def norm_back(unit, rate, gain, grad):
    scaled = grad * gain
    return rate * (
        scaled
        - jnp.mean(scaled, axis=-1, keepdims=True)
        - unit * jnp.mean(scaled * unit, axis=-1, keepdims=True)
    )


def block_parts(key_block, query_block, rows):
    key_at = key_block * rows + lax.broadcasted_iota(jnp.int32, (rows, rows), 0)
    query_at = query_block * rows + lax.broadcasted_iota(jnp.int32, (rows, rows), 1)
    return key_at, query_at


def head_mask(values, head):
    lanes = lax.broadcasted_iota(jnp.int32, values.shape, 1)
    return jnp.where(lanes // HEAD_DIM == head, values, jnp.zeros_like(values))


def scores_block(keys, query_head, slope, distance, allowed):
    raw = lax.dot_general(keys, query_head, NT, preferred_element_type=F32)
    return jnp.where(allowed, raw * HEAD_DIM ** (-0.5) - slope * distance, MASKED)


def attend_kernel(rows, heads, low_ref, slope_ref, start_ref, q_ref, k_ref, v_ref, out_ref, total_ref):
    block = pl.program_id(0)
    low = low_ref[block]
    starts = start_ref[...]
    queries = q_ref[...]
    query_heads = [head_mask(queries, head) for head in range(heads)]

    def parts(key_block):
        key_at, query_at = block_parts(key_block, block, rows)
        allowed = (key_at <= query_at) & (key_at >= starts)
        at = pl.ds(pl.multiple_of(key_block * rows, rows), rows)
        return (query_at - key_at).astype(F32), allowed, at

    def step(key_block, carried):
        distance, allowed, at = parts(key_block)
        keys = k_ref[at, :]
        values = v_ref[at, :]
        following = []
        for head in range(heads):
            top, total, accum = carried[head]
            scores = scores_block(keys, query_heads[head], slope_ref[head], distance, allowed)
            new_top = jnp.maximum(top, jnp.max(scores, axis=0, keepdims=True))
            shrink = jnp.exp(top - new_top)
            weights = jnp.exp(scores - new_top)
            total = total * shrink + jnp.sum(weights, axis=0, keepdims=True)
            accum = accum * shrink + lax.dot_general(
                values, weights.astype(BF16), TN, preferred_element_type=F32
            )
            following.append((new_top, total, accum))
        return following

    width = out_ref.shape[1]
    begin = (jnp.full((1, rows), MASKED, F32), jnp.zeros((1, rows), F32), jnp.zeros((width, rows), F32))
    done = lax.fori_loop(low, block + 1, step, [begin] * heads)
    for head in range(heads):
        top, total, accum = done[head]
        total_ref[head : head + 1, :] = top + jnp.log(total)
        span = slice(head * HEAD_DIM, (head + 1) * HEAD_DIM)
        out_ref[:, span] = jnp.transpose(accum[span, :] / total)


def attend_back_kernel(
    rows, heads, low_ref, slope_ref, start_ref, total_ref, delta_ref, q_ref, g_ref, k_ref, v_ref,
    dq_ref, dk_ref, dv_ref, dk_sum, dv_sum,
):
    block = pl.program_id(0)
    low = low_ref[block]
    starts = start_ref[...]
    query_heads = [head_mask(q_ref[...], head) for head in range(heads)]
    grad_heads = [head_mask(g_ref[...], head) for head in range(heads)]
    log_totals = [total_ref[head : head + 1, :] for head in range(heads)]
    deltas = [delta_ref[head : head + 1, :] for head in range(heads)]

    @pl.when(block == 0)
    def clear():
        dk_sum[...] = jnp.zeros_like(dk_sum)
        dv_sum[...] = jnp.zeros_like(dv_sum)

    def step(key_block, accum):
        key_at, query_at = block_parts(key_block, block, rows)
        allowed = (key_at <= query_at) & (key_at >= starts)
        distance = (query_at - key_at).astype(F32)
        at = pl.ds(pl.multiple_of(key_block * rows, rows), rows)
        keys = k_ref[at, :]
        values = v_ref[at, :]
        dk_part = jnp.zeros(keys.shape, F32)
        dv_part = jnp.zeros(keys.shape, F32)
        for head in range(heads):
            scores = scores_block(keys, query_heads[head], slope_ref[head], distance, allowed)
            probs = jnp.exp(scores - log_totals[head])
            grad_probs = lax.dot_general(values, grad_heads[head], NT, preferred_element_type=F32)
            grad_scores = (probs * (grad_probs - deltas[head])).astype(BF16)
            dv_part = dv_part + jnp.dot(
                probs.astype(BF16), grad_heads[head], preferred_element_type=F32
            )
            dk_part = dk_part + jnp.dot(grad_scores, query_heads[head], preferred_element_type=F32)
            accum = accum + lax.dot_general(
                grad_scores, head_mask(keys, head), TN, preferred_element_type=F32
            )
        dk_sum[at, :] += dk_part
        dv_sum[at, :] += dv_part
        return accum

    grad = lax.fori_loop(low, block + 1, step, jnp.zeros(dq_ref.shape, F32))
    dq_ref[...] = (grad * HEAD_DIM ** (-0.5)).astype(BF16)

    @pl.when(block == pl.num_programs(0) - 1)
    def store():
        dk_ref[...] = (dk_sum[...] * HEAD_DIM ** (-0.5)).astype(BF16)
        dv_ref[...] = dv_sum[...].astype(BF16)


def attend(queries, keys, values, starts, low, slopes, rows):
    seq_len, width = queries.shape
    heads = width // HEAD_DIM
    whole = pl.BlockSpec((seq_len, width), lambda i: (0, 0))
    block = pl.BlockSpec((rows, width), lambda i: (i, 0))
    row = pl.BlockSpec((1, rows), lambda i: (0, i))
    stat = pl.BlockSpec((heads, rows), lambda i: (0, i))
    scalar = pl.BlockSpec(memory_space=pltpu.SMEM)
    return pl.pallas_call(
        functools.partial(attend_kernel, rows, heads),
        grid=(seq_len // rows,),
        in_specs=[scalar, scalar, row, block, whole, whole],
        out_specs=[block, stat],
        out_shape=[
            jax.ShapeDtypeStruct((seq_len, width), F32),
            jax.ShapeDtypeStruct((heads, seq_len), F32),
        ],
        cost_estimate=pl.CostEstimate(flops=0, bytes_accessed=BUSY // 3, transcendentals=0),
        name="attend",
    )(low, slopes, starts, queries, keys, values)


def attend_back(queries, keys, values, grads, starts, low, slopes, log_total, delta, rows):
    seq_len, width = queries.shape
    heads = width // HEAD_DIM
    whole = pl.BlockSpec((seq_len, width), lambda i: (0, 0))
    block = pl.BlockSpec((rows, width), lambda i: (i, 0))
    row = pl.BlockSpec((1, rows), lambda i: (0, i))
    stat = pl.BlockSpec((heads, rows), lambda i: (0, i))
    scalar = pl.BlockSpec(memory_space=pltpu.SMEM)
    return pl.pallas_call(
        functools.partial(attend_back_kernel, rows, heads),
        grid=(seq_len // rows,),
        in_specs=[scalar, scalar, row, stat, stat, block, block, whole, whole],
        out_specs=[block, whole, whole],
        out_shape=[jax.ShapeDtypeStruct((seq_len, width), BF16)] * 3,
        scratch_shapes=[pltpu.VMEM((seq_len, width), F32)] * 2,
        cost_estimate=pl.CostEstimate(flops=0, bytes_accessed=BUSY // 3, transcendentals=0),
        name="attend_back",
    )(low, slopes, starts, log_total, delta, queries, grads, keys, values)


def to_sequence(rows_in, count):
    halves = rows_in.reshape(count, 2, rows_in.shape[0] // (2 * count), -1)
    return jnp.concatenate([halves[:, 0], halves[::-1, 1]], axis=0).reshape(rows_in.shape)


def to_layout(rows_in, count):
    blocks = rows_in.reshape(2, count, rows_in.shape[0] // (2 * count), -1)
    return jnp.stack([blocks[0], blocks[1, ::-1]], axis=1).reshape(rows_in.shape)


def gather_beside(rows_in):
    return lax.all_gather(rows_in, "ctx", axis=0, tiled=True)


def sum_beside(partial):
    return lax.psum_scatter(partial.astype(BF16), "ctx", scatter_dimension=0, tiled=True).astype(F32)


def exchange(blocks):
    total, width = blocks.shape
    tiles = -(-width // 1024) * 8
    padded = jnp.pad(blocks, ((0, 0), (0, tiles * 128 - width))).reshape(total, tiles, 128)
    got = lax.all_to_all(padded, BOTH, split_axis=0, concat_axis=0)
    return got.reshape(total, tiles * 128)[:, :width]


MESH_ID = pl.DeviceIdType.MESH

def remote(source, target, send_sem, recv_sem, device):
    return pltpu.make_async_remote_copy(
        src_ref=source, dst_ref=target, send_sem=send_sem, recv_sem=recv_sem,
        device_id=device, device_id_type=MESH_ID,
    )


def place_of(line, side, core):
    return (line * 2 + side) * 2 + core


def own_place():
    me = lax.axis_index("ctx")
    return me, me // 4, (me // 2) % 2, me % 2


def greet(lines):
    me, line, side, core = own_place()
    barrier = pltpu.get_barrier_semaphore()

    def signal(target):
        pl.semaphore_signal(barrier, inc=1, device_id={"ctx": target}, device_id_type=MESH_ID)

    signal(place_of(line, side, 1 - core))
    signal(place_of(line, 1 - side, core))

    @pl.when(line > 0)
    def below():
        signal(me - 4)

    @pl.when(line < lines - 1)
    def above():
        signal(me + 4)

    pl.semaphore_wait(
        barrier, 2 + jnp.where(line > 0, 1, 0) + jnp.where(line < lines - 1, 1, 0)
    )


def gather_kernel(
    count, pieces, own_ref, out_ref, keep_sem, up_sem, down_sem, across_sem, chip_sem, recv_sem
):
    lines = count // 4
    me, line, side, core = own_place()
    partner = place_of(line, side, 1 - core)
    across = place_of(line, 1 - side, core)
    rows = own_ref.shape[0] // pieces

    def part(block, k):
        return out_ref.at[block, pl.ds(pl.multiple_of(k * rows, rows), rows), :]

    def mine(k):
        return own_ref.at[pl.ds(pl.multiple_of(k * rows, rows), rows), :]

    def to_up(source, block, slot, k):
        return remote(source, part(block, k), up_sem.at[slot, k], recv_sem.at[block, k], {"ctx": me + 4})

    def to_down(source, block, slot, k):
        return remote(source, part(block, k), down_sem.at[slot, k], recv_sem.at[block, k], {"ctx": me - 4})

    def to_across(source, block, k):
        return remote(
            source, part(block, k), across_sem.at[block // 4, k], recv_sem.at[block, k], {"ctx": across}
        )

    def to_partner(source, block, k):
        return remote(
            source, part(block, k), chip_sem.at[block // 2, k], recv_sem.at[block, k], {"ctx": partner}
        )

    def arrived(block, k):
        to_partner(part(block, k), block, k).wait_recv()

    def each_piece(body):
        def step(k, carried):
            body(k)
            return carried

        lax.fori_loop(0, pieces, step, 0)

    greet(lines)
    keep = pltpu.make_async_copy(own_ref, out_ref.at[me], keep_sem)
    keep.start()

    def first(k):
        @pl.when(line < lines - 1)
        def up():
            to_up(mine(k), me, 0, k).start()

        @pl.when(line > 0)
        def down():
            to_down(mine(k), me, 0, k).start()

        to_across(mine(k), me, k).start()
        to_partner(mine(k), me, k).start()

    each_piece(first)
    for hops in range(1, lines):
        def relay(k, hops=hops):
            @pl.when(line >= hops)
            def from_below():
                block = me - 4 * hops
                arrived(block, k)
                if hops < lines - 1:
                    @pl.when(line < lines - 1)
                    def up():
                        to_up(part(block, k), block, hops, k).start()

                to_across(part(block, k), block, k).start()
                to_partner(part(block, k), block, k).start()

            @pl.when(line < lines - hops)
            def from_above():
                block = me + 4 * hops
                arrived(block, k)
                if hops < lines - 1:
                    @pl.when(line > 0)
                    def down():
                        to_down(part(block, k), block, hops, k).start()

                to_across(part(block, k), block, k).start()
                to_partner(part(block, k), block, k).start()

        each_piece(relay)

    def hand_over(block):
        def one(k):
            arrived(block, k)
            to_partner(part(block, k), block, k).start()

        each_piece(one)

    hand_over(across)
    for hops in range(1, lines):
        @pl.when(line >= hops)
        def from_below(hops=hops):
            hand_over(across - 4 * hops)

        @pl.when(line < lines - hops)
        def from_above(hops=hops):
            hand_over(across + 4 * hops)

    def settle(index, carried):
        def one(k):
            arrived(index * 2 + 1 - core, k)
            to_partner(part(me, k), index * 2 + core, k).wait_send()

        each_piece(one)
        return carried

    lax.fori_loop(0, count // 2, settle, 0)

    def settle_across(index, carried):
        each_piece(lambda k: to_across(part(me, k), index * 4, k).wait_send())
        return carried

    lax.fori_loop(0, lines, settle_across, 0)
    for hops in range(lines - 1):
        @pl.when((line >= hops) & (line < lines - 1))
        def up(hops=hops):
            each_piece(lambda k: to_up(part(me, k), me, hops, k).wait_send())

        @pl.when((line < lines - hops) & (line > 0))
        def down(hops=hops):
            each_piece(lambda k: to_down(part(me, k), me, hops, k).wait_send())

    keep.wait()


def gather_rows(own, pieces=2):
    count = lax.axis_size("ctx")
    lines = count // 4
    rows, width = own.shape
    gathered = pl.pallas_call(
        functools.partial(gather_kernel, count, pieces),
        out_shape=jax.ShapeDtypeStruct((count, rows, width), own.dtype),
        in_specs=[pl.BlockSpec(memory_space=pltpu.VMEM)],
        out_specs=pl.BlockSpec(memory_space=pl.ANY),
        scratch_shapes=[
            pltpu.SemaphoreType.DMA,
            pltpu.SemaphoreType.DMA((lines, pieces)),
            pltpu.SemaphoreType.DMA((lines, pieces)),
            pltpu.SemaphoreType.DMA((lines, pieces)),
            pltpu.SemaphoreType.DMA((count // 2, pieces)),
            pltpu.SemaphoreType.DMA((count, pieces)),
        ],
        compiler_params=pltpu.CompilerParams(collective_id=0, has_side_effects=True),
        cost_estimate=pl.CostEstimate(flops=0, bytes_accessed=BUSY, transcendentals=0),
        name="gather_rows",
    )(own)
    return gathered.reshape(count * rows, width)


def begin_kernel(count, pieces, shared, *refs):
    inputs = len(shared) + 2
    own_ref, sources, down_ref = refs[0], refs[1 : inputs - 1], refs[inputs - 1]
    out_ref, targets, down_out = refs[inputs], refs[inputs + 1 : 2 * inputs - 1], refs[2 * inputs - 1]
    (
        keep_sem, up_sem, down_sem, across_sem, chip_sem, recv_sem,
        give_sem, take_sem, pass_sem, passed_sem, stay_sem, pair_sem,
    ) = refs[2 * inputs :]
    lines = count // 4
    me, line, side, core = own_place()
    half = lax.axis_index("fsdp")
    partner = place_of(line, side, 1 - core)
    across = place_of(line, 1 - side, core)
    rows = own_ref.shape[0] // pieces

    barrier = pltpu.get_barrier_semaphore()

    def enter(step, carried):
        pl.semaphore_signal(
            barrier, inc=1, device_id={"ctx": lax.rem(me + step, count)}, device_id_type=MESH_ID
        )
        return carried

    lax.fori_loop(1, count, enter, 0)
    pl.semaphore_signal(barrier, inc=1, device_id={"fsdp": 1 - half}, device_id_type=MESH_ID)
    pl.semaphore_wait(barrier, count)

    moves = []
    for source, target, (parts, kind) in zip(sources, targets, shared):
        wide = target.shape[2] // parts
        for part in range(parts):
            def block(goal, source=source, part=part, kind=kind, wide=wide, parts=parts):
                if kind == "same":
                    return source
                if kind == "blocks":
                    return source.at[goal]
                first = part * (source.shape[1] // parts) + goal * wide
                return source.at[:, pl.ds(pl.multiple_of(first, 128), wide)]

            def place(sender, side_of, target=target, part=part, wide=wide, parts=parts):
                at = target.at[sender * 2 + side_of]
                return at if parts == 1 else at.at[:, pl.ds(part * wide, wide)]

            moves.append((block, place))

    def origin(step):
        return lax.rem(me + count - step, count)

    def give(step, m):
        goal = lax.rem(me + step, count)
        block, place = moves[m]
        return remote(block(goal), place(me, half), give_sem.at[step, m], take_sem.at[step, m], {"ctx": goal})

    def taken(step, m):
        at = moves[m][1](origin(step), half)
        return remote(at, at, give_sem.at[step, m], take_sem.at[step, m], {"ctx": origin(step)})

    def hand(step, m, side_of):
        at = moves[m][1](origin(step), side_of)
        return remote(at, at, pass_sem.at[step, m], passed_sem.at[step, m], {"fsdp": 1 - half})

    def hand_own(m):
        block, place = moves[m]
        return remote(block(me), place(me, half), pass_sem.at[0, m], passed_sem.at[0, m], {"fsdp": 1 - half})

    def stay(m):
        block, place = moves[m]
        return pltpu.make_async_copy(block(me), place(me, half), stay_sem.at[m])

    def each_step(first, last, body):
        def step_body(step, carried):
            for m in range(len(moves)):
                body(step, m)
            return carried

        lax.fori_loop(first, last, step_body, 0)

    down_stay = pltpu.make_async_copy(down_ref, down_out.at[half], stay_sem.at[len(moves)])

    def down_pair(side_of):
        return remote(down_ref, down_out.at[side_of], pair_sem.at[0], pair_sem.at[1], {"fsdp": 1 - half})

    def part(block, k):
        return out_ref.at[block, pl.ds(pl.multiple_of(k * rows, rows), rows), :]

    def mine(k):
        return own_ref.at[pl.ds(pl.multiple_of(k * rows, rows), rows), :]

    def to_up(source, block, slot, k):
        return remote(source, part(block, k), up_sem.at[slot, k], recv_sem.at[block, k], {"ctx": me + 4})

    def to_down(source, block, slot, k):
        return remote(source, part(block, k), down_sem.at[slot, k], recv_sem.at[block, k], {"ctx": me - 4})

    def to_across(source, block, k):
        return remote(
            source, part(block, k), across_sem.at[block // 4, k], recv_sem.at[block, k], {"ctx": across}
        )

    def to_partner(source, block, k):
        return remote(
            source, part(block, k), chip_sem.at[block // 2, k], recv_sem.at[block, k], {"ctx": partner}
        )

    def arrived(block, k):
        to_partner(part(block, k), block, k).wait_recv()

    def each_piece(body):
        def step(k, carried):
            body(k)
            return carried

        lax.fori_loop(0, pieces, step, 0)

    keep = pltpu.make_async_copy(own_ref, out_ref.at[me], keep_sem)

    def first(k):
        @pl.when(line < lines - 1)
        def up():
            to_up(mine(k), me, 0, k).start()

        @pl.when(line > 0)
        def down():
            to_down(mine(k), me, 0, k).start()

        to_across(mine(k), me, k).start()
        to_partner(mine(k), me, k).start()

    each_piece(first)
    each_step(1, count, lambda step, m: give(step, m).start())
    down_pair(half).start()
    for m in range(len(moves)):
        hand_own(m).start()
    keep.start()
    down_stay.start()
    for m in range(len(moves)):
        stay(m).start()

    def pass_on(step, m):
        taken(step, m).wait_recv()
        hand(step, m, half).start()

    for hops in range(1, lines):
        def relay(k, hops=hops):
            @pl.when(line >= hops)
            def from_below():
                block = me - 4 * hops
                arrived(block, k)
                if hops < lines - 1:
                    @pl.when(line < lines - 1)
                    def up():
                        to_up(part(block, k), block, hops, k).start()

                to_across(part(block, k), block, k).start()
                to_partner(part(block, k), block, k).start()

            @pl.when(line < lines - hops)
            def from_above():
                block = me + 4 * hops
                arrived(block, k)
                if hops < lines - 1:
                    @pl.when(line > 0)
                    def down():
                        to_down(part(block, k), block, hops, k).start()

                to_across(part(block, k), block, k).start()
                to_partner(part(block, k), block, k).start()

        each_piece(relay)
        each_step(
            1 + (hops - 1) * (count - 1) // (lines - 1), 1 + hops * (count - 1) // (lines - 1), pass_on
        )

    def hand_over(block):
        def one(k):
            arrived(block, k)
            to_partner(part(block, k), block, k).start()

        each_piece(one)

    hand_over(across)
    for hops in range(1, lines):
        @pl.when(line >= hops)
        def from_below(hops=hops):
            hand_over(across - 4 * hops)

        @pl.when(line < lines - hops)
        def from_above(hops=hops):
            hand_over(across + 4 * hops)

    def settle(index, carried):
        def one(k):
            arrived(index * 2 + 1 - core, k)
            to_partner(part(me, k), index * 2 + core, k).wait_send()

        each_piece(one)
        return carried

    lax.fori_loop(0, count // 2, settle, 0)

    def settle_across(index, carried):
        each_piece(lambda k: to_across(part(me, k), index * 4, k).wait_send())
        return carried

    lax.fori_loop(0, lines, settle_across, 0)
    for hops in range(lines - 1):
        @pl.when((line >= hops) & (line < lines - 1))
        def up(hops=hops):
            each_piece(lambda k: to_up(part(me, k), me, hops, k).wait_send())

        @pl.when((line < lines - hops) & (line > 0))
        def down(hops=hops):
            each_piece(lambda k: to_down(part(me, k), me, hops, k).wait_send())

    each_step(0, count, lambda step, m: hand(step, m, 1 - half).wait_recv())
    each_step(1, count, lambda step, m: hand(step, m, half).wait_send())
    each_step(1, count, lambda step, m: give(step, m).wait_send())
    for m in range(len(moves)):
        hand_own(m).wait_send()
        stay(m).wait()
    down_pair(1 - half).wait_recv()
    down_pair(half).wait_send()
    down_stay.wait()
    keep.wait()


def begin(own, w_qkv, w_up, w_down, vectors, pieces=2):
    count = lax.axis_size("ctx")
    lines = count // 4
    rows, width = own.shape
    owned = w_qkv.shape[0]
    qkv_cols = w_qkv.shape[1] // count
    up_cols = w_up.shape[1] // count
    if qkv_cols % 384 == 0:
        shared = [(3, "columns")]
    else:
        w_qkv = w_qkv.reshape(owned, 3, count, -1).transpose(2, 0, 1, 3).reshape(count, owned, qkv_cols)
        shared = [(1, "blocks")]
    shared += [(1, "columns"), (1, "same")]
    moves = sum(parts for parts, _ in shared)
    in_vmem = pl.BlockSpec(memory_space=pltpu.VMEM)
    anywhere = pl.BlockSpec(memory_space=pl.ANY)
    rows_all, qkv, up, vectors_all, down = pl.pallas_call(
        functools.partial(begin_kernel, count, pieces, tuple(shared)),
        out_shape=[
            jax.ShapeDtypeStruct((count, rows, width), own.dtype),
            jax.ShapeDtypeStruct((count * 2, owned, qkv_cols), BF16),
            jax.ShapeDtypeStruct((count * 2, owned, up_cols), BF16),
            jax.ShapeDtypeStruct((count * 2, *vectors.shape), F32),
            jax.ShapeDtypeStruct((2, *w_down.shape), BF16),
        ],
        in_specs=[in_vmem] * 5,
        out_specs=[anywhere] * 5,
        scratch_shapes=[
            pltpu.SemaphoreType.DMA,
            pltpu.SemaphoreType.DMA((lines, pieces)),
            pltpu.SemaphoreType.DMA((lines, pieces)),
            pltpu.SemaphoreType.DMA((lines, pieces)),
            pltpu.SemaphoreType.DMA((count // 2, pieces)),
            pltpu.SemaphoreType.DMA((count, pieces)),
            pltpu.SemaphoreType.DMA((count, moves)),
            pltpu.SemaphoreType.DMA((count, moves)),
            pltpu.SemaphoreType.DMA((count, moves)),
            pltpu.SemaphoreType.DMA((count, moves)),
            pltpu.SemaphoreType.DMA((moves + 1,)),
            pltpu.SemaphoreType.DMA((2,)),
        ],
        compiler_params=pltpu.CompilerParams(collective_id=3, has_side_effects=True),
        cost_estimate=pl.CostEstimate(flops=0, bytes_accessed=BUSY, transcendentals=0),
        name="begin",
    )(own, w_qkv, w_up, vectors, w_down)
    return (
        rows_all.reshape(count * rows, width),
        qkv.reshape(-1, qkv_cols),
        up.reshape(-1, up_cols),
        down.reshape(-1, width),
        vectors_all.reshape(count * 2, -1),
    )


def project_kernel(rows_ref, gain_ref, shift_ref, weight_ref, bias_ref, normed_ref, out_ref):
    unit, _ = norm_parts(rows_ref[...].astype(F32))
    normed = (unit * gain_ref[...] + shift_ref[...]).astype(BF16)
    normed_ref[...] = normed
    projected = jnp.dot(normed, weight_ref[...], preferred_element_type=F32)
    out_ref[...] = (projected + bias_ref[...]).astype(BF16)


def project(rows_in, gain, shift, weight, bias, block=256):
    total, width = rows_in.shape
    columns = weight.shape[1]
    row = pl.BlockSpec((1, width), lambda i: (0, 0))
    return pl.pallas_call(
        project_kernel,
        grid=(total // block,),
        in_specs=[
            pl.BlockSpec((block, width), lambda i: (i, 0)),
            row,
            row,
            pl.BlockSpec((width, columns), lambda i: (0, 0)),
            pl.BlockSpec((1, columns), lambda i: (0, 0)),
        ],
        out_specs=[
            pl.BlockSpec((block, width), lambda i: (i, 0)),
            pl.BlockSpec((block, columns), lambda i: (i, 0)),
        ],
        out_shape=[
            jax.ShapeDtypeStruct((total, width), BF16),
            jax.ShapeDtypeStruct((total, columns), BF16),
        ],
        cost_estimate=pl.CostEstimate(
            flops=2 * total * width * columns, bytes_accessed=6 * total * width, transcendentals=0
        ),
        name="project",
    )(rows_in, gain[None], shift[None], weight, bias[None])


def feed_kernel(
    normed_ref, grad_ref, up_ref, down_ref, bias_ref,
    activated_ref, grad_hidden_ref, terms_ref, branch_ref, sums_ref,
):
    hidden = jnp.dot(normed_ref[...], up_ref[...], preferred_element_type=F32) + bias_ref[...]
    grad_activated = lax.dot_general(grad_ref[...], down_ref[...], NT, preferred_element_type=F32)
    normal = 0.5 * (1.0 + lax.erf(hidden * 0.5**0.5))
    density = jnp.exp(-0.5 * hidden * hidden) * (2.0 * math.pi) ** -0.5
    activated = (hidden * normal).astype(BF16)
    grad_hidden = (grad_activated * (normal + hidden * density)).astype(BF16)
    activated_ref[...] = activated
    grad_hidden_ref[...] = grad_hidden
    terms = lax.dot_general(grad_hidden, up_ref[...], NT, preferred_element_type=F32)
    terms_ref[...] = terms.astype(BF16)
    branch = jnp.dot(activated, down_ref[...], preferred_element_type=F32)
    branch_ref[...] = branch.astype(BF16)

    @pl.when(pl.program_id(0) == 0)
    def clear():
        sums_ref[...] = jnp.zeros_like(sums_ref)

    sums_ref[...] += jnp.sum(grad_hidden.astype(F32), axis=0, keepdims=True)


def feed(normed, grads, w_up, w_down, bias, block=256):
    total, width = normed.shape
    hidden = w_up.shape[1]
    wide = pl.BlockSpec((block, width), lambda i: (i, 0))
    narrow_rows = pl.BlockSpec((block, hidden), lambda i: (i, 0))
    return pl.pallas_call(
        feed_kernel,
        grid=(total // block,),
        in_specs=[
            wide,
            wide,
            pl.BlockSpec((width, hidden), lambda i: (0, 0)),
            pl.BlockSpec((hidden, width), lambda i: (0, 0)),
            pl.BlockSpec((1, hidden), lambda i: (0, 0)),
        ],
        out_specs=[narrow_rows, narrow_rows, wide, wide, pl.BlockSpec((1, hidden), lambda i: (0, 0))],
        out_shape=[
            jax.ShapeDtypeStruct((total, hidden), BF16),
            jax.ShapeDtypeStruct((total, hidden), BF16),
            jax.ShapeDtypeStruct((total, width), BF16),
            jax.ShapeDtypeStruct((total, width), BF16),
            jax.ShapeDtypeStruct((1, hidden), F32),
        ],
        cost_estimate=pl.CostEstimate(flops=0, bytes_accessed=BUSY // 3, transcendentals=0),
        name="feed",
    )(normed, grads, w_up, w_down, bias[None])


def sum_kernel(
    count, pieces, part_ref, grad_ref, pair_ref, out_ref, got_ref, pair_out,
    held, chip_in, across_in, line_in, grad_in, grad_sum, load_sem,
    chip_send, chip_recv, across_send, across_recv, line_send, line_recv,
    pass_sem, passed_sem, give_sem, take_sem, pair_sem,
):
    lines = count // 4
    me, line, side, core = own_place()
    partner = place_of(line, side, 1 - core)
    across = place_of(line, 1 - side, core)
    rows = out_ref.shape[0] // pieces

    def at(ref, block, k):
        return ref.at[block, pl.ds(pl.multiple_of(k * rows, rows), rows), :]

    def to_partner(pair, k):
        return remote(
            at(part_ref, pair * 2 + 1 - core, k), at(chip_in, pair, k),
            chip_send.at[pair, k], chip_recv.at[pair, k], {"ctx": partner},
        )

    def to_across(goal, k):
        return remote(
            at(held, goal * 2 + 1 - side, k), at(across_in, goal, k),
            across_send.at[goal, k], across_recv.at[goal, k], {"ctx": across},
        )

    def to_next(goal, target, slot, k):
        return remote(
            at(held, goal * 2 + side, k), at(line_in, slot, k),
            line_send.at[goal, k], line_recv.at[slot, k], {"ctx": target},
        )

    def each_piece(body):
        def step(k, carried):
            body(k)
            return carried

        lax.fori_loop(0, pieces, step, 0)

    def far_first(visit, between=None):
        for hops in range(lines - 1, 0, -1):
            @pl.when(line + hops < lines)
            def ahead(hops=hops):
                visit(line + hops, 1)

            @pl.when(line >= hops)
            def behind(hops=hops):
                visit(line - hops, -1)

            if between is not None:
                between(lines - hops)

    half = lax.axis_index("fsdp")
    barrier = pltpu.get_barrier_semaphore()

    def enter(step, carried):
        pl.semaphore_signal(
            barrier, inc=1, device_id={"ctx": lax.rem(me + step, count)}, device_id_type=MESH_ID
        )
        return carried

    def hand(step):
        goal = lax.rem(me + step, count)
        return remote(
            grad_ref.at[goal, 1 - half], grad_in.at[goal], pass_sem.at[step], passed_sem.at[step],
            {"fsdp": 1 - half},
        )

    def give_grad(step):
        goal = lax.rem(me + step, count)
        return remote(
            grad_sum.at[goal], got_ref.at[me], give_sem.at[step], take_sem.at[step], {"ctx": goal}
        )

    def take_grad(step):
        source = lax.rem(me + count - step, count)
        return remote(
            grad_sum.at[source], got_ref.at[source], give_sem.at[step], take_sem.at[step], {"ctx": source}
        )

    def each_step(first, last, body):
        def step_body(step, carried):
            body(step)
            return carried

        lax.fori_loop(first, last, step_body, 0)

    def pass_on(step):
        goal = lax.rem(me + step, count)
        hand(step).wait_recv()
        grad_sum[goal] = (grad_ref[goal, half].astype(F32) + grad_in[goal].astype(F32)).astype(BF16)
        give_grad(step).start()

    def pair_copy():
        return remote(pair_ref.at[1 - half], pair_out, pair_sem.at[0], pair_sem.at[1], {"fsdp": 1 - half})

    loads = [
        pltpu.make_async_copy(part_ref.at[pair * 2 + core], held.at[pair], load_sem.at[pair])
        for pair in range(count // 2)
    ]
    for load in loads:
        load.start()
    lax.fori_loop(1, count, enter, 0)
    pl.semaphore_signal(barrier, inc=1, device_id={"fsdp": 1 - half}, device_id_type=MESH_ID)
    pl.semaphore_wait(barrier, count)

    def give(goal, way):
        each_piece(lambda k: to_partner(goal * 2 + 1 - side, k).start())

    def give_same(goal, way):
        each_piece(lambda k: to_partner(goal * 2 + side, k).start())

    each_step(1, count, lambda step: hand(step).start())
    hand(0).start()
    pair_copy().start()
    far_first(give)
    give(line, 0)
    far_first(give_same)
    give_same(line, 0)
    for load in loads:
        load.wait()

    def read(ref, block, k):
        return ref[block, pl.ds(pl.multiple_of(k * rows, rows), rows), :].astype(F32)

    def write(block, k, value):
        held[block, pl.ds(pl.multiple_of(k * rows, rows), rows), :] = value.astype(held.dtype)

    def cross(goal, way):
        pair = goal * 2 + 1 - side

        def one(k):
            to_partner(pair, k).wait_recv()
            write(pair, k, read(held, pair, k) + read(chip_in, pair, k))
            to_across(goal, k).start()

        each_piece(one)

    far_first(cross)
    cross(line, 0)

    def two_sums(goal, k):
        pair = goal * 2 + side
        to_partner(pair, k).wait_recv()
        to_across(goal, k).wait_recv()
        return read(held, pair, k) + read(chip_in, pair, k) + read(across_in, goal, k)

    def along(goal, way):
        pair = goal * 2 + side
        target = me + 4 * way
        arriving = goal
        if way == 1:
            slot = goal
            fed = line > 0
        else:
            fed = line < lines - 1
            slot = jnp.where(goal == line - 1, lines, goal)

        def one(k):
            total = two_sums(goal, k)
            write(pair, k, total)

            @pl.when(fed)
            def add():
                to_next(goal, target, arriving, k).wait_recv()
                write(pair, k, total + read(line_in, arriving, k))

            to_next(goal, target, slot, k).start()

        each_piece(one)

    def share_of_steps(turn):
        each_step(
            1 + (turn - 1) * (count - 1) // (lines - 1), 1 + turn * (count - 1) // (lines - 1), pass_on
        )

    far_first(along, share_of_steps)
    hand(0).wait_recv()
    grad_sum[me] = (grad_ref[me, half].astype(F32) + grad_in[me].astype(F32)).astype(BF16)
    stay = pltpu.make_async_copy(grad_sum.at[me], got_ref.at[me], pair_sem.at[2])
    stay.start()

    def last(k):
        span = pl.ds(pl.multiple_of(k * rows, rows), rows)
        out_ref[span, :] = two_sums(line, k)

        @pl.when(line > 0)
        def from_below():
            to_next(line, me, line, k).wait_recv()
            out_ref[span, :] += read(line_in, line, k)

        @pl.when(line < lines - 1)
        def from_above():
            to_next(line, me, lines, k).wait_recv()
            out_ref[span, :] += read(line_in, lines, k)

    each_piece(last)

    def settle(index, carried):
        each_piece(lambda k: to_partner(index, k).wait_send())
        return carried

    lax.fori_loop(0, count // 2, settle, 0)

    def settle_line(goal, carried):
        each_piece(lambda k: to_across(goal, k).wait_send())

        @pl.when(goal != line)
        def sent():
            each_piece(lambda k: to_next(goal, me, goal, k).wait_send())

        return carried

    lax.fori_loop(0, lines, settle_line, 0)
    each_step(1, count, lambda step: take_grad(step).wait_recv())
    each_step(1, count, lambda step: give_grad(step).wait_send())
    each_step(0, count, lambda step: hand(step).wait_send())
    pair_copy().wait_recv()
    pair_copy().wait_send()
    stay.wait()


def sum_rows(partial, grad, pair_grad, collective_id, pieces=2):
    count = lax.axis_size("ctx")
    lines = count // 4
    width = partial.shape[1]
    rows = partial.shape[0] // count
    owned, columns = grad.shape[0] // (2 * count), grad.shape[1]
    anywhere = pl.BlockSpec(memory_space=pl.ANY)
    pair_shape = (pair_grad.shape[0] // 2, pair_grad.shape[1])
    return pl.pallas_call(
        functools.partial(sum_kernel, count, pieces),
        out_shape=[
            jax.ShapeDtypeStruct((rows, width), F32),
            jax.ShapeDtypeStruct((count, owned, columns), BF16),
            jax.ShapeDtypeStruct(pair_shape, BF16),
        ],
        in_specs=[anywhere, pl.BlockSpec(memory_space=pltpu.VMEM), anywhere],
        out_specs=[pl.BlockSpec(memory_space=pltpu.VMEM), anywhere, anywhere],
        scratch_shapes=[
            pltpu.VMEM((count // 2, rows, width), BF16),
            pltpu.VMEM((count // 2, rows, width), BF16),
            pltpu.VMEM((lines, rows, width), BF16),
            pltpu.VMEM((lines + 1, rows, width), BF16),
            pltpu.VMEM((count, owned, columns), BF16),
            pltpu.VMEM((count, owned, columns), BF16),
            pltpu.SemaphoreType.DMA((count // 2,)),
            pltpu.SemaphoreType.DMA((count // 2, pieces)),
            pltpu.SemaphoreType.DMA((count // 2, pieces)),
            pltpu.SemaphoreType.DMA((lines, pieces)),
            pltpu.SemaphoreType.DMA((lines, pieces)),
            pltpu.SemaphoreType.DMA((lines, pieces)),
            pltpu.SemaphoreType.DMA((lines + 1, pieces)),
            pltpu.SemaphoreType.DMA((count,)),
            pltpu.SemaphoreType.DMA((count,)),
            pltpu.SemaphoreType.DMA((count,)),
            pltpu.SemaphoreType.DMA((count,)),
            pltpu.SemaphoreType.DMA((3,)),
        ],
        compiler_params=pltpu.CompilerParams(
            collective_id=collective_id, has_side_effects=True, vmem_limit_bytes=63 * 2**20
        ),
        cost_estimate=pl.CostEstimate(flops=0, bytes_accessed=BUSY, transcendentals=0),
        name="sum_rows",
    )(
        partial.astype(BF16).reshape(count, rows, width),
        grad.reshape(count, 2, owned, columns),
        pair_grad.reshape(2, *pair_shape),
    )


def own_half(pair_grad, other):
    half = pair_grad.shape[0] // 2
    kept = lax.dynamic_slice_in_dim(pair_grad, lax.axis_index("fsdp") * half, half, 0)
    return kept.astype(F32) + other.astype(F32)


def in_order(got, parts):
    count, owned, _ = got.shape
    return got.reshape(count, owned, parts, -1).transpose(1, 2, 0, 3).reshape(owned, -1).astype(F32)


def weight_grad(rows_in, grads):
    terms = lax.dot_general(rows_in, grads, TN, preferred_element_type=F32).astype(BF16)
    return lax.optimization_barrier(terms)


def columns_to_rows(slice_in):
    count = lax.axis_size("ctx")
    rows = slice_in.shape[0] // count
    mine = lax.all_to_all(slice_in.reshape(count, rows, -1), "ctx", split_axis=0, concat_axis=0)
    return mine.transpose(1, 0, 2).reshape(rows, -1)


def widen(columns, share):
    if share == 1:
        return columns
    count = lax.axis_size("ctx")
    groups = [list(range(first, first + share)) for first in range(0, count, share)]
    return lax.all_gather(
        columns, "ctx", axis=columns.ndim - 1, tiled=True, axis_index_groups=groups
    )


def narrow(columns, share):
    if share == 1:
        return columns
    width = columns.shape[-1] // share
    place = lax.rem(lax.axis_index("ctx"), share)
    return lax.dynamic_slice_in_dim(columns, place * width, width, columns.ndim - 1)


def on_device(
    tokens, doc_lengths, ln1_gain, ln1_bias, w_qkv, bias_q, bias_v, w_out, b_out,
    ln2_gain, ln2_bias, w_up, b_up, w_down, b_down, cotangent,
):
    count = lax.axis_size("ctx")
    rank = lax.axis_index("ctx")
    pair_rank = lax.axis_index("fsdp")
    tok_rows, width = tokens.shape[1:]
    seq_len = tok_rows * count
    own_cols = width // count
    share = max(1, HEAD_DIM // own_cols)
    head_count = width // HEAD_DIM
    heads = own_cols * share // HEAD_DIM
    rows = min(256, seq_len)

    lengths = doc_lengths[0]
    doc_starts = jnp.cumsum(lengths) - lengths
    positions = jnp.arange(seq_len, dtype=jnp.int32)
    starts = jnp.max(
        jnp.where(doc_starts[None, :] <= positions[:, None], doc_starts[None, :], 0), axis=1
    ).astype(jnp.int32)
    low = starts[::rows] // rows
    starts = starts[None, :]
    first_head = (rank // share) * heads
    head_ids = (first_head + jnp.arange(heads)).astype(F32)
    slopes = 2.0 ** (-8.0 * (head_ids + 1.0) / head_count)

    vectors = [ln1_gain, ln1_bias, b_out, ln2_gain, ln2_bias, b_down, bias_q, bias_v, b_up]
    devices = count * lax.axis_size("fsdp")
    own_vectors = jnp.concatenate([vector.astype(F32) for vector in vectors])
    tiles = -(-own_vectors.shape[0] // 1024) * 8
    own_vectors = jnp.pad(own_vectors, (0, tiles * 128 - own_vectors.shape[0])).reshape(tiles, 128)
    tokens_all, w_qkv_own, w_up_own, w_down_own, everywhere = begin(
        tokens[0], w_qkv, w_up, w_down, own_vectors
    )
    at = 0
    whole_vectors = []
    for vector in vectors:
        whole_vectors.append(everywhere[:, at : at + vector.shape[0]].reshape(-1))
        at += vector.shape[0]
    gain_one, shift_one, b_out_all, gain_two, shift_two, b_down_all = whole_vectors[:6]
    head_at = first_head * HEAD_DIM
    bias_q_own, bias_v_own = (
        lax.dynamic_slice_in_dim(vector, head_at, heads * HEAD_DIM) for vector in whole_vectors[6:8]
    )
    ff_cols = whole_vectors[8].shape[0] // count
    b_up_own = lax.dynamic_slice_in_dim(whole_vectors[8], rank * ff_cols, ff_cols)

    w_qkv_head = widen(w_qkv_own.reshape(width, 3, -1), share).reshape(width, -1)
    w_out_all = lax.all_gather(w_out, BOTH, axis=0, tiled=True)

    inputs = tokens[0].astype(F32)
    unit_one, rate_one = norm_parts(inputs)
    grad_out = cotangent[0]
    tokens_all, cotangent_rows = lax.optimization_barrier((tokens_all, grad_out))
    grad_out_all = gather_beside(cotangent_rows)

    head_width = heads * HEAD_DIM
    shift = jnp.concatenate([bias_q_own, jnp.zeros(head_width, F32), bias_v_own])
    normed_all, projected = project(tokens_all, gain_one, shift_one, w_qkv_head, shift)
    projected = to_sequence(projected, count)
    queries, keys, values = (
        projected[:, part * head_width : (part + 1) * head_width] for part in range(3)
    )
    attended_full, log_total = attend(queries, keys, values, starts, low, slopes, rows)
    attended_own = narrow(to_layout(attended_full.astype(BF16), count), share)
    attended = columns_to_rows(attended_own)
    middle = inputs + jnp.dot(attended, w_out_all, preferred_element_type=F32) + b_out_all

    unit_two, rate_two = norm_parts(middle)
    normed_two = (unit_two * gain_two + shift_two).astype(BF16)
    normed_two_all = gather_rows(normed_two)
    activated, grad_hidden, terms, branch_terms, grad_hidden_sums = feed(
        normed_two_all, grad_out_all, w_up_own, w_down_own, b_up_own
    )
    w_down_terms = weight_grad(activated, grad_out_all)
    grad_normed_two, w_up_got, w_down_other = sum_rows(
        terms,
        weight_grad(normed_two_all, grad_hidden),
        w_down_terms,
        1,
    )
    grad_w_up = in_order(w_up_got, 1)
    grad_w_down = own_half(w_down_terms, w_down_other)

    grad_middle = grad_out.astype(F32) + norm_back(unit_two, rate_two, gain_two, grad_normed_two)
    grad_branch = grad_middle.astype(BF16)
    grad_branch, branch_terms = lax.optimization_barrier((grad_branch, branch_terms))
    branch = sum_beside(branch_terms)
    grad_branch_all = gather_rows(grad_branch)
    w_out_head = lax.dynamic_slice_in_dim(w_out_all, head_at, head_width, 0)
    grad_heads = lax.dot_general(
        grad_branch_all, w_out_head, NT, preferred_element_type=F32
    ).astype(BF16)
    grad_heads = to_sequence(grad_heads, count)

    delta = (grad_heads.astype(F32) * attended_full).reshape(seq_len, heads, HEAD_DIM)
    delta = jnp.sum(delta, axis=-1).T
    grad_parts = attend_back(
        queries, keys, values, grad_heads, starts, low, slopes, log_total, delta, rows
    )
    grad_qkv = jnp.concatenate(
        [narrow(to_layout(part, count), share) for part in grad_parts], axis=1
    )
    column_sums = jnp.sum(grad_qkv.astype(F32), axis=0)
    w_out_terms = weight_grad(attended_own, grad_branch_all)
    grad_normed, w_qkv_got, w_out_other = sum_rows(
        lax.dot_general(grad_qkv, w_qkv_own, NT, preferred_element_type=F32),
        weight_grad(normed_all, grad_qkv),
        w_out_terms,
        2,
    )
    grad_w_qkv = in_order(w_qkv_got, 3)
    grad_w_out = own_half(w_out_terms, w_out_other)
    branch, middle, grad_normed = lax.optimization_barrier((branch, middle, grad_normed))
    outputs = (middle + branch + b_down_all).astype(BF16)
    grad_inputs = grad_middle + norm_back(unit_one, rate_one, gain_one, grad_normed)

    pair = devices // count
    full_sums = jnp.stack(
        [
            jnp.sum(grad_normed * unit_one, axis=0),
            jnp.sum(grad_normed, axis=0),
            jnp.sum(grad_normed_two * unit_two, axis=0),
            jnp.sum(grad_normed_two, axis=0),
            jnp.sum(grad_branch.astype(F32), axis=0),
            jnp.sum(grad_out.astype(F32), axis=0),
        ]
    )
    full_sums = full_sums.reshape(6, devices, -1).transpose(1, 0, 2).reshape(devices, -1)
    own_sums = jnp.concatenate(
        [
            column_sums[:own_cols].reshape(pair, -1),
            column_sums[2 * own_cols :].reshape(pair, -1),
            grad_hidden_sums.reshape(pair, -1),
        ],
        axis=1,
    )
    here = (jnp.arange(count) == rank)[:, None, None]
    own_sums = jnp.where(here, own_sums[None], 0.0).reshape(devices, -1)
    sums = jnp.sum(exchange(jnp.concatenate([full_sums, own_sums], axis=1)), axis=0)
    share_of = width // devices
    (
        grad_ln1_gain, grad_ln1_bias, grad_ln2_gain, grad_ln2_bias, grad_b_out, grad_b_down,
        grad_bias_q, grad_bias_v,
    ) = sums[: 8 * share_of].reshape(8, share_of)
    grad_b_up = sums[8 * share_of :]
    return (
        outputs[None],
        grad_inputs[None],
        grad_ln1_gain,
        grad_ln1_bias,
        grad_w_qkv,
        grad_bias_q,
        grad_bias_v,
        grad_w_out,
        grad_b_out,
        grad_ln2_gain,
        grad_ln2_bias,
        grad_w_up,
        grad_b_up,
        grad_w_down,
        grad_b_down,
    )


def solution(mesh):
    spread = P(BOTH)
    matrix = P(BOTH, None)
    rows = P("fsdp", "ctx", None)
    placed = (
        rows, P("fsdp", None), spread, spread, matrix, spread, spread, matrix, spread,
        spread, spread, matrix, spread, matrix, spread, rows,
    )
    results = (
        rows, rows, spread, spread, matrix, spread, spread, matrix, spread,
        spread, spread, matrix, spread, matrix, spread,
    )
    return jax.shard_map(
        on_device, mesh=mesh, in_specs=placed, out_specs=results, check_vma=False
    )
```

```python
import functools
import math

import jax
import jax.numpy as jnp
from jax import lax
from jax.experimental import pallas as pl
from jax.experimental.pallas import tpu as pltpu
from jax.sharding import PartitionSpec as P

HEAD_DIM = 64
EPSILON = 1e-05
MASKED = -1e30
BOTH = ("ctx", "fsdp")
NT = (((1,), (1,)), ((), ()))
TN = (((0,), (0,)), ((), ()))
F32 = jnp.float32
BF16 = jnp.bfloat16
BUSY = 160 * 2**20


def norm_parts(values):
    centred = values - jnp.mean(values, axis=-1, keepdims=True)
    rate = lax.rsqrt(jnp.mean(centred * centred, axis=-1, keepdims=True) + EPSILON)
    return centred * rate, rate


def norm_back(unit, rate, gain, grad):
    scaled = grad * gain
    return rate * (
        scaled
        - jnp.mean(scaled, axis=-1, keepdims=True)
        - unit * jnp.mean(scaled * unit, axis=-1, keepdims=True)
    )


def block_parts(key_block, query_block, rows):
    key_at = key_block * rows + lax.broadcasted_iota(jnp.int32, (rows, rows), 0)
    query_at = query_block * rows + lax.broadcasted_iota(jnp.int32, (rows, rows), 1)
    return key_at, query_at


def head_mask(values, head):
    lanes = lax.broadcasted_iota(jnp.int32, values.shape, 1)
    return jnp.where(lanes // HEAD_DIM == head, values, jnp.zeros_like(values))


def scores_block(keys, query_head, slope, distance, allowed):
    raw = lax.dot_general(keys, query_head, NT, preferred_element_type=F32)
    return jnp.where(allowed, raw * HEAD_DIM ** (-0.5) - slope * distance, MASKED)


def attend_kernel(rows, heads, low_ref, slope_ref, start_ref, q_ref, k_ref, v_ref, out_ref, total_ref):
    block = pl.program_id(0)
    low = low_ref[block]
    starts = start_ref[...]
    queries = q_ref[...]
    query_heads = [head_mask(queries, head) for head in range(heads)]

    def parts(key_block):
        key_at, query_at = block_parts(key_block, block, rows)
        allowed = (key_at <= query_at) & (key_at >= starts)
        at = pl.ds(pl.multiple_of(key_block * rows, rows), rows)
        return (query_at - key_at).astype(F32), allowed, at

    def step(key_block, carried):
        distance, allowed, at = parts(key_block)
        keys = k_ref[at, :]
        values = v_ref[at, :]
        following = []
        for head in range(heads):
            top, total, accum = carried[head]
            scores = scores_block(keys, query_heads[head], slope_ref[head], distance, allowed)
            new_top = jnp.maximum(top, jnp.max(scores, axis=0, keepdims=True))
            shrink = jnp.exp(top - new_top)
            weights = jnp.exp(scores - new_top)
            total = total * shrink + jnp.sum(weights, axis=0, keepdims=True)
            accum = accum * shrink + lax.dot_general(
                values, weights.astype(BF16), TN, preferred_element_type=F32
            )
            following.append((new_top, total, accum))
        return following

    width = out_ref.shape[1]
    begin = (jnp.full((1, rows), MASKED, F32), jnp.zeros((1, rows), F32), jnp.zeros((width, rows), F32))
    done = lax.fori_loop(low, block + 1, step, [begin] * heads)
    for head in range(heads):
        top, total, accum = done[head]
        total_ref[head : head + 1, :] = top + jnp.log(total)
        span = slice(head * HEAD_DIM, (head + 1) * HEAD_DIM)
        out_ref[:, span] = jnp.transpose(accum[span, :] / total)


def attend_back_kernel(
    rows, heads, low_ref, slope_ref, start_ref, total_ref, delta_ref, q_ref, g_ref, k_ref, v_ref,
    dq_ref, dk_ref, dv_ref, dk_sum, dv_sum,
):
    block = pl.program_id(0)
    low = low_ref[block]
    starts = start_ref[...]
    query_heads = [head_mask(q_ref[...], head) for head in range(heads)]
    grad_heads = [head_mask(g_ref[...], head) for head in range(heads)]
    log_totals = [total_ref[head : head + 1, :] for head in range(heads)]
    deltas = [delta_ref[head : head + 1, :] for head in range(heads)]

    @pl.when(block == 0)
    def clear():
        dk_sum[...] = jnp.zeros_like(dk_sum)
        dv_sum[...] = jnp.zeros_like(dv_sum)

    def step(key_block, accum):
        key_at, query_at = block_parts(key_block, block, rows)
        allowed = (key_at <= query_at) & (key_at >= starts)
        distance = (query_at - key_at).astype(F32)
        at = pl.ds(pl.multiple_of(key_block * rows, rows), rows)
        keys = k_ref[at, :]
        values = v_ref[at, :]
        dk_part = jnp.zeros(keys.shape, F32)
        dv_part = jnp.zeros(keys.shape, F32)
        for head in range(heads):
            scores = scores_block(keys, query_heads[head], slope_ref[head], distance, allowed)
            probs = jnp.exp(scores - log_totals[head])
            grad_probs = lax.dot_general(values, grad_heads[head], NT, preferred_element_type=F32)
            grad_scores = (probs * (grad_probs - deltas[head])).astype(BF16)
            dv_part = dv_part + jnp.dot(
                probs.astype(BF16), grad_heads[head], preferred_element_type=F32
            )
            dk_part = dk_part + jnp.dot(grad_scores, query_heads[head], preferred_element_type=F32)
            accum = accum + lax.dot_general(
                grad_scores, head_mask(keys, head), TN, preferred_element_type=F32
            )
        dk_sum[at, :] += dk_part
        dv_sum[at, :] += dv_part
        return accum

    grad = lax.fori_loop(low, block + 1, step, jnp.zeros(dq_ref.shape, F32))
    dq_ref[...] = (grad * HEAD_DIM ** (-0.5)).astype(BF16)

    @pl.when(block == pl.num_programs(0) - 1)
    def store():
        dk_ref[...] = (dk_sum[...] * HEAD_DIM ** (-0.5)).astype(BF16)
        dv_ref[...] = dv_sum[...].astype(BF16)


def attend(queries, keys, values, starts, low, slopes, rows):
    seq_len, width = queries.shape
    heads = width // HEAD_DIM
    whole = pl.BlockSpec((seq_len, width), lambda i: (0, 0))
    block = pl.BlockSpec((rows, width), lambda i: (i, 0))
    row = pl.BlockSpec((1, rows), lambda i: (0, i))
    stat = pl.BlockSpec((heads, rows), lambda i: (0, i))
    scalar = pl.BlockSpec(memory_space=pltpu.SMEM)
    return pl.pallas_call(
        functools.partial(attend_kernel, rows, heads),
        grid=(seq_len // rows,),
        in_specs=[scalar, scalar, row, block, whole, whole],
        out_specs=[block, stat],
        out_shape=[
            jax.ShapeDtypeStruct((seq_len, width), F32),
            jax.ShapeDtypeStruct((heads, seq_len), F32),
        ],
        cost_estimate=pl.CostEstimate(flops=0, bytes_accessed=BUSY // 3, transcendentals=0),
        name="attend",
    )(low, slopes, starts, queries, keys, values)


def attend_back(queries, keys, values, grads, starts, low, slopes, log_total, delta, rows):
    seq_len, width = queries.shape
    heads = width // HEAD_DIM
    whole = pl.BlockSpec((seq_len, width), lambda i: (0, 0))
    block = pl.BlockSpec((rows, width), lambda i: (i, 0))
    row = pl.BlockSpec((1, rows), lambda i: (0, i))
    stat = pl.BlockSpec((heads, rows), lambda i: (0, i))
    scalar = pl.BlockSpec(memory_space=pltpu.SMEM)
    return pl.pallas_call(
        functools.partial(attend_back_kernel, rows, heads),
        grid=(seq_len // rows,),
        in_specs=[scalar, scalar, row, stat, stat, block, block, whole, whole],
        out_specs=[block, whole, whole],
        out_shape=[jax.ShapeDtypeStruct((seq_len, width), BF16)] * 3,
        scratch_shapes=[pltpu.VMEM((seq_len, width), F32)] * 2,
        cost_estimate=pl.CostEstimate(flops=0, bytes_accessed=BUSY // 3, transcendentals=0),
        name="attend_back",
    )(low, slopes, starts, log_total, delta, queries, grads, keys, values)


def to_sequence(rows_in, count):
    halves = rows_in.reshape(count, 2, rows_in.shape[0] // (2 * count), -1)
    return jnp.concatenate([halves[:, 0], halves[::-1, 1]], axis=0).reshape(rows_in.shape)


def to_layout(rows_in, count):
    blocks = rows_in.reshape(2, count, rows_in.shape[0] // (2 * count), -1)
    return jnp.stack([blocks[0], blocks[1, ::-1]], axis=1).reshape(rows_in.shape)


def gather_beside(rows_in):
    return lax.all_gather(rows_in, "ctx", axis=0, tiled=True)


def sum_beside(partial):
    return lax.psum_scatter(partial.astype(BF16), "ctx", scatter_dimension=0, tiled=True).astype(F32)


def exchange(blocks):
    total, width = blocks.shape
    tiles = -(-width // 1024) * 8
    padded = jnp.pad(blocks, ((0, 0), (0, tiles * 128 - width))).reshape(total, tiles, 128)
    got = lax.all_to_all(padded, BOTH, split_axis=0, concat_axis=0)
    return got.reshape(total, tiles * 128)[:, :width]


MESH_ID = pl.DeviceIdType.MESH

def remote(source, target, send_sem, recv_sem, device):
    return pltpu.make_async_remote_copy(
        src_ref=source, dst_ref=target, send_sem=send_sem, recv_sem=recv_sem,
        device_id=device, device_id_type=MESH_ID,
    )


def place_of(line, side, core):
    return (line * 2 + side) * 2 + core


def own_place():
    me = lax.axis_index("ctx")
    return me, me // 4, (me // 2) % 2, me % 2


def greet(lines):
    me, line, side, core = own_place()
    barrier = pltpu.get_barrier_semaphore()

    def signal(target):
        pl.semaphore_signal(barrier, inc=1, device_id={"ctx": target}, device_id_type=MESH_ID)

    signal(place_of(line, side, 1 - core))
    signal(place_of(line, 1 - side, core))

    @pl.when(line > 0)
    def below():
        signal(me - 4)

    @pl.when(line < lines - 1)
    def above():
        signal(me + 4)

    pl.semaphore_wait(
        barrier, 2 + jnp.where(line > 0, 1, 0) + jnp.where(line < lines - 1, 1, 0)
    )


def gather_kernel(
    count, pieces, own_ref, out_ref, keep_sem, up_sem, down_sem, across_sem, chip_sem, recv_sem
):
    lines = count // 4
    me, line, side, core = own_place()
    partner = place_of(line, side, 1 - core)
    across = place_of(line, 1 - side, core)
    rows = own_ref.shape[0] // pieces

    def part(block, k):
        return out_ref.at[block, pl.ds(pl.multiple_of(k * rows, rows), rows), :]

    def mine(k):
        return own_ref.at[pl.ds(pl.multiple_of(k * rows, rows), rows), :]

    def to_up(source, block, slot, k):
        return remote(source, part(block, k), up_sem.at[slot, k], recv_sem.at[block, k], {"ctx": me + 4})

    def to_down(source, block, slot, k):
        return remote(source, part(block, k), down_sem.at[slot, k], recv_sem.at[block, k], {"ctx": me - 4})

    def to_across(source, block, k):
        return remote(
            source, part(block, k), across_sem.at[block // 4, k], recv_sem.at[block, k], {"ctx": across}
        )

    def to_partner(source, block, k):
        return remote(
            source, part(block, k), chip_sem.at[block // 2, k], recv_sem.at[block, k], {"ctx": partner}
        )

    def arrived(block, k):
        to_partner(part(block, k), block, k).wait_recv()

    def each_piece(body):
        def step(k, carried):
            body(k)
            return carried

        lax.fori_loop(0, pieces, step, 0)

    greet(lines)
    keep = pltpu.make_async_copy(own_ref, out_ref.at[me], keep_sem)
    keep.start()

    def first(k):
        @pl.when(line < lines - 1)
        def up():
            to_up(mine(k), me, 0, k).start()

        @pl.when(line > 0)
        def down():
            to_down(mine(k), me, 0, k).start()

        to_across(mine(k), me, k).start()
        to_partner(mine(k), me, k).start()

    each_piece(first)
    for hops in range(1, lines):
        def relay(k, hops=hops):
            @pl.when(line >= hops)
            def from_below():
                block = me - 4 * hops
                arrived(block, k)
                if hops < lines - 1:
                    @pl.when(line < lines - 1)
                    def up():
                        to_up(part(block, k), block, hops, k).start()

                to_across(part(block, k), block, k).start()
                to_partner(part(block, k), block, k).start()

            @pl.when(line < lines - hops)
            def from_above():
                block = me + 4 * hops
                arrived(block, k)
                if hops < lines - 1:
                    @pl.when(line > 0)
                    def down():
                        to_down(part(block, k), block, hops, k).start()

                to_across(part(block, k), block, k).start()
                to_partner(part(block, k), block, k).start()

        each_piece(relay)

    def hand_over(block):
        def one(k):
            arrived(block, k)
            to_partner(part(block, k), block, k).start()

        each_piece(one)

    hand_over(across)
    for hops in range(1, lines):
        @pl.when(line >= hops)
        def from_below(hops=hops):
            hand_over(across - 4 * hops)

        @pl.when(line < lines - hops)
        def from_above(hops=hops):
            hand_over(across + 4 * hops)

    def settle(index, carried):
        def one(k):
            arrived(index * 2 + 1 - core, k)
            to_partner(part(me, k), index * 2 + core, k).wait_send()

        each_piece(one)
        return carried

    lax.fori_loop(0, count // 2, settle, 0)

    def settle_across(index, carried):
        each_piece(lambda k: to_across(part(me, k), index * 4, k).wait_send())
        return carried

    lax.fori_loop(0, lines, settle_across, 0)
    for hops in range(lines - 1):
        @pl.when((line >= hops) & (line < lines - 1))
        def up(hops=hops):
            each_piece(lambda k: to_up(part(me, k), me, hops, k).wait_send())

        @pl.when((line < lines - hops) & (line > 0))
        def down(hops=hops):
            each_piece(lambda k: to_down(part(me, k), me, hops, k).wait_send())

    keep.wait()


def gather_rows(own, pieces=2):
    count = lax.axis_size("ctx")
    lines = count // 4
    rows, width = own.shape
    gathered = pl.pallas_call(
        functools.partial(gather_kernel, count, pieces),
        out_shape=jax.ShapeDtypeStruct((count, rows, width), own.dtype),
        in_specs=[pl.BlockSpec(memory_space=pltpu.VMEM)],
        out_specs=pl.BlockSpec(memory_space=pl.ANY),
        scratch_shapes=[
            pltpu.SemaphoreType.DMA,
            pltpu.SemaphoreType.DMA((lines, pieces)),
            pltpu.SemaphoreType.DMA((lines, pieces)),
            pltpu.SemaphoreType.DMA((lines, pieces)),
            pltpu.SemaphoreType.DMA((count // 2, pieces)),
            pltpu.SemaphoreType.DMA((count, pieces)),
        ],
        compiler_params=pltpu.CompilerParams(collective_id=0, has_side_effects=True),
        cost_estimate=pl.CostEstimate(flops=0, bytes_accessed=BUSY, transcendentals=0),
        name="gather_rows",
    )(own)
    return gathered.reshape(count * rows, width)


def supply_kernel(count, pieces, shared, *refs):
    inputs = len(shared) + 2
    own_ref, sources, pair_ref = refs[0], refs[1 : inputs - 1], refs[inputs - 1]
    out_ref, targets = refs[inputs], refs[inputs + 1 : 2 * inputs - 1]
    pair_out = refs[2 * inputs - 1]
    (
        keep_sem, up_sem, down_sem, across_sem, chip_sem, recv_sem,
        give_sem, take_sem, pass_sem, passed_sem, stay_sem, pair_sem,
    ) = refs[2 * inputs :]
    lines = count // 4
    me, line, side, core = own_place()
    half = lax.axis_index("fsdp")
    partner = place_of(line, side, 1 - core)
    across = place_of(line, 1 - side, core)
    rows = own_ref.shape[0] // pieces

    barrier = pltpu.get_barrier_semaphore()

    def enter(step, carried):
        pl.semaphore_signal(
            barrier, inc=1, device_id={"ctx": lax.rem(me + step, count)}, device_id_type=MESH_ID
        )
        return carried

    lax.fori_loop(1, count, enter, 0)
    pl.semaphore_signal(barrier, inc=1, device_id={"fsdp": 1 - half}, device_id_type=MESH_ID)
    pl.semaphore_wait(barrier, count)

    moves = []
    for source, target, (parts, kind) in zip(sources, targets, shared):
        wide = target.shape[2] // parts
        for part in range(parts):
            def block(goal, source=source, part=part, kind=kind, wide=wide, parts=parts):
                if kind == "same":
                    return source
                if kind == "blocks":
                    return source.at[goal]
                first = part * (source.shape[1] // parts) + goal * wide
                return source.at[:, pl.ds(pl.multiple_of(first, 128), wide)]

            def place(sender, side_of, target=target, part=part, wide=wide, parts=parts):
                at = target.at[sender * 2 + side_of]
                return at if parts == 1 else at.at[:, pl.ds(part * wide, wide)]

            moves.append((block, place))

    def origin(step):
        return lax.rem(me + count - step, count)

    def give(step, m):
        goal = lax.rem(me + step, count)
        block, place = moves[m]
        return remote(block(goal), place(me, half), give_sem.at[step, m], take_sem.at[step, m], {"ctx": goal})

    def taken(step, m):
        at = moves[m][1](origin(step), half)
        return remote(at, at, give_sem.at[step, m], take_sem.at[step, m], {"ctx": origin(step)})

    def hand(step, m, side_of):
        at = moves[m][1](origin(step), side_of)
        return remote(at, at, pass_sem.at[step, m], passed_sem.at[step, m], {"fsdp": 1 - half})

    def hand_own(m):
        block, place = moves[m]
        return remote(block(me), place(me, half), pass_sem.at[0, m], passed_sem.at[0, m], {"fsdp": 1 - half})

    def stay(m):
        block, place = moves[m]
        return pltpu.make_async_copy(block(me), place(me, half), stay_sem.at[m])

    def each_step(first, last, body):
        def step_body(step, carried):
            for m in range(len(moves)):
                body(step, m)
            return carried

        lax.fori_loop(first, last, step_body, 0)

    pair_stay = pltpu.make_async_copy(pair_ref, pair_out.at[half], stay_sem.at[len(moves)])

    def pair_copy(side_of):
        return remote(pair_ref, pair_out.at[side_of], pair_sem.at[0], pair_sem.at[1], {"fsdp": 1 - half})

    def part(block, k):
        return out_ref.at[block, pl.ds(pl.multiple_of(k * rows, rows), rows), :]

    def mine(k):
        return own_ref.at[pl.ds(pl.multiple_of(k * rows, rows), rows), :]

    def to_up(source, block, slot, k):
        return remote(source, part(block, k), up_sem.at[slot, k], recv_sem.at[block, k], {"ctx": me + 4})

    def to_down(source, block, slot, k):
        return remote(source, part(block, k), down_sem.at[slot, k], recv_sem.at[block, k], {"ctx": me - 4})

    def to_across(source, block, k):
        return remote(
            source, part(block, k), across_sem.at[block // 4, k], recv_sem.at[block, k], {"ctx": across}
        )

    def to_partner(source, block, k):
        return remote(
            source, part(block, k), chip_sem.at[block // 2, k], recv_sem.at[block, k], {"ctx": partner}
        )

    def arrived(block, k):
        to_partner(part(block, k), block, k).wait_recv()

    def each_piece(body):
        def step(k, carried):
            body(k)
            return carried

        lax.fori_loop(0, pieces, step, 0)

    keep = pltpu.make_async_copy(own_ref, out_ref.at[me], keep_sem)

    def first(k):
        @pl.when(line < lines - 1)
        def up():
            to_up(mine(k), me, 0, k).start()

        @pl.when(line > 0)
        def down():
            to_down(mine(k), me, 0, k).start()

        to_across(mine(k), me, k).start()
        to_partner(mine(k), me, k).start()

    each_piece(first)
    each_step(1, count, lambda step, m: give(step, m).start())
    pair_copy(half).start()
    for m in range(len(moves)):
        hand_own(m).start()
    keep.start()
    pair_stay.start()
    for m in range(len(moves)):
        stay(m).start()

    def pass_on(step, m):
        taken(step, m).wait_recv()
        hand(step, m, half).start()

    for hops in range(1, lines):
        def relay(k, hops=hops):
            @pl.when(line >= hops)
            def from_below():
                block = me - 4 * hops
                arrived(block, k)
                if hops < lines - 1:
                    @pl.when(line < lines - 1)
                    def up():
                        to_up(part(block, k), block, hops, k).start()

                to_across(part(block, k), block, k).start()
                to_partner(part(block, k), block, k).start()

            @pl.when(line < lines - hops)
            def from_above():
                block = me + 4 * hops
                arrived(block, k)
                if hops < lines - 1:
                    @pl.when(line > 0)
                    def down():
                        to_down(part(block, k), block, hops, k).start()

                to_across(part(block, k), block, k).start()
                to_partner(part(block, k), block, k).start()

        each_piece(relay)
        each_step(
            1 + (hops - 1) * (count - 1) // (lines - 1), 1 + hops * (count - 1) // (lines - 1), pass_on
        )

    def hand_over(block):
        def one(k):
            arrived(block, k)
            to_partner(part(block, k), block, k).start()

        each_piece(one)

    hand_over(across)
    for hops in range(1, lines):
        @pl.when(line >= hops)
        def from_below(hops=hops):
            hand_over(across - 4 * hops)

        @pl.when(line < lines - hops)
        def from_above(hops=hops):
            hand_over(across + 4 * hops)

    def settle(index, carried):
        def one(k):
            arrived(index * 2 + 1 - core, k)
            to_partner(part(me, k), index * 2 + core, k).wait_send()

        each_piece(one)
        return carried

    lax.fori_loop(0, count // 2, settle, 0)

    def settle_across(index, carried):
        each_piece(lambda k: to_across(part(me, k), index * 4, k).wait_send())
        return carried

    lax.fori_loop(0, lines, settle_across, 0)
    for hops in range(lines - 1):
        @pl.when((line >= hops) & (line < lines - 1))
        def up(hops=hops):
            each_piece(lambda k: to_up(part(me, k), me, hops, k).wait_send())

        @pl.when((line < lines - hops) & (line > 0))
        def down(hops=hops):
            each_piece(lambda k: to_down(part(me, k), me, hops, k).wait_send())

    each_step(0, count, lambda step, m: hand(step, m, 1 - half).wait_recv())
    each_step(1, count, lambda step, m: hand(step, m, half).wait_send())
    each_step(1, count, lambda step, m: give(step, m).wait_send())
    for m in range(len(moves)):
        hand_own(m).wait_send()
        stay(m).wait()
    pair_copy(1 - half).wait_recv()
    pair_copy(half).wait_send()
    pair_stay.wait()
    keep.wait()


def supply(own, arrays, shared, pair_array, collective_id, name, pieces=2):
    count = lax.axis_size("ctx")
    lines = count // 4
    rows, width = own.shape
    targets = []
    for array, (_, kind) in zip(arrays, shared):
        if kind == "columns":
            block = (array.shape[0], array.shape[1] // count)
        else:
            block = array.shape if kind == "same" else array.shape[1:]
        targets.append(jax.ShapeDtypeStruct((count * 2, *block), array.dtype))
    moves = sum(parts for parts, _ in shared)
    operands = [own, *arrays, pair_array]
    rows_all, *got, pair_all = pl.pallas_call(
        functools.partial(supply_kernel, count, pieces, tuple(shared)),
        out_shape=[
            jax.ShapeDtypeStruct((count, rows, width), own.dtype),
            *targets,
            jax.ShapeDtypeStruct((2, *pair_array.shape), pair_array.dtype),
        ],
        in_specs=[pl.BlockSpec(memory_space=pltpu.VMEM)] * len(operands),
        out_specs=[pl.BlockSpec(memory_space=pl.ANY)] * len(operands),
        scratch_shapes=[
            pltpu.SemaphoreType.DMA,
            pltpu.SemaphoreType.DMA((lines, pieces)),
            pltpu.SemaphoreType.DMA((lines, pieces)),
            pltpu.SemaphoreType.DMA((lines, pieces)),
            pltpu.SemaphoreType.DMA((count // 2, pieces)),
            pltpu.SemaphoreType.DMA((count, pieces)),
            pltpu.SemaphoreType.DMA((count, moves)),
            pltpu.SemaphoreType.DMA((count, moves)),
            pltpu.SemaphoreType.DMA((count, moves)),
            pltpu.SemaphoreType.DMA((count, moves)),
            pltpu.SemaphoreType.DMA((moves + 1,)),
            pltpu.SemaphoreType.DMA((2,)),
        ],
        compiler_params=pltpu.CompilerParams(collective_id=collective_id, has_side_effects=True),
        cost_estimate=pl.CostEstimate(flops=0, bytes_accessed=BUSY, transcendentals=0),
        name=name,
    )(*operands)
    return rows_all.reshape(count * rows, width), got, pair_all.reshape(-1, pair_array.shape[1])


def project_kernel(rows_ref, gain_ref, shift_ref, weight_ref, bias_ref, normed_ref, out_ref):
    unit, _ = norm_parts(rows_ref[...].astype(F32))
    normed = (unit * gain_ref[...] + shift_ref[...]).astype(BF16)
    normed_ref[...] = normed
    projected = jnp.dot(normed, weight_ref[...], preferred_element_type=F32)
    out_ref[...] = (projected + bias_ref[...]).astype(BF16)


def project(rows_in, gain, shift, weight, bias, block=256):
    total, width = rows_in.shape
    columns = weight.shape[1]
    row = pl.BlockSpec((1, width), lambda i: (0, 0))
    return pl.pallas_call(
        project_kernel,
        grid=(total // block,),
        in_specs=[
            pl.BlockSpec((block, width), lambda i: (i, 0)),
            row,
            row,
            pl.BlockSpec((width, columns), lambda i: (0, 0)),
            pl.BlockSpec((1, columns), lambda i: (0, 0)),
        ],
        out_specs=[
            pl.BlockSpec((block, width), lambda i: (i, 0)),
            pl.BlockSpec((block, columns), lambda i: (i, 0)),
        ],
        out_shape=[
            jax.ShapeDtypeStruct((total, width), BF16),
            jax.ShapeDtypeStruct((total, columns), BF16),
        ],
        cost_estimate=pl.CostEstimate(
            flops=2 * total * width * columns, bytes_accessed=6 * total * width, transcendentals=0
        ),
        name="project",
    )(rows_in, gain[None], shift[None], weight, bias[None])


def feed_kernel(
    normed_ref, grad_ref, up_ref, down_ref, bias_ref,
    activated_ref, grad_hidden_ref, terms_ref, branch_ref, sums_ref,
):
    hidden = jnp.dot(normed_ref[...], up_ref[...], preferred_element_type=F32) + bias_ref[...]
    grad_activated = lax.dot_general(grad_ref[...], down_ref[...], NT, preferred_element_type=F32)
    normal = 0.5 * (1.0 + lax.erf(hidden * 0.5**0.5))
    density = jnp.exp(-0.5 * hidden * hidden) * (2.0 * math.pi) ** -0.5
    activated = (hidden * normal).astype(BF16)
    grad_hidden = (grad_activated * (normal + hidden * density)).astype(BF16)
    activated_ref[...] = activated
    grad_hidden_ref[...] = grad_hidden
    terms = lax.dot_general(grad_hidden, up_ref[...], NT, preferred_element_type=F32)
    terms_ref[...] = terms.astype(BF16)
    branch = jnp.dot(activated, down_ref[...], preferred_element_type=F32)
    branch_ref[...] = branch.astype(BF16)

    @pl.when(pl.program_id(0) == 0)
    def clear():
        sums_ref[...] = jnp.zeros_like(sums_ref)

    sums_ref[...] += jnp.sum(grad_hidden.astype(F32), axis=0, keepdims=True)


def feed(normed, grads, w_up, w_down, bias, block=256):
    total, width = normed.shape
    hidden = w_up.shape[1]
    wide = pl.BlockSpec((block, width), lambda i: (i, 0))
    narrow_rows = pl.BlockSpec((block, hidden), lambda i: (i, 0))
    return pl.pallas_call(
        feed_kernel,
        grid=(total // block,),
        in_specs=[
            wide,
            wide,
            pl.BlockSpec((width, hidden), lambda i: (0, 0)),
            pl.BlockSpec((hidden, width), lambda i: (0, 0)),
            pl.BlockSpec((1, hidden), lambda i: (0, 0)),
        ],
        out_specs=[narrow_rows, narrow_rows, wide, wide, pl.BlockSpec((1, hidden), lambda i: (0, 0))],
        out_shape=[
            jax.ShapeDtypeStruct((total, hidden), BF16),
            jax.ShapeDtypeStruct((total, hidden), BF16),
            jax.ShapeDtypeStruct((total, width), BF16),
            jax.ShapeDtypeStruct((total, width), BF16),
            jax.ShapeDtypeStruct((1, hidden), F32),
        ],
        cost_estimate=pl.CostEstimate(flops=0, bytes_accessed=BUSY // 3, transcendentals=0),
        name="feed",
    )(normed, grads, w_up, w_down, bias[None])


def sum_kernel(
    count, pieces, riders, *refs
):
    if riders:
        (
            part_ref, grad_ref, pair_ref, out_ref, got_ref, pair_out,
            held, chip_in, across_in, line_in, grad_in, grad_sum, load_sem,
            chip_send, chip_recv, across_send, across_recv, line_send, line_recv,
            pass_sem, passed_sem, give_sem, take_sem, pair_sem,
        ) = refs
    else:
        (
            part_ref, out_ref, held, chip_in, across_in, line_in, load_sem,
            chip_send, chip_recv, across_send, across_recv, line_send, line_recv,
        ) = refs
    lines = count // 4
    me, line, side, core = own_place()
    partner = place_of(line, side, 1 - core)
    across = place_of(line, 1 - side, core)
    rows = out_ref.shape[0] // pieces

    def at(ref, block, k):
        return ref.at[block, pl.ds(pl.multiple_of(k * rows, rows), rows), :]

    def to_partner(pair, k):
        return remote(
            at(part_ref, pair * 2 + 1 - core, k), at(chip_in, pair, k),
            chip_send.at[pair, k], chip_recv.at[pair, k], {"ctx": partner},
        )

    def to_across(goal, k):
        return remote(
            at(held, goal * 2 + 1 - side, k), at(across_in, goal, k),
            across_send.at[goal, k], across_recv.at[goal, k], {"ctx": across},
        )

    def to_next(goal, target, slot, k):
        return remote(
            at(held, goal * 2 + side, k), at(line_in, slot, k),
            line_send.at[goal, k], line_recv.at[slot, k], {"ctx": target},
        )

    def each_piece(body):
        def step(k, carried):
            body(k)
            return carried

        lax.fori_loop(0, pieces, step, 0)

    def far_first(visit, between=None):
        for hops in range(lines - 1, 0, -1):
            @pl.when(line + hops < lines)
            def ahead(hops=hops):
                visit(line + hops, 1)

            @pl.when(line >= hops)
            def behind(hops=hops):
                visit(line - hops, -1)

            if between is not None:
                between(lines - hops)

    half = lax.axis_index("fsdp")
    barrier = pltpu.get_barrier_semaphore()

    def enter(step, carried):
        pl.semaphore_signal(
            barrier, inc=1, device_id={"ctx": lax.rem(me + step, count)}, device_id_type=MESH_ID
        )
        return carried

    def hand(step):
        goal = lax.rem(me + step, count)
        return remote(
            grad_ref.at[goal, 1 - half], grad_in.at[goal], pass_sem.at[step], passed_sem.at[step],
            {"fsdp": 1 - half},
        )

    def give_grad(step):
        goal = lax.rem(me + step, count)
        return remote(
            grad_sum.at[goal], got_ref.at[me], give_sem.at[step], take_sem.at[step], {"ctx": goal}
        )

    def take_grad(step):
        source = lax.rem(me + count - step, count)
        return remote(
            grad_sum.at[source], got_ref.at[source], give_sem.at[step], take_sem.at[step], {"ctx": source}
        )

    def each_step(first, last, body):
        def step_body(step, carried):
            body(step)
            return carried

        lax.fori_loop(first, last, step_body, 0)

    def pass_on(step):
        goal = lax.rem(me + step, count)
        hand(step).wait_recv()
        grad_sum[goal] = (grad_ref[goal, half].astype(F32) + grad_in[goal].astype(F32)).astype(BF16)
        give_grad(step).start()

    def pair_copy():
        return remote(pair_ref.at[1 - half], pair_out, pair_sem.at[0], pair_sem.at[1], {"fsdp": 1 - half})

    loads = [
        pltpu.make_async_copy(part_ref.at[pair * 2 + core], held.at[pair], load_sem.at[pair])
        for pair in range(count // 2)
    ]
    for load in loads:
        load.start()
    lax.fori_loop(1, count, enter, 0)
    pl.semaphore_signal(barrier, inc=1, device_id={"fsdp": 1 - half}, device_id_type=MESH_ID)
    pl.semaphore_wait(barrier, count)

    def give(goal, way):
        each_piece(lambda k: to_partner(goal * 2 + 1 - side, k).start())

    def give_same(goal, way):
        each_piece(lambda k: to_partner(goal * 2 + side, k).start())

    if riders:
        each_step(1, count, lambda step: hand(step).start())
        hand(0).start()
        pair_copy().start()
    far_first(give)
    give(line, 0)
    far_first(give_same)
    give_same(line, 0)
    for load in loads:
        load.wait()

    def read(ref, block, k):
        return ref[block, pl.ds(pl.multiple_of(k * rows, rows), rows), :].astype(F32)

    def write(block, k, value):
        held[block, pl.ds(pl.multiple_of(k * rows, rows), rows), :] = value.astype(held.dtype)

    def cross(goal, way):
        pair = goal * 2 + 1 - side

        def one(k):
            to_partner(pair, k).wait_recv()
            write(pair, k, read(held, pair, k) + read(chip_in, pair, k))
            to_across(goal, k).start()

        each_piece(one)

    far_first(cross)
    cross(line, 0)

    def two_sums(goal, k):
        pair = goal * 2 + side
        to_partner(pair, k).wait_recv()
        to_across(goal, k).wait_recv()
        return read(held, pair, k) + read(chip_in, pair, k) + read(across_in, goal, k)

    def along(goal, way):
        pair = goal * 2 + side
        target = me + 4 * way
        arriving = goal
        if way == 1:
            slot = goal
            fed = line > 0
        else:
            fed = line < lines - 1
            slot = jnp.where(goal == line - 1, lines, goal)

        def one(k):
            total = two_sums(goal, k)
            write(pair, k, total)

            @pl.when(fed)
            def add():
                to_next(goal, target, arriving, k).wait_recv()
                write(pair, k, total + read(line_in, arriving, k))

            to_next(goal, target, slot, k).start()

        each_piece(one)

    def share_of_steps(turn):
        each_step(
            1 + (turn - 1) * (count - 1) // (lines - 1), 1 + turn * (count - 1) // (lines - 1), pass_on
        )

    far_first(along, share_of_steps if riders else None)
    if riders:
        hand(0).wait_recv()
        grad_sum[me] = (grad_ref[me, half].astype(F32) + grad_in[me].astype(F32)).astype(BF16)
        stay = pltpu.make_async_copy(grad_sum.at[me], got_ref.at[me], pair_sem.at[2])
        stay.start()

    def last(k):
        span = pl.ds(pl.multiple_of(k * rows, rows), rows)
        out_ref[span, :] = two_sums(line, k)

        @pl.when(line > 0)
        def from_below():
            to_next(line, me, line, k).wait_recv()
            out_ref[span, :] += read(line_in, line, k)

        @pl.when(line < lines - 1)
        def from_above():
            to_next(line, me, lines, k).wait_recv()
            out_ref[span, :] += read(line_in, lines, k)

    each_piece(last)

    def settle(index, carried):
        each_piece(lambda k: to_partner(index, k).wait_send())
        return carried

    lax.fori_loop(0, count // 2, settle, 0)

    def settle_line(goal, carried):
        each_piece(lambda k: to_across(goal, k).wait_send())

        @pl.when(goal != line)
        def sent():
            each_piece(lambda k: to_next(goal, me, goal, k).wait_send())

        return carried

    lax.fori_loop(0, lines, settle_line, 0)
    if riders:
        each_step(1, count, lambda step: take_grad(step).wait_recv())
        each_step(1, count, lambda step: give_grad(step).wait_send())
        each_step(0, count, lambda step: hand(step).wait_send())
        pair_copy().wait_recv()
        pair_copy().wait_send()
        stay.wait()


def sum_rows(partial, collective_id, grad=None, pair_grad=None, pieces=2):
    count = lax.axis_size("ctx")
    lines = count // 4
    width = partial.shape[1]
    rows = partial.shape[0] // count
    riders = grad is not None
    anywhere = pl.BlockSpec(memory_space=pl.ANY)
    in_vmem = pl.BlockSpec(memory_space=pltpu.VMEM)
    operands = [partial.astype(BF16).reshape(count, rows, width)]
    results = [jax.ShapeDtypeStruct((rows, width), F32)]
    buffers = [
        pltpu.VMEM((count // 2, rows, width), BF16),
        pltpu.VMEM((count // 2, rows, width), BF16),
        pltpu.VMEM((lines, rows, width), BF16),
        pltpu.VMEM((lines + 1, rows, width), BF16),
    ]
    semaphores = [(count // 2,)] + [(count // 2, pieces)] * 2 + [(lines, pieces)] * 3 + [(lines + 1, pieces)]
    if riders:
        owned, columns = grad.shape[0] // (2 * count), grad.shape[1]
        pair_shape = (pair_grad.shape[0] // 2, pair_grad.shape[1])
        operands += [grad.reshape(count, 2, owned, columns), pair_grad.reshape(2, *pair_shape)]
        results += [
            jax.ShapeDtypeStruct((count, owned, columns), BF16),
            jax.ShapeDtypeStruct(pair_shape, BF16),
        ]
        buffers += [pltpu.VMEM((count, owned, columns), BF16)] * 2
        semaphores += [(count,)] * 4 + [(3,)]
    done = pl.pallas_call(
        functools.partial(sum_kernel, count, pieces, riders),
        out_shape=results,
        in_specs=[anywhere] + [in_vmem, anywhere] * riders,
        out_specs=[in_vmem] + [anywhere] * (2 * riders),
        scratch_shapes=buffers + [pltpu.SemaphoreType.DMA(shape) for shape in semaphores],
        compiler_params=pltpu.CompilerParams(
            collective_id=collective_id, has_side_effects=True, vmem_limit_bytes=63 * 2**20
        ),
        cost_estimate=pl.CostEstimate(flops=0, bytes_accessed=BUSY, transcendentals=0),
        name="sum_rows",
    )(*operands)
    return done if riders else done[0]


def own_half(pair_grad, other):
    half = pair_grad.shape[0] // 2
    kept = lax.dynamic_slice_in_dim(pair_grad, lax.axis_index("fsdp") * half, half, 0)
    return kept.astype(F32) + other.astype(F32)


def in_order(got, parts):
    count, owned, _ = got.shape
    return got.reshape(count, owned, parts, -1).transpose(1, 2, 0, 3).reshape(owned, -1).astype(F32)


def weight_grad(rows_in, grads):
    terms = lax.dot_general(rows_in, grads, TN, preferred_element_type=F32).astype(BF16)
    return lax.optimization_barrier(terms)


def widen(columns, share, axis=-1):
    if share == 1:
        return columns
    count = lax.axis_size("ctx")
    groups = [list(range(first, first + share)) for first in range(0, count, share)]
    return lax.all_gather(
        columns, "ctx", axis=axis % columns.ndim, tiled=True, axis_index_groups=groups
    )


def narrow(columns, share):
    if share == 1:
        return columns
    width = columns.shape[-1] // share
    place = lax.rem(lax.axis_index("ctx"), share)
    return lax.dynamic_slice_in_dim(columns, place * width, width, columns.ndim - 1)


def on_device(
    tokens, doc_lengths, ln1_gain, ln1_bias, w_qkv, bias_q, bias_v, w_out, b_out,
    ln2_gain, ln2_bias, w_up, b_up, w_down, b_down, cotangent,
):
    count = lax.axis_size("ctx")
    rank = lax.axis_index("ctx")
    pair_rank = lax.axis_index("fsdp")
    tok_rows, width = tokens.shape[1:]
    seq_len = tok_rows * count
    own_cols = width // count
    share = max(1, HEAD_DIM // own_cols)
    head_count = width // HEAD_DIM
    heads = own_cols * share // HEAD_DIM
    rows = min(256, seq_len)

    lengths = doc_lengths[0]
    doc_starts = jnp.cumsum(lengths) - lengths
    positions = jnp.arange(seq_len, dtype=jnp.int32)
    starts = jnp.max(
        jnp.where(doc_starts[None, :] <= positions[:, None], doc_starts[None, :], 0), axis=1
    ).astype(jnp.int32)
    low = starts[::rows] // rows
    starts = starts[None, :]
    first_head = (rank // share) * heads
    head_ids = (first_head + jnp.arange(heads)).astype(F32)
    slopes = 2.0 ** (-8.0 * (head_ids + 1.0) / head_count)

    vectors = [ln1_gain, ln1_bias, b_out, ln2_gain, ln2_bias, b_down, bias_q, bias_v, b_up]
    devices = count * lax.axis_size("fsdp")
    own_vectors = jnp.concatenate([vector.astype(F32) for vector in vectors])
    tiles = -(-own_vectors.shape[0] // 1024) * 8
    own_vectors = jnp.pad(own_vectors, (0, tiles * 128 - own_vectors.shape[0])).reshape(tiles, 128)
    if own_cols % 128 == 0:
        qkv_blocks, qkv_kind = w_qkv, (3, "columns")
    else:
        split = w_qkv.reshape(w_qkv.shape[0], 3, count, own_cols).transpose(2, 0, 1, 3)
        qkv_blocks, qkv_kind = split.reshape(count, w_qkv.shape[0], -1), (1, "blocks")
    tokens_all, (w_qkv_own, everywhere), w_out_own = supply(
        tokens[0], [qkv_blocks, own_vectors], [qkv_kind, (1, "same")], w_out, 3, "begin"
    )
    w_qkv_own = w_qkv_own.reshape(width, -1)
    everywhere = everywhere.reshape(devices, -1)
    at = 0
    whole_vectors = []
    for vector in vectors:
        whole_vectors.append(everywhere[:, at : at + vector.shape[0]].reshape(-1))
        at += vector.shape[0]
    gain_one, shift_one, b_out_all, gain_two, shift_two, b_down_all = whole_vectors[:6]
    head_at = first_head * HEAD_DIM
    bias_q_own, bias_v_own = (
        lax.dynamic_slice_in_dim(vector, head_at, heads * HEAD_DIM) for vector in whole_vectors[6:8]
    )
    ff_cols = whole_vectors[8].shape[0] // count
    b_up_own = lax.dynamic_slice_in_dim(whole_vectors[8], rank * ff_cols, ff_cols)

    w_qkv_head = widen(w_qkv_own.reshape(width, 3, -1), share).reshape(width, -1)
    w_out_head = widen(w_out_own, share, 0)

    inputs = tokens[0].astype(F32)
    unit_one, rate_one = norm_parts(inputs)
    grad_out = cotangent[0]
    tokens_all, cotangent_rows = lax.optimization_barrier((tokens_all, grad_out))
    grad_out_all = gather_beside(cotangent_rows)

    head_width = heads * HEAD_DIM
    shift = jnp.concatenate([bias_q_own, jnp.zeros(head_width, F32), bias_v_own])
    normed_all, projected = project(tokens_all, gain_one, shift_one, w_qkv_head, shift)
    projected = to_sequence(projected, count)
    queries, keys, values = (
        projected[:, part * head_width : (part + 1) * head_width] for part in range(3)
    )
    attended_full, log_total = attend(queries, keys, values, starts, low, slopes, rows)
    attended_own = narrow(to_layout(attended_full.astype(BF16), count), share)
    attended_terms = jnp.dot(attended_own, w_out_own, preferred_element_type=F32)
    middle = inputs + sum_rows(attended_terms, 4) + b_out_all

    unit_two, rate_two = norm_parts(middle)
    normed_two = (unit_two * gain_two + shift_two).astype(BF16)
    normed_two_all, (w_up_own,), w_down_own = supply(
        normed_two, [w_up], [(1, "columns")], w_down, 5, "middle"
    )
    w_up_own = w_up_own.reshape(width, -1)
    activated, grad_hidden, terms, branch_terms, grad_hidden_sums = feed(
        normed_two_all, grad_out_all, w_up_own, w_down_own, b_up_own
    )
    w_down_terms = weight_grad(activated, grad_out_all)
    grad_normed_two, w_up_got, w_down_other = sum_rows(
        terms, 1, weight_grad(normed_two_all, grad_hidden), w_down_terms
    )

    grad_middle = grad_out.astype(F32) + norm_back(unit_two, rate_two, gain_two, grad_normed_two)
    grad_branch = grad_middle.astype(BF16)
    grad_branch, branch_terms = lax.optimization_barrier((grad_branch, branch_terms))
    branch = sum_beside(branch_terms)
    grad_branch_all = gather_rows(grad_branch)
    grad_heads = lax.dot_general(
        grad_branch_all, w_out_head, NT, preferred_element_type=F32
    ).astype(BF16)
    grad_heads = to_sequence(grad_heads, count)

    delta = (grad_heads.astype(F32) * attended_full).reshape(seq_len, heads, HEAD_DIM)
    delta = jnp.sum(delta, axis=-1).T
    grad_parts = attend_back(
        queries, keys, values, grad_heads, starts, low, slopes, log_total, delta, rows
    )
    grad_qkv = jnp.concatenate(
        [narrow(to_layout(part, count), share) for part in grad_parts], axis=1
    )
    column_sums = jnp.sum(grad_qkv.astype(F32), axis=0)
    w_out_terms = weight_grad(attended_own, grad_branch_all)
    grad_normed, w_qkv_got, w_out_other = sum_rows(
        lax.dot_general(grad_qkv, w_qkv_own, NT, preferred_element_type=F32),
        2,
        weight_grad(normed_all, grad_qkv),
        w_out_terms,
    )
    branch, middle, grad_normed = lax.optimization_barrier((branch, middle, grad_normed))
    outputs = (middle + branch + b_down_all).astype(BF16)
    grad_inputs = grad_middle + norm_back(unit_one, rate_one, gain_one, grad_normed)

    pair = devices // count
    full_sums = jnp.stack(
        [
            jnp.sum(grad_normed * unit_one, axis=0),
            jnp.sum(grad_normed, axis=0),
            jnp.sum(grad_normed_two * unit_two, axis=0),
            jnp.sum(grad_normed_two, axis=0),
            jnp.sum(grad_branch.astype(F32), axis=0),
            jnp.sum(grad_out.astype(F32), axis=0),
        ]
    )
    full_sums = full_sums.reshape(6, devices, -1).transpose(1, 0, 2).reshape(devices, -1)
    own_sums = jnp.concatenate(
        [
            column_sums[:own_cols].reshape(pair, -1),
            column_sums[2 * own_cols :].reshape(pair, -1),
            grad_hidden_sums.reshape(pair, -1),
        ],
        axis=1,
    )
    full_sums, w_qkv_got, w_up_got, w_out_other, w_down_other = lax.optimization_barrier(
        (full_sums, w_qkv_got, w_up_got, w_out_other, w_down_other)
    )
    grad_w_qkv = in_order(w_qkv_got, 3)
    grad_w_up = in_order(w_up_got, 1)
    grad_w_out = own_half(w_out_terms, w_out_other)
    grad_w_down = own_half(w_down_terms, w_down_other)
    here = (jnp.arange(count) == rank)[:, None, None]
    own_sums = jnp.where(here, own_sums[None], 0.0).reshape(devices, -1)
    sums = jnp.sum(exchange(jnp.concatenate([full_sums, own_sums], axis=1)), axis=0)
    share_of = width // devices
    (
        grad_ln1_gain, grad_ln1_bias, grad_ln2_gain, grad_ln2_bias, grad_b_out, grad_b_down,
        grad_bias_q, grad_bias_v,
    ) = sums[: 8 * share_of].reshape(8, share_of)
    grad_b_up = sums[8 * share_of :]
    return (
        outputs[None],
        grad_inputs[None],
        grad_ln1_gain,
        grad_ln1_bias,
        grad_w_qkv,
        grad_bias_q,
        grad_bias_v,
        grad_w_out,
        grad_b_out,
        grad_ln2_gain,
        grad_ln2_bias,
        grad_w_up,
        grad_b_up,
        grad_w_down,
        grad_b_down,
    )


def solution(mesh):
    spread = P(BOTH)
    matrix = P(BOTH, None)
    rows = P("fsdp", "ctx", None)
    placed = (
        rows, P("fsdp", None), spread, spread, matrix, spread, spread, matrix, spread,
        spread, spread, matrix, spread, matrix, spread, rows,
    )
    results = (
        rows, rows, spread, spread, matrix, spread, spread, matrix, spread,
        spread, spread, matrix, spread, matrix, spread,
    )
    return jax.shard_map(
        on_device, mesh=mesh, in_specs=placed, out_specs=results, check_vma=False
    )
```

```python
import functools
import math

import jax
import jax.numpy as jnp
from jax import lax
from jax.experimental import pallas as pl
from jax.experimental.pallas import tpu as pltpu
from jax.sharding import PartitionSpec as P

HEAD_DIM = 64
EPSILON = 1e-05
MASKED = -1e30
BOTH = ("ctx", "fsdp")
NT = (((1,), (1,)), ((), ()))
TN = (((0,), (0,)), ((), ()))
F32 = jnp.float32
BF16 = jnp.bfloat16
BUSY = 160 * 2**20


def norm_parts(values):
    centred = values - jnp.mean(values, axis=-1, keepdims=True)
    rate = lax.rsqrt(jnp.mean(centred * centred, axis=-1, keepdims=True) + EPSILON)
    return centred * rate, rate


def norm_back(unit, rate, gain, grad):
    scaled = grad * gain
    return rate * (
        scaled
        - jnp.mean(scaled, axis=-1, keepdims=True)
        - unit * jnp.mean(scaled * unit, axis=-1, keepdims=True)
    )


def block_parts(key_block, query_block, rows):
    key_at = key_block * rows + lax.broadcasted_iota(jnp.int32, (rows, rows), 0)
    query_at = query_block * rows + lax.broadcasted_iota(jnp.int32, (rows, rows), 1)
    return key_at, query_at


def head_mask(values, head):
    lanes = lax.broadcasted_iota(jnp.int32, values.shape, 1)
    return jnp.where(lanes // HEAD_DIM == head, values, jnp.zeros_like(values))


def scores_block(keys, query_head, slope, distance, allowed):
    raw = lax.dot_general(keys, query_head, NT, preferred_element_type=F32)
    return jnp.where(allowed, raw * HEAD_DIM ** (-0.5) - slope * distance, MASKED)


def attend_kernel(rows, heads, low_ref, slope_ref, start_ref, q_ref, k_ref, v_ref, out_ref, total_ref):
    block = pl.program_id(0)
    low = low_ref[block]
    starts = start_ref[...]
    queries = q_ref[...]
    query_heads = [head_mask(queries, head) for head in range(heads)]

    def parts(key_block):
        key_at, query_at = block_parts(key_block, block, rows)
        allowed = (key_at <= query_at) & (key_at >= starts)
        at = pl.ds(pl.multiple_of(key_block * rows, rows), rows)
        return (query_at - key_at).astype(F32), allowed, at

    def step(key_block, carried):
        distance, allowed, at = parts(key_block)
        keys = k_ref[at, :]
        values = v_ref[at, :]
        following = []
        for head in range(heads):
            top, total, accum = carried[head]
            scores = scores_block(keys, query_heads[head], slope_ref[head], distance, allowed)
            new_top = jnp.maximum(top, jnp.max(scores, axis=0, keepdims=True))
            shrink = jnp.exp(top - new_top)
            weights = jnp.exp(scores - new_top)
            total = total * shrink + jnp.sum(weights, axis=0, keepdims=True)
            accum = accum * shrink + lax.dot_general(
                values, weights.astype(BF16), TN, preferred_element_type=F32
            )
            following.append((new_top, total, accum))
        return following

    width = out_ref.shape[1]
    begin = (jnp.full((1, rows), MASKED, F32), jnp.zeros((1, rows), F32), jnp.zeros((width, rows), F32))
    done = lax.fori_loop(low, block + 1, step, [begin] * heads)
    for head in range(heads):
        top, total, accum = done[head]
        total_ref[head : head + 1, :] = top + jnp.log(total)
        span = slice(head * HEAD_DIM, (head + 1) * HEAD_DIM)
        out_ref[:, span] = jnp.transpose(accum[span, :] / total)


def attend_back_kernel(
    rows, heads, low_ref, slope_ref, start_ref, total_ref, delta_ref, q_ref, g_ref, k_ref, v_ref,
    dq_ref, dk_ref, dv_ref, dk_sum, dv_sum,
):
    block = pl.program_id(0)
    low = low_ref[block]
    starts = start_ref[...]
    query_heads = [head_mask(q_ref[...], head) for head in range(heads)]
    grad_heads = [head_mask(g_ref[...], head) for head in range(heads)]
    log_totals = [total_ref[head : head + 1, :] for head in range(heads)]
    deltas = [delta_ref[head : head + 1, :] for head in range(heads)]

    @pl.when(block == 0)
    def clear():
        dk_sum[...] = jnp.zeros_like(dk_sum)
        dv_sum[...] = jnp.zeros_like(dv_sum)

    def step(key_block, accum):
        key_at, query_at = block_parts(key_block, block, rows)
        allowed = (key_at <= query_at) & (key_at >= starts)
        distance = (query_at - key_at).astype(F32)
        at = pl.ds(pl.multiple_of(key_block * rows, rows), rows)
        keys = k_ref[at, :]
        values = v_ref[at, :]
        dk_part = jnp.zeros(keys.shape, F32)
        dv_part = jnp.zeros(keys.shape, F32)
        for head in range(heads):
            scores = scores_block(keys, query_heads[head], slope_ref[head], distance, allowed)
            probs = jnp.exp(scores - log_totals[head])
            grad_probs = lax.dot_general(values, grad_heads[head], NT, preferred_element_type=F32)
            grad_scores = (probs * (grad_probs - deltas[head])).astype(BF16)
            dv_part = dv_part + jnp.dot(
                probs.astype(BF16), grad_heads[head], preferred_element_type=F32
            )
            dk_part = dk_part + jnp.dot(grad_scores, query_heads[head], preferred_element_type=F32)
            accum = accum + lax.dot_general(
                grad_scores, head_mask(keys, head), TN, preferred_element_type=F32
            )
        dk_sum[at, :] += dk_part
        dv_sum[at, :] += dv_part
        return accum

    grad = lax.fori_loop(low, block + 1, step, jnp.zeros(dq_ref.shape, F32))
    dq_ref[...] = (grad * HEAD_DIM ** (-0.5)).astype(BF16)

    @pl.when(block == pl.num_programs(0) - 1)
    def store():
        dk_ref[...] = (dk_sum[...] * HEAD_DIM ** (-0.5)).astype(BF16)
        dv_ref[...] = dv_sum[...].astype(BF16)


def attend(queries, keys, values, starts, low, slopes, rows):
    seq_len, width = queries.shape
    heads = width // HEAD_DIM
    whole = pl.BlockSpec((seq_len, width), lambda i: (0, 0))
    block = pl.BlockSpec((rows, width), lambda i: (i, 0))
    row = pl.BlockSpec((1, rows), lambda i: (0, i))
    stat = pl.BlockSpec((heads, rows), lambda i: (0, i))
    scalar = pl.BlockSpec(memory_space=pltpu.SMEM)
    return pl.pallas_call(
        functools.partial(attend_kernel, rows, heads),
        grid=(seq_len // rows,),
        in_specs=[scalar, scalar, row, block, whole, whole],
        out_specs=[block, stat],
        out_shape=[
            jax.ShapeDtypeStruct((seq_len, width), F32),
            jax.ShapeDtypeStruct((heads, seq_len), F32),
        ],
        cost_estimate=pl.CostEstimate(flops=0, bytes_accessed=BUSY // 3, transcendentals=0),
        name="attend",
    )(low, slopes, starts, queries, keys, values)


def attend_back(queries, keys, values, grads, starts, low, slopes, log_total, delta, rows):
    seq_len, width = queries.shape
    heads = width // HEAD_DIM
    whole = pl.BlockSpec((seq_len, width), lambda i: (0, 0))
    block = pl.BlockSpec((rows, width), lambda i: (i, 0))
    row = pl.BlockSpec((1, rows), lambda i: (0, i))
    stat = pl.BlockSpec((heads, rows), lambda i: (0, i))
    scalar = pl.BlockSpec(memory_space=pltpu.SMEM)
    return pl.pallas_call(
        functools.partial(attend_back_kernel, rows, heads),
        grid=(seq_len // rows,),
        in_specs=[scalar, scalar, row, stat, stat, block, block, whole, whole],
        out_specs=[block, whole, whole],
        out_shape=[jax.ShapeDtypeStruct((seq_len, width), BF16)] * 3,
        scratch_shapes=[pltpu.VMEM((seq_len, width), F32)] * 2,
        cost_estimate=pl.CostEstimate(flops=0, bytes_accessed=BUSY // 3, transcendentals=0),
        name="attend_back",
    )(low, slopes, starts, log_total, delta, queries, grads, keys, values)


def to_sequence(rows_in, count):
    halves = rows_in.reshape(count, 2, rows_in.shape[0] // (2 * count), -1)
    return jnp.concatenate([halves[:, 0], halves[::-1, 1]], axis=0).reshape(rows_in.shape)


def to_layout(rows_in, count):
    blocks = rows_in.reshape(2, count, rows_in.shape[0] // (2 * count), -1)
    return jnp.stack([blocks[0], blocks[1, ::-1]], axis=1).reshape(rows_in.shape)


def gather_beside(rows_in):
    return lax.all_gather(rows_in, "ctx", axis=0, tiled=True)


def sum_beside(partial):
    return lax.psum_scatter(partial.astype(BF16), "ctx", scatter_dimension=0, tiled=True).astype(F32)


def exchange(blocks):
    total, width = blocks.shape
    tiles = -(-width // 1024) * 8
    padded = jnp.pad(blocks, ((0, 0), (0, tiles * 128 - width))).reshape(total, tiles, 128)
    got = lax.all_to_all(padded, BOTH, split_axis=0, concat_axis=0)
    return got.reshape(total, tiles * 128)[:, :width]


MESH_ID = pl.DeviceIdType.MESH

def remote(source, target, send_sem, recv_sem, device):
    return pltpu.make_async_remote_copy(
        src_ref=source, dst_ref=target, send_sem=send_sem, recv_sem=recv_sem,
        device_id=device, device_id_type=MESH_ID,
    )


def place_of(line, side, core):
    return (line * 2 + side) * 2 + core


def own_place():
    me = lax.axis_index("ctx")
    return me, me // 4, (me // 2) % 2, me % 2


def greet(lines):
    me, line, side, core = own_place()
    barrier = pltpu.get_barrier_semaphore()

    def signal(target):
        pl.semaphore_signal(barrier, inc=1, device_id={"ctx": target}, device_id_type=MESH_ID)

    signal(place_of(line, side, 1 - core))
    signal(place_of(line, 1 - side, core))

    @pl.when(line > 0)
    def below():
        signal(me - 4)

    @pl.when(line < lines - 1)
    def above():
        signal(me + 4)

    pl.semaphore_wait(
        barrier, 2 + jnp.where(line > 0, 1, 0) + jnp.where(line < lines - 1, 1, 0)
    )


def gather_kernel(
    count, pieces, own_ref, out_ref, keep_sem, up_sem, down_sem, across_sem, chip_sem, recv_sem
):
    lines = count // 4
    me, line, side, core = own_place()
    partner = place_of(line, side, 1 - core)
    across = place_of(line, 1 - side, core)
    rows = own_ref.shape[0] // pieces

    def part(block, k):
        return out_ref.at[block, pl.ds(pl.multiple_of(k * rows, rows), rows), :]

    def mine(k):
        return own_ref.at[pl.ds(pl.multiple_of(k * rows, rows), rows), :]

    def to_up(source, block, slot, k):
        return remote(source, part(block, k), up_sem.at[slot, k], recv_sem.at[block, k], {"ctx": me + 4})

    def to_down(source, block, slot, k):
        return remote(source, part(block, k), down_sem.at[slot, k], recv_sem.at[block, k], {"ctx": me - 4})

    def to_across(source, block, k):
        return remote(
            source, part(block, k), across_sem.at[block // 4, k], recv_sem.at[block, k], {"ctx": across}
        )

    def to_partner(source, block, k):
        return remote(
            source, part(block, k), chip_sem.at[block // 2, k], recv_sem.at[block, k], {"ctx": partner}
        )

    def arrived(block, k):
        to_partner(part(block, k), block, k).wait_recv()

    def each_piece(body):
        def step(k, carried):
            body(k)
            return carried

        lax.fori_loop(0, pieces, step, 0)

    greet(lines)
    keep = pltpu.make_async_copy(own_ref, out_ref.at[me], keep_sem)
    keep.start()

    def first(k):
        @pl.when(line < lines - 1)
        def up():
            to_up(mine(k), me, 0, k).start()

        @pl.when(line > 0)
        def down():
            to_down(mine(k), me, 0, k).start()

        to_across(mine(k), me, k).start()
        to_partner(mine(k), me, k).start()

    each_piece(first)
    for hops in range(1, lines):
        def relay(k, hops=hops):
            @pl.when(line >= hops)
            def from_below():
                block = me - 4 * hops
                arrived(block, k)
                if hops < lines - 1:
                    @pl.when(line < lines - 1)
                    def up():
                        to_up(part(block, k), block, hops, k).start()

                to_across(part(block, k), block, k).start()
                to_partner(part(block, k), block, k).start()

            @pl.when(line < lines - hops)
            def from_above():
                block = me + 4 * hops
                arrived(block, k)
                if hops < lines - 1:
                    @pl.when(line > 0)
                    def down():
                        to_down(part(block, k), block, hops, k).start()

                to_across(part(block, k), block, k).start()
                to_partner(part(block, k), block, k).start()

        each_piece(relay)

    def hand_over(block):
        def one(k):
            arrived(block, k)
            to_partner(part(block, k), block, k).start()

        each_piece(one)

    hand_over(across)
    for hops in range(1, lines):
        @pl.when(line >= hops)
        def from_below(hops=hops):
            hand_over(across - 4 * hops)

        @pl.when(line < lines - hops)
        def from_above(hops=hops):
            hand_over(across + 4 * hops)

    def settle(index, carried):
        def one(k):
            arrived(index * 2 + 1 - core, k)
            to_partner(part(me, k), index * 2 + core, k).wait_send()

        each_piece(one)
        return carried

    lax.fori_loop(0, count // 2, settle, 0)

    def settle_across(index, carried):
        each_piece(lambda k: to_across(part(me, k), index * 4, k).wait_send())
        return carried

    lax.fori_loop(0, lines, settle_across, 0)
    for hops in range(lines - 1):
        @pl.when((line >= hops) & (line < lines - 1))
        def up(hops=hops):
            each_piece(lambda k: to_up(part(me, k), me, hops, k).wait_send())

        @pl.when((line < lines - hops) & (line > 0))
        def down(hops=hops):
            each_piece(lambda k: to_down(part(me, k), me, hops, k).wait_send())

    keep.wait()


def gather_rows(own, pieces=2):
    count = lax.axis_size("ctx")
    lines = count // 4
    rows, width = own.shape
    gathered = pl.pallas_call(
        functools.partial(gather_kernel, count, pieces),
        out_shape=jax.ShapeDtypeStruct((count, rows, width), own.dtype),
        in_specs=[pl.BlockSpec(memory_space=pltpu.VMEM)],
        out_specs=pl.BlockSpec(memory_space=pl.ANY),
        scratch_shapes=[
            pltpu.SemaphoreType.DMA,
            pltpu.SemaphoreType.DMA((lines, pieces)),
            pltpu.SemaphoreType.DMA((lines, pieces)),
            pltpu.SemaphoreType.DMA((lines, pieces)),
            pltpu.SemaphoreType.DMA((count // 2, pieces)),
            pltpu.SemaphoreType.DMA((count, pieces)),
        ],
        compiler_params=pltpu.CompilerParams(collective_id=0, has_side_effects=True),
        cost_estimate=pl.CostEstimate(flops=0, bytes_accessed=BUSY, transcendentals=0),
        name="gather_rows",
    )(own)
    return gathered.reshape(count * rows, width)


def supply_kernel(count, pieces, shared, *refs):
    inputs = len(shared) + 2
    own_ref, sources, pair_ref = refs[0], refs[1 : inputs - 1], refs[inputs - 1]
    out_ref, targets = refs[inputs], refs[inputs + 1 : 2 * inputs - 1]
    pair_out = refs[2 * inputs - 1]
    (
        keep_sem, up_sem, down_sem, across_sem, chip_sem, recv_sem,
        give_sem, take_sem, pass_sem, passed_sem, stay_sem, pair_sem,
    ) = refs[2 * inputs :]
    lines = count // 4
    me, line, side, core = own_place()
    half = lax.axis_index("fsdp")
    partner = place_of(line, side, 1 - core)
    across = place_of(line, 1 - side, core)
    rows = own_ref.shape[0] // pieces

    barrier = pltpu.get_barrier_semaphore()

    def enter(step, carried):
        pl.semaphore_signal(
            barrier, inc=1, device_id={"ctx": lax.rem(me + step, count)}, device_id_type=MESH_ID
        )
        return carried

    lax.fori_loop(1, count, enter, 0)
    pl.semaphore_signal(barrier, inc=1, device_id={"fsdp": 1 - half}, device_id_type=MESH_ID)
    pl.semaphore_wait(barrier, count)

    moves = []
    for source, target, (parts, kind) in zip(sources, targets, shared):
        wide = target.shape[2] // parts
        for part in range(parts):
            def block(goal, source=source, part=part, kind=kind, wide=wide, parts=parts):
                if kind == "same":
                    return source
                if kind == "blocks":
                    return source.at[goal]
                first = part * (source.shape[1] // parts) + goal * wide
                return source.at[:, pl.ds(pl.multiple_of(first, 128), wide)]

            def place(sender, side_of, target=target, part=part, wide=wide, parts=parts):
                at = target.at[sender * 2 + side_of]
                return at if parts == 1 else at.at[:, pl.ds(part * wide, wide)]

            moves.append((block, place))

    def origin(step):
        return lax.rem(me + count - step, count)

    def give(step, m):
        goal = lax.rem(me + step, count)
        block, place = moves[m]
        return remote(block(goal), place(me, half), give_sem.at[step, m], take_sem.at[step, m], {"ctx": goal})

    def taken(step, m):
        at = moves[m][1](origin(step), half)
        return remote(at, at, give_sem.at[step, m], take_sem.at[step, m], {"ctx": origin(step)})

    def hand(step, m, side_of):
        at = moves[m][1](origin(step), side_of)
        return remote(at, at, pass_sem.at[step, m], passed_sem.at[step, m], {"fsdp": 1 - half})

    def hand_own(m):
        block, place = moves[m]
        return remote(block(me), place(me, half), pass_sem.at[0, m], passed_sem.at[0, m], {"fsdp": 1 - half})

    def stay(m):
        block, place = moves[m]
        return pltpu.make_async_copy(block(me), place(me, half), stay_sem.at[m])

    def each_step(first, last, body):
        def step_body(step, carried):
            for m in range(len(moves)):
                body(step, m)
            return carried

        lax.fori_loop(first, last, step_body, 0)

    pair_stay = pltpu.make_async_copy(pair_ref, pair_out.at[half], stay_sem.at[len(moves)])

    def pair_copy(side_of):
        return remote(pair_ref, pair_out.at[side_of], pair_sem.at[0], pair_sem.at[1], {"fsdp": 1 - half})

    def part(block, k):
        return out_ref.at[block, pl.ds(pl.multiple_of(k * rows, rows), rows), :]

    def mine(k):
        return own_ref.at[pl.ds(pl.multiple_of(k * rows, rows), rows), :]

    def to_up(source, block, slot, k):
        return remote(source, part(block, k), up_sem.at[slot, k], recv_sem.at[block, k], {"ctx": me + 4})

    def to_down(source, block, slot, k):
        return remote(source, part(block, k), down_sem.at[slot, k], recv_sem.at[block, k], {"ctx": me - 4})

    def to_across(source, block, k):
        return remote(
            source, part(block, k), across_sem.at[block // 4, k], recv_sem.at[block, k], {"ctx": across}
        )

    def to_partner(source, block, k):
        return remote(
            source, part(block, k), chip_sem.at[block // 2, k], recv_sem.at[block, k], {"ctx": partner}
        )

    def arrived(block, k):
        to_partner(part(block, k), block, k).wait_recv()

    def each_piece(body):
        def step(k, carried):
            body(k)
            return carried

        lax.fori_loop(0, pieces, step, 0)

    keep = pltpu.make_async_copy(own_ref, out_ref.at[me], keep_sem)

    def first(k):
        @pl.when(line < lines - 1)
        def up():
            to_up(mine(k), me, 0, k).start()

        @pl.when(line > 0)
        def down():
            to_down(mine(k), me, 0, k).start()

        to_across(mine(k), me, k).start()
        to_partner(mine(k), me, k).start()

    each_piece(first)
    each_step(1, count, lambda step, m: give(step, m).start())
    pair_copy(half).start()
    for m in range(len(moves)):
        hand_own(m).start()
    keep.start()
    pair_stay.start()
    for m in range(len(moves)):
        stay(m).start()

    def pass_on(step, m):
        taken(step, m).wait_recv()
        hand(step, m, half).start()

    for hops in range(1, lines):
        def relay(k, hops=hops):
            @pl.when(line >= hops)
            def from_below():
                block = me - 4 * hops
                arrived(block, k)
                if hops < lines - 1:
                    @pl.when(line < lines - 1)
                    def up():
                        to_up(part(block, k), block, hops, k).start()

                to_across(part(block, k), block, k).start()
                to_partner(part(block, k), block, k).start()

            @pl.when(line < lines - hops)
            def from_above():
                block = me + 4 * hops
                arrived(block, k)
                if hops < lines - 1:
                    @pl.when(line > 0)
                    def down():
                        to_down(part(block, k), block, hops, k).start()

                to_across(part(block, k), block, k).start()
                to_partner(part(block, k), block, k).start()

        each_piece(relay)
        each_step(
            1 + (hops - 1) * (count - 1) // (lines - 1), 1 + hops * (count - 1) // (lines - 1), pass_on
        )

    def hand_over(block):
        def one(k):
            arrived(block, k)
            to_partner(part(block, k), block, k).start()

        each_piece(one)

    hand_over(across)
    for hops in range(1, lines):
        @pl.when(line >= hops)
        def from_below(hops=hops):
            hand_over(across - 4 * hops)

        @pl.when(line < lines - hops)
        def from_above(hops=hops):
            hand_over(across + 4 * hops)

    def settle(index, carried):
        def one(k):
            arrived(index * 2 + 1 - core, k)
            to_partner(part(me, k), index * 2 + core, k).wait_send()

        each_piece(one)
        return carried

    lax.fori_loop(0, count // 2, settle, 0)

    def settle_across(index, carried):
        each_piece(lambda k: to_across(part(me, k), index * 4, k).wait_send())
        return carried

    lax.fori_loop(0, lines, settle_across, 0)
    for hops in range(lines - 1):
        @pl.when((line >= hops) & (line < lines - 1))
        def up(hops=hops):
            each_piece(lambda k: to_up(part(me, k), me, hops, k).wait_send())

        @pl.when((line < lines - hops) & (line > 0))
        def down(hops=hops):
            each_piece(lambda k: to_down(part(me, k), me, hops, k).wait_send())

    each_step(0, count, lambda step, m: hand(step, m, 1 - half).wait_recv())
    each_step(1, count, lambda step, m: hand(step, m, half).wait_send())
    each_step(1, count, lambda step, m: give(step, m).wait_send())
    for m in range(len(moves)):
        hand_own(m).wait_send()
        stay(m).wait()
    pair_copy(1 - half).wait_recv()
    pair_copy(half).wait_send()
    pair_stay.wait()
    keep.wait()


def supply(own, arrays, shared, pair_array, collective_id, name, pieces=2):
    count = lax.axis_size("ctx")
    lines = count // 4
    rows, width = own.shape
    targets = []
    for array, (_, kind) in zip(arrays, shared):
        if kind == "columns":
            block = (array.shape[0], array.shape[1] // count)
        else:
            block = array.shape if kind == "same" else array.shape[1:]
        targets.append(jax.ShapeDtypeStruct((count * 2, *block), array.dtype))
    moves = sum(parts for parts, _ in shared)
    operands = [own, *arrays, pair_array]
    rows_all, *got, pair_all = pl.pallas_call(
        functools.partial(supply_kernel, count, pieces, tuple(shared)),
        out_shape=[
            jax.ShapeDtypeStruct((count, rows, width), own.dtype),
            *targets,
            jax.ShapeDtypeStruct((2, *pair_array.shape), pair_array.dtype),
        ],
        in_specs=[pl.BlockSpec(memory_space=pltpu.VMEM)] * len(operands),
        out_specs=[pl.BlockSpec(memory_space=pl.ANY)] * len(operands),
        scratch_shapes=[
            pltpu.SemaphoreType.DMA,
            pltpu.SemaphoreType.DMA((lines, pieces)),
            pltpu.SemaphoreType.DMA((lines, pieces)),
            pltpu.SemaphoreType.DMA((lines, pieces)),
            pltpu.SemaphoreType.DMA((count // 2, pieces)),
            pltpu.SemaphoreType.DMA((count, pieces)),
            pltpu.SemaphoreType.DMA((count, moves)),
            pltpu.SemaphoreType.DMA((count, moves)),
            pltpu.SemaphoreType.DMA((count, moves)),
            pltpu.SemaphoreType.DMA((count, moves)),
            pltpu.SemaphoreType.DMA((moves + 1,)),
            pltpu.SemaphoreType.DMA((2,)),
        ],
        compiler_params=pltpu.CompilerParams(collective_id=collective_id, has_side_effects=True),
        cost_estimate=pl.CostEstimate(flops=0, bytes_accessed=BUSY, transcendentals=0),
        name=name,
    )(*operands)
    return rows_all.reshape(count * rows, width), got, pair_all.reshape(-1, pair_array.shape[1])


def project_kernel(rows_ref, gain_ref, shift_ref, weight_ref, bias_ref, normed_ref, out_ref):
    unit, _ = norm_parts(rows_ref[...].astype(F32))
    normed = (unit * gain_ref[...] + shift_ref[...]).astype(BF16)
    normed_ref[...] = normed
    projected = jnp.dot(normed, weight_ref[...], preferred_element_type=F32)
    out_ref[...] = (projected + bias_ref[...]).astype(BF16)


def project(rows_in, gain, shift, weight, bias, block=256):
    total, width = rows_in.shape
    columns = weight.shape[1]
    row = pl.BlockSpec((1, width), lambda i: (0, 0))
    return pl.pallas_call(
        project_kernel,
        grid=(total // block,),
        in_specs=[
            pl.BlockSpec((block, width), lambda i: (i, 0)),
            row,
            row,
            pl.BlockSpec((width, columns), lambda i: (0, 0)),
            pl.BlockSpec((1, columns), lambda i: (0, 0)),
        ],
        out_specs=[
            pl.BlockSpec((block, width), lambda i: (i, 0)),
            pl.BlockSpec((block, columns), lambda i: (i, 0)),
        ],
        out_shape=[
            jax.ShapeDtypeStruct((total, width), BF16),
            jax.ShapeDtypeStruct((total, columns), BF16),
        ],
        cost_estimate=pl.CostEstimate(
            flops=2 * total * width * columns, bytes_accessed=6 * total * width, transcendentals=0
        ),
        name="project",
    )(rows_in, gain[None], shift[None], weight, bias[None])


def feed_kernel(
    normed_ref, grad_ref, up_ref, down_ref, bias_ref,
    activated_ref, grad_hidden_ref, terms_ref, branch_ref, sums_ref,
):
    hidden = jnp.dot(normed_ref[...], up_ref[...], preferred_element_type=F32) + bias_ref[...]
    grad_activated = lax.dot_general(grad_ref[...], down_ref[...], NT, preferred_element_type=F32)
    normal = 0.5 * (1.0 + lax.erf(hidden * 0.5**0.5))
    density = jnp.exp(-0.5 * hidden * hidden) * (2.0 * math.pi) ** -0.5
    activated = (hidden * normal).astype(BF16)
    grad_hidden = (grad_activated * (normal + hidden * density)).astype(BF16)
    activated_ref[...] = activated
    grad_hidden_ref[...] = grad_hidden
    terms = lax.dot_general(grad_hidden, up_ref[...], NT, preferred_element_type=F32)
    terms_ref[...] = terms.astype(BF16)
    branch = jnp.dot(activated, down_ref[...], preferred_element_type=F32)
    branch_ref[...] = branch.astype(BF16)

    @pl.when(pl.program_id(0) == 0)
    def clear():
        sums_ref[...] = jnp.zeros_like(sums_ref)

    sums_ref[...] += jnp.sum(grad_hidden.astype(F32), axis=0, keepdims=True)


def feed(normed, grads, w_up, w_down, bias, block=256):
    total, width = normed.shape
    hidden = w_up.shape[1]
    wide = pl.BlockSpec((block, width), lambda i: (i, 0))
    narrow_rows = pl.BlockSpec((block, hidden), lambda i: (i, 0))
    return pl.pallas_call(
        feed_kernel,
        grid=(total // block,),
        in_specs=[
            wide,
            wide,
            pl.BlockSpec((width, hidden), lambda i: (0, 0)),
            pl.BlockSpec((hidden, width), lambda i: (0, 0)),
            pl.BlockSpec((1, hidden), lambda i: (0, 0)),
        ],
        out_specs=[narrow_rows, narrow_rows, wide, wide, pl.BlockSpec((1, hidden), lambda i: (0, 0))],
        out_shape=[
            jax.ShapeDtypeStruct((total, hidden), BF16),
            jax.ShapeDtypeStruct((total, hidden), BF16),
            jax.ShapeDtypeStruct((total, width), BF16),
            jax.ShapeDtypeStruct((total, width), BF16),
            jax.ShapeDtypeStruct((1, hidden), F32),
        ],
        cost_estimate=pl.CostEstimate(flops=0, bytes_accessed=BUSY // 3, transcendentals=0),
        name="feed",
    )(normed, grads, w_up, w_down, bias[None])


def sum_kernel(
    count, pieces, riders, *refs
):
    if riders:
        (
            part_ref, grad_ref, pair_ref, out_ref, got_ref, pair_out,
            held, chip_in, across_in, line_in, grad_in, grad_sum, load_sem,
            chip_send, chip_recv, across_send, across_recv, line_send, line_recv,
            pass_sem, passed_sem, give_sem, take_sem, pair_sem,
        ) = refs
    else:
        (
            part_ref, out_ref, held, chip_in, across_in, line_in, load_sem,
            chip_send, chip_recv, across_send, across_recv, line_send, line_recv,
        ) = refs
    lines = count // 4
    me, line, side, core = own_place()
    partner = place_of(line, side, 1 - core)
    across = place_of(line, 1 - side, core)
    rows = out_ref.shape[0] // pieces

    def at(ref, block, k):
        return ref.at[block, pl.ds(pl.multiple_of(k * rows, rows), rows), :]

    def to_partner(pair, k):
        return remote(
            at(part_ref, pair * 2 + 1 - core, k), at(chip_in, pair, k),
            chip_send.at[pair, k], chip_recv.at[pair, k], {"ctx": partner},
        )

    def to_across(goal, k):
        return remote(
            at(held, goal * 2 + 1 - side, k), at(across_in, goal, k),
            across_send.at[goal, k], across_recv.at[goal, k], {"ctx": across},
        )

    def to_next(goal, target, slot, k):
        return remote(
            at(held, goal * 2 + side, k), at(line_in, slot, k),
            line_send.at[goal, k], line_recv.at[slot, k], {"ctx": target},
        )

    def each_piece(body):
        def step(k, carried):
            body(k)
            return carried

        lax.fori_loop(0, pieces, step, 0)

    def far_first(visit, between=None):
        for hops in range(lines - 1, 0, -1):
            @pl.when(line + hops < lines)
            def ahead(hops=hops):
                visit(line + hops, 1)

            @pl.when(line >= hops)
            def behind(hops=hops):
                visit(line - hops, -1)

            if between is not None:
                between(lines - hops)

    half = lax.axis_index("fsdp")
    barrier = pltpu.get_barrier_semaphore()

    def enter(step, carried):
        pl.semaphore_signal(
            barrier, inc=1, device_id={"ctx": lax.rem(me + step, count)}, device_id_type=MESH_ID
        )
        return carried

    def hand(step):
        goal = lax.rem(me + step, count)
        return remote(
            grad_ref.at[goal, 1 - half], grad_in.at[goal], pass_sem.at[step], passed_sem.at[step],
            {"fsdp": 1 - half},
        )

    def give_grad(step):
        goal = lax.rem(me + step, count)
        return remote(
            grad_sum.at[goal], got_ref.at[me], give_sem.at[step], take_sem.at[step], {"ctx": goal}
        )

    def take_grad(step):
        source = lax.rem(me + count - step, count)
        return remote(
            grad_sum.at[source], got_ref.at[source], give_sem.at[step], take_sem.at[step], {"ctx": source}
        )

    def each_step(first, last, body):
        def step_body(step, carried):
            body(step)
            return carried

        lax.fori_loop(first, last, step_body, 0)

    def pass_on(step):
        goal = lax.rem(me + step, count)
        hand(step).wait_recv()
        grad_sum[goal] = (grad_ref[goal, half].astype(F32) + grad_in[goal].astype(F32)).astype(BF16)
        give_grad(step).start()

    def pair_copy():
        return remote(pair_ref.at[1 - half], pair_out, pair_sem.at[0], pair_sem.at[1], {"fsdp": 1 - half})

    loads = [
        pltpu.make_async_copy(part_ref.at[pair * 2 + core], held.at[pair], load_sem.at[pair])
        for pair in range(count // 2)
    ]
    for load in loads:
        load.start()
    lax.fori_loop(1, count, enter, 0)
    pl.semaphore_signal(barrier, inc=1, device_id={"fsdp": 1 - half}, device_id_type=MESH_ID)
    pl.semaphore_wait(barrier, count)

    def give(goal, way):
        each_piece(lambda k: to_partner(goal * 2 + 1 - side, k).start())

    def give_same(goal, way):
        each_piece(lambda k: to_partner(goal * 2 + side, k).start())

    if riders:
        each_step(1, count, lambda step: hand(step).start())
        hand(0).start()
        pair_copy().start()
    far_first(give)
    give(line, 0)
    far_first(give_same)
    give_same(line, 0)
    for load in loads:
        load.wait()

    def read(ref, block, k):
        return ref[block, pl.ds(pl.multiple_of(k * rows, rows), rows), :].astype(F32)

    def write(block, k, value):
        held[block, pl.ds(pl.multiple_of(k * rows, rows), rows), :] = value.astype(held.dtype)

    def cross(goal, way):
        pair = goal * 2 + 1 - side

        def one(k):
            to_partner(pair, k).wait_recv()
            write(pair, k, read(held, pair, k) + read(chip_in, pair, k))
            to_across(goal, k).start()

        each_piece(one)

    far_first(cross)
    cross(line, 0)

    def two_sums(goal, k):
        pair = goal * 2 + side
        to_partner(pair, k).wait_recv()
        to_across(goal, k).wait_recv()
        return read(held, pair, k) + read(chip_in, pair, k) + read(across_in, goal, k)

    def along(goal, way):
        pair = goal * 2 + side
        target = me + 4 * way
        arriving = goal
        if way == 1:
            slot = goal
            fed = line > 0
        else:
            fed = line < lines - 1
            slot = jnp.where(goal == line - 1, lines, goal)

        def one(k):
            total = two_sums(goal, k)
            write(pair, k, total)

            @pl.when(fed)
            def add():
                to_next(goal, target, arriving, k).wait_recv()
                write(pair, k, total + read(line_in, arriving, k))

            to_next(goal, target, slot, k).start()

        each_piece(one)

    def share_of_steps(turn):
        each_step(
            1 + (turn - 1) * (count - 1) // (lines - 1), 1 + turn * (count - 1) // (lines - 1), pass_on
        )

    far_first(along, share_of_steps if riders else None)
    if riders:
        hand(0).wait_recv()
        grad_sum[me] = (grad_ref[me, half].astype(F32) + grad_in[me].astype(F32)).astype(BF16)
        stay = pltpu.make_async_copy(grad_sum.at[me], got_ref.at[me], pair_sem.at[2])
        stay.start()

    def last(k):
        span = pl.ds(pl.multiple_of(k * rows, rows), rows)
        out_ref[span, :] = two_sums(line, k)

        @pl.when(line > 0)
        def from_below():
            to_next(line, me, line, k).wait_recv()
            out_ref[span, :] += read(line_in, line, k)

        @pl.when(line < lines - 1)
        def from_above():
            to_next(line, me, lines, k).wait_recv()
            out_ref[span, :] += read(line_in, lines, k)

    each_piece(last)

    def settle(index, carried):
        each_piece(lambda k: to_partner(index, k).wait_send())
        return carried

    lax.fori_loop(0, count // 2, settle, 0)

    def settle_line(goal, carried):
        each_piece(lambda k: to_across(goal, k).wait_send())

        @pl.when(goal != line)
        def sent():
            each_piece(lambda k: to_next(goal, me, goal, k).wait_send())

        return carried

    lax.fori_loop(0, lines, settle_line, 0)
    if riders:
        each_step(1, count, lambda step: take_grad(step).wait_recv())
        each_step(1, count, lambda step: give_grad(step).wait_send())
        each_step(0, count, lambda step: hand(step).wait_send())
        pair_copy().wait_recv()
        pair_copy().wait_send()
        stay.wait()


def sum_rows(partial, collective_id, grad=None, pair_grad=None, pieces=2):
    count = lax.axis_size("ctx")
    lines = count // 4
    width = partial.shape[1]
    rows = partial.shape[0] // count
    riders = grad is not None
    anywhere = pl.BlockSpec(memory_space=pl.ANY)
    in_vmem = pl.BlockSpec(memory_space=pltpu.VMEM)
    operands = [partial.astype(BF16).reshape(count, rows, width)]
    results = [jax.ShapeDtypeStruct((rows, width), F32)]
    buffers = [
        pltpu.VMEM((count // 2, rows, width), BF16),
        pltpu.VMEM((count // 2, rows, width), BF16),
        pltpu.VMEM((lines, rows, width), BF16),
        pltpu.VMEM((lines + 1, rows, width), BF16),
    ]
    semaphores = [(count // 2,)] + [(count // 2, pieces)] * 2 + [(lines, pieces)] * 3 + [(lines + 1, pieces)]
    if riders:
        owned, columns = grad.shape[0] // (2 * count), grad.shape[1]
        pair_shape = (pair_grad.shape[0] // 2, pair_grad.shape[1])
        operands += [grad.reshape(count, 2, owned, columns), pair_grad.reshape(2, *pair_shape)]
        results += [
            jax.ShapeDtypeStruct((count, owned, columns), BF16),
            jax.ShapeDtypeStruct(pair_shape, BF16),
        ]
        buffers += [pltpu.VMEM((count, owned, columns), BF16)] * 2
        semaphores += [(count,)] * 4 + [(3,)]
    done = pl.pallas_call(
        functools.partial(sum_kernel, count, pieces, riders),
        out_shape=results,
        in_specs=[anywhere] + [in_vmem, anywhere] * riders,
        out_specs=[in_vmem] + [anywhere] * (2 * riders),
        scratch_shapes=buffers + [pltpu.SemaphoreType.DMA(shape) for shape in semaphores],
        compiler_params=pltpu.CompilerParams(
            collective_id=collective_id, has_side_effects=True, vmem_limit_bytes=63 * 2**20
        ),
        cost_estimate=pl.CostEstimate(flops=0, bytes_accessed=BUSY, transcendentals=0),
        name="sum_rows",
    )(*operands)
    return done if riders else done[0]


def own_half(pair_grad, other):
    half = pair_grad.shape[0] // 2
    kept = lax.dynamic_slice_in_dim(pair_grad, lax.axis_index("fsdp") * half, half, 0)
    return kept.astype(F32) + other.astype(F32)


def in_order(got, parts):
    count, owned, _ = got.shape
    return got.reshape(count, owned, parts, -1).transpose(1, 2, 0, 3).reshape(owned, -1).astype(F32)


def weight_grad(rows_in, grads):
    terms = lax.dot_general(rows_in, grads, TN, preferred_element_type=F32).astype(BF16)
    return lax.optimization_barrier(terms)


def widen(columns, share, axis=-1):
    if share == 1:
        return columns
    count = lax.axis_size("ctx")
    groups = [list(range(first, first + share)) for first in range(0, count, share)]
    return lax.all_gather(
        columns, "ctx", axis=axis % columns.ndim, tiled=True, axis_index_groups=groups
    )


def narrow(columns, share):
    if share == 1:
        return columns
    width = columns.shape[-1] // share
    place = lax.rem(lax.axis_index("ctx"), share)
    return lax.dynamic_slice_in_dim(columns, place * width, width, columns.ndim - 1)


def on_device(
    tokens, doc_lengths, ln1_gain, ln1_bias, w_qkv, bias_q, bias_v, w_out, b_out,
    ln2_gain, ln2_bias, w_up, b_up, w_down, b_down, cotangent,
):
    count = lax.axis_size("ctx")
    rank = lax.axis_index("ctx")
    pair_rank = lax.axis_index("fsdp")
    tok_rows, width = tokens.shape[1:]
    seq_len = tok_rows * count
    own_cols = width // count
    share = max(1, HEAD_DIM // own_cols)
    head_count = width // HEAD_DIM
    heads = own_cols * share // HEAD_DIM
    rows = min(256, seq_len)

    lengths = doc_lengths[0]
    doc_starts = jnp.cumsum(lengths) - lengths
    positions = jnp.arange(seq_len, dtype=jnp.int32)
    starts = jnp.max(
        jnp.where(doc_starts[None, :] <= positions[:, None], doc_starts[None, :], 0), axis=1
    ).astype(jnp.int32)
    low = starts[::rows] // rows
    starts = starts[None, :]
    first_head = (rank // share) * heads
    head_ids = (first_head + jnp.arange(heads)).astype(F32)
    slopes = 2.0 ** (-8.0 * (head_ids + 1.0) / head_count)

    vectors = [ln1_gain, ln1_bias, b_out, ln2_gain, ln2_bias, b_down, bias_q, bias_v, b_up]
    devices = count * lax.axis_size("fsdp")
    own_vectors = jnp.concatenate([vector.astype(F32) for vector in vectors])
    tiles = -(-own_vectors.shape[0] // 1024) * 8
    own_vectors = jnp.pad(own_vectors, (0, tiles * 128 - own_vectors.shape[0])).reshape(tiles, 128)
    if own_cols % 128 == 0:
        qkv_blocks, qkv_kind = w_qkv, (3, "columns")
    else:
        split = w_qkv.reshape(w_qkv.shape[0], 3, count, own_cols).transpose(2, 0, 1, 3)
        qkv_blocks, qkv_kind = split.reshape(count, w_qkv.shape[0], -1), (1, "blocks")
    tokens_all, (w_qkv_own, everywhere), w_out_own = supply(
        tokens[0], [qkv_blocks, own_vectors], [qkv_kind, (1, "same")], w_out, 3, "begin"
    )
    w_qkv_own = w_qkv_own.reshape(width, -1)
    everywhere = everywhere.reshape(devices, -1)
    at = 0
    whole_vectors = []
    for vector in vectors:
        whole_vectors.append(everywhere[:, at : at + vector.shape[0]].reshape(-1))
        at += vector.shape[0]
    gain_one, shift_one, b_out_all, gain_two, shift_two, b_down_all = whole_vectors[:6]
    head_at = first_head * HEAD_DIM
    bias_q_own, bias_v_own = (
        lax.dynamic_slice_in_dim(vector, head_at, heads * HEAD_DIM) for vector in whole_vectors[6:8]
    )
    ff_cols = whole_vectors[8].shape[0] // count
    b_up_own = lax.dynamic_slice_in_dim(whole_vectors[8], rank * ff_cols, ff_cols)

    w_qkv_head = widen(w_qkv_own.reshape(width, 3, -1), share).reshape(width, -1)
    w_out_head = widen(w_out_own, share, 0)

    inputs = tokens[0].astype(F32)
    unit_one, rate_one = norm_parts(inputs)
    grad_out = cotangent[0]
    tokens_all, cotangent_rows = lax.optimization_barrier((tokens_all, grad_out))
    grad_out_all = gather_beside(cotangent_rows)

    head_width = heads * HEAD_DIM
    shift = jnp.concatenate([bias_q_own, jnp.zeros(head_width, F32), bias_v_own])
    normed_all, projected = project(tokens_all, gain_one, shift_one, w_qkv_head, shift)
    projected = to_sequence(projected, count)
    queries, keys, values = (
        projected[:, part * head_width : (part + 1) * head_width] for part in range(3)
    )
    attended_full, log_total = attend(queries, keys, values, starts, low, slopes, rows)
    attended_own = narrow(to_layout(attended_full.astype(BF16), count), share)
    attended_terms = jnp.dot(attended_own, w_out_own, preferred_element_type=F32)
    middle = inputs + sum_rows(attended_terms, 4) + b_out_all

    unit_two, rate_two = norm_parts(middle)
    normed_two = (unit_two * gain_two + shift_two).astype(BF16)
    normed_two_all, (w_up_own,), w_down_own = supply(
        normed_two, [w_up], [(1, "columns")], w_down, 5, "middle"
    )
    w_up_own = w_up_own.reshape(width, -1)
    activated, grad_hidden, terms, branch_terms, grad_hidden_sums = feed(
        normed_two_all, grad_out_all, w_up_own, w_down_own, b_up_own
    )
    w_down_terms = weight_grad(activated, grad_out_all)
    grad_normed_two, w_up_got, w_down_other = sum_rows(
        terms, 1, weight_grad(normed_two_all, grad_hidden), w_down_terms
    )

    grad_middle = grad_out.astype(F32) + norm_back(unit_two, rate_two, gain_two, grad_normed_two)
    grad_branch = grad_middle.astype(BF16)
    grad_branch, branch_terms = lax.optimization_barrier((grad_branch, branch_terms))
    branch = sum_beside(branch_terms)
    grad_branch_all = gather_rows(grad_branch)
    grad_heads = lax.dot_general(
        grad_branch_all, w_out_head, NT, preferred_element_type=F32
    ).astype(BF16)
    grad_heads = to_sequence(grad_heads, count)

    delta = (grad_heads.astype(F32) * attended_full).reshape(seq_len, heads, HEAD_DIM)
    delta = jnp.sum(delta, axis=-1).T
    grad_parts = attend_back(
        queries, keys, values, grad_heads, starts, low, slopes, log_total, delta, rows
    )
    grad_qkv = jnp.concatenate(
        [narrow(to_layout(part, count), share) for part in grad_parts], axis=1
    )
    grad_qkv = lax.optimization_barrier(grad_qkv)
    column_sums = jnp.sum(grad_qkv.astype(F32), axis=0)
    w_out_terms = weight_grad(attended_own, grad_branch_all)
    grad_normed, w_qkv_got, w_out_other = sum_rows(
        lax.dot_general(grad_qkv, w_qkv_own, NT, preferred_element_type=F32),
        2,
        weight_grad(normed_all, grad_qkv),
        w_out_terms,
    )
    branch, middle, grad_normed = lax.optimization_barrier((branch, middle, grad_normed))
    outputs = (middle + branch + b_down_all).astype(BF16)
    grad_inputs = grad_middle + norm_back(unit_one, rate_one, gain_one, grad_normed)

    pair = devices // count
    full_sums = jnp.stack(
        [
            jnp.sum(grad_normed * unit_one, axis=0),
            jnp.sum(grad_normed, axis=0),
            jnp.sum(grad_normed_two * unit_two, axis=0),
            jnp.sum(grad_normed_two, axis=0),
            jnp.sum(grad_branch.astype(F32), axis=0),
            jnp.sum(grad_out.astype(F32), axis=0),
        ]
    )
    full_sums = full_sums.reshape(6, devices, -1).transpose(1, 0, 2).reshape(devices, -1)
    own_sums = jnp.concatenate(
        [
            column_sums[:own_cols].reshape(pair, -1),
            column_sums[2 * own_cols :].reshape(pair, -1),
            grad_hidden_sums.reshape(pair, -1),
        ],
        axis=1,
    )
    full_sums, w_qkv_got, w_up_got, w_out_other, w_down_other = lax.optimization_barrier(
        (full_sums, w_qkv_got, w_up_got, w_out_other, w_down_other)
    )
    grad_w_qkv = in_order(w_qkv_got, 3)
    grad_w_up = in_order(w_up_got, 1)
    grad_w_out = own_half(w_out_terms, w_out_other)
    grad_w_down = own_half(w_down_terms, w_down_other)
    here = (jnp.arange(count) == rank)[:, None, None]
    own_sums = jnp.where(here, own_sums[None], 0.0).reshape(devices, -1)
    sums = jnp.sum(exchange(jnp.concatenate([full_sums, own_sums], axis=1)), axis=0)
    share_of = width // devices
    (
        grad_ln1_gain, grad_ln1_bias, grad_ln2_gain, grad_ln2_bias, grad_b_out, grad_b_down,
        grad_bias_q, grad_bias_v,
    ) = sums[: 8 * share_of].reshape(8, share_of)
    grad_b_up = sums[8 * share_of :]
    return (
        outputs[None],
        grad_inputs[None],
        grad_ln1_gain,
        grad_ln1_bias,
        grad_w_qkv,
        grad_bias_q,
        grad_bias_v,
        grad_w_out,
        grad_b_out,
        grad_ln2_gain,
        grad_ln2_bias,
        grad_w_up,
        grad_b_up,
        grad_w_down,
        grad_b_down,
    )


def solution(mesh):
    spread = P(BOTH)
    matrix = P(BOTH, None)
    rows = P("fsdp", "ctx", None)
    placed = (
        rows, P("fsdp", None), spread, spread, matrix, spread, spread, matrix, spread,
        spread, spread, matrix, spread, matrix, spread, rows,
    )
    results = (
        rows, rows, spread, spread, matrix, spread, spread, matrix, spread,
        spread, spread, matrix, spread, matrix, spread,
    )
    return jax.shard_map(
        on_device, mesh=mesh, in_specs=placed, out_specs=results, check_vma=False
    )
```
